32 devices in a mesh: dp: 4 (over y, core), expert: 8 (over z, x).
Axes of the slice: x: 2, y: 2, z: 4, core: 2. Of those that a mesh axis runs over, the one named last changes fastest.
Arguments:
- tokens: bfloat16 [2, 32, 128, 2048], P(None, ('dp', 'expert')), may hold values from -6 to 6
- out_cotangent: bfloat16 [2, 32, 128, 2048], P(None, ('dp', 'expert')), may hold values from -6 to 6
- lengths: int32 [2, 32], P(None, ('dp', 'expert')), may hold values from 32 to 128
- routes: int32 [2, 32, 128, 8], P(None, ('dp', 'expert')), may hold values from 0 to 15, all different within a row
- priority: int32 [2, 32, 1024], P(None, ('dp', 'expert')), may hold values from 0 to 1023, each once within a row
- attn_gain: bfloat16 [2048], P(('dp', 'expert')), may hold values from 0.5 to 2
- query_weight: bfloat16 [2048, 2048], P(('dp', 'expert')), may hold values from -0.125 to 0.125
- key_weight: bfloat16 [2048, 2048], P(('dp', 'expert')), may hold values from -0.125 to 0.125
- value_weight: bfloat16 [2048, 2048], P(('dp', 'expert')), may hold values from -0.125 to 0.125
- output_weight: bfloat16 [2048, 2048], P(('dp', 'expert')), may hold values from -1 to 1
- query_gain: bfloat16 [128], P(('dp', 'expert')), may hold values from 0.5 to 2
- key_gain: bfloat16 [128], P(('dp', 'expert')), may hold values from 0.5 to 2
- ffn_gain: bfloat16 [2048], P(('dp', 'expert')), may hold values from 0.5 to 2
- router_weight: bfloat16 [2048, 16], P(('dp', 'expert')), may hold values from -0.0625 to 0.0625
- gate_weight: bfloat16 [16, 2048, 1024], P('expert', 'dp'), may hold values from -0.125 to 0.125
- up_weight: bfloat16 [16, 2048, 1024], P('expert', 'dp'), may hold values from -0.125 to 0.125
- down_weight: bfloat16 [16, 1024, 2048], P('expert', 'dp'), may hold values from -1.5 to 1.5
Outputs:
- layer_out: bfloat16 [2, 32, 128, 2048], P(None, ('dp', 'expert'))
- tokens_grad: float32 [2, 32, 128, 2048], P(None, ('dp', 'expert'))
- attn_gain_grad: float32 [2048], P(('dp', 'expert'))
- query_weight_grad: float32 [2048, 2048], P(('dp', 'expert'))
- key_weight_grad: float32 [2048, 2048], P(('dp', 'expert'))
- value_weight_grad: float32 [2048, 2048], P(('dp', 'expert'))
- output_weight_grad: float32 [2048, 2048], P(('dp', 'expert'))
- query_gain_grad: float32 [128], P(('dp', 'expert'))
- key_gain_grad: float32 [128], P(('dp', 'expert'))
- ffn_gain_grad: float32 [2048], P(('dp', 'expert'))
- router_weight_grad: float32 [2048, 16], P(('dp', 'expert'))
- gate_weight_grad: float32 [16, 2048, 1024], P('expert', 'dp')
- up_weight_grad: float32 [16, 2048, 1024], P('expert', 'dp')
- down_weight_grad: float32 [16, 1024, 2048], P('expert', 'dp')
The draws below stay inside these ranges and needn't reach their ends.
Inputs may be any that keep to these rules, and one draw needn't show every extreme that they name: `routes`: each token names 8 different experts. `priority`: for each sequence a permutation of its 1024 pairs, pair t * 8 + k being token t's k-th route.
All inputs are finite; a program needn't handle non-finite values.
Results may differ from the reference program's by a relative error of at most 0.023.
Values may be sent and summed in bfloat16 or wider, within the bound.
No kernel may reach another device: no remote copies, remote signals or barrier semaphores. Data moves between devices by JAX's collectives and lax.ppermute only.
A program may use at most 320 MiB of HBM per device.

```python
import math
from functools import partial
import jax
import jax.numpy as jnp
from jax import lax

D = 2048
HEADS = 16
HD = 128
FF = 1024
TOP = 8
SEQ = 128
MB = 2
EXPERTS = 16
NSEQ = 32
CAP = 80


def draw_lengths(key, part):
    drawn = jax.random.randint(key, (MB, NSEQ), SEQ // 4, SEQ + 1, dtype=jnp.int32)
    return drawn.at[0, 0].set(SEQ).at[0, 1].set(SEQ // 4)


def steps_of(stream_key, dims, split, low, largest):
    level, own = 1.0, jax.random.fold_in(stream_key, 6)
    for position, blocks in split:
        steps = jnp.exp(jax.random.uniform(jax.random.fold_in(own, position), (blocks,), jnp.float32, low / len(split), largest / len(split)))
        level = level * jnp.repeat(steps, dims[position] // blocks).reshape([-1 if axis == position else 1 for axis in range(len(dims))])
    return level


def picks_of(key, rows, amount, top, lift):
    order = jax.random.permutation(jax.random.fold_in(key, 1), amount)
    pull = order
    for power in range(3):
        pull = pull * pull // amount
    pull = pull * lift // amount
    chance = jax.random.randint(jax.random.fold_in(key, 2), (rows, amount), 0, 4096) + pull
    fixed_rows = jax.random.permutation(jax.random.fold_in(key, 3), rows)[jnp.arange(amount) % rows]
    chance = jnp.where(jnp.arange(rows)[:, None] == fixed_rows[None, :], 1 << 14, chance)
    score = chance * amount + jnp.arange(amount)
    return lax.top_k(score.astype(jnp.int32), top)[1].astype(jnp.int32)


def gaussian(rng, extent, deviation, limit, shards=(), kind=jnp.bfloat16):
    values = deviation * jax.random.normal(rng, extent, jnp.float32)
    if shards:
        values = values * steps_of(rng, extent, shards, -0.22, 0.18)
    return jnp.clip(values, -limit, limit).astype(kind)


def setup_inputs(seed: int = 0) -> dict:
    arg_keys = jax.random.split(jax.random.key(seed), 18)
    return {
        "tokens": gaussian(arg_keys[0], (MB, NSEQ, SEQ, D), 1.0, 6.0, ((1, 32),)),
        "out_cotangent": gaussian(arg_keys[1], (MB, NSEQ, SEQ, D), 1.0, 6.0, ((1, 32),)),
        "lengths": draw_lengths(jax.random.fold_in(arg_keys[17], 71), 0),
        "routes": picks_of(arg_keys[3], MB * NSEQ * SEQ, EXPERTS, TOP, 4096).reshape((MB, NSEQ, SEQ, TOP)),
        "priority": jax.vmap(lambda own: jax.random.permutation(own, SEQ * TOP))(jax.random.split(arg_keys[4], MB * NSEQ)).reshape((MB, NSEQ, SEQ * TOP)).astype(jnp.int32),
        "attn_gain": jnp.clip(jnp.exp(math.log(2.0) - 1.3862944 * jax.random.uniform(arg_keys[5], (D,), jnp.float32) ** steps_of(arg_keys[5], (D,), ((0, 32),), -0.2, 0.2)), 0.5, 2.0).astype(jnp.bfloat16),
        "query_weight": gaussian(arg_keys[6], (D, D), D ** -0.5, 0.125, ((0, 32),)),
        "key_weight": gaussian(arg_keys[7], (D, D), D ** -0.5, 0.125, ((0, 32),)),
        "value_weight": gaussian(arg_keys[8], (D, D), D ** -0.5, 0.125, ((0, 32),)),
        "output_weight": gaussian(arg_keys[9], (D, D), (D // 64) ** -0.5, 1.0, ((0, 32),)),
        "query_gain": jnp.clip(jnp.exp(math.log(2.0) - 1.3862944 * jax.random.uniform(arg_keys[10], (HD,), jnp.float32) ** steps_of(arg_keys[10], (HD,), ((0, 32),), -0.2, 0.2)), 0.5, 2.0).astype(jnp.bfloat16),
        "key_gain": jnp.clip(jnp.exp(math.log(2.0) - 1.3862944 * jax.random.uniform(arg_keys[11], (HD,), jnp.float32) ** steps_of(arg_keys[11], (HD,), ((0, 32),), -0.2, 0.2)), 0.5, 2.0).astype(jnp.bfloat16),
        "ffn_gain": jnp.clip(jnp.exp(math.log(2.0) - 1.3862944 * jax.random.uniform(arg_keys[12], (D,), jnp.float32) ** steps_of(arg_keys[12], (D,), ((0, 32),), -0.2, 0.2)), 0.5, 2.0).astype(jnp.bfloat16),
        "router_weight": gaussian(arg_keys[13], (D, EXPERTS), (4 * D) ** -0.5, 0.0625, ((0, 32),)),
        "gate_weight": gaussian(arg_keys[14], (EXPERTS, D, FF), D ** -0.5, 0.125, ((0, 8), (1, 4))),
        "up_weight": gaussian(arg_keys[15], (EXPERTS, D, FF), D ** -0.5, 0.125, ((0, 8), (1, 4))),
        "down_weight": gaussian(arg_keys[16], (EXPERTS, FF, D), (FF // 64) ** -0.5, 1.5, ((0, 8), (1, 4))),
    }


EPSILON = 1e-06
THETA = 50000.0
NEGATIVE = -1e+30
HIGHEST = lax.Precision.HIGHEST

@jax.custom_vjp
def low(v):
    return lax.optimization_barrier(v.astype(jnp.bfloat16)).astype(jnp.float32)

@jax.custom_vjp
def low_back(v):
    return v

def low_keep(v):
    return (low(v), None)

def low_pass(kept, grad):
    return (grad,)

def back_keep(v):
    return (v, None)

def back_low(kept, grad):
    return (low(grad),)
low.defvjp(low_keep, low_pass)
low_back.defvjp(back_keep, back_low)

def matmul(left, right):
    return jnp.dot(left, right, precision=HIGHEST)

def norm_rows(values, gain_row):
    return values * lax.rsqrt(lax.optimization_barrier(jnp.mean(values * values, axis=-1, keepdims=True)) + EPSILON) * gain_row

def rotate(values):
    row_count = values.shape[0]
    half_size = values.shape[-1] // 2
    frequency = THETA ** (-jnp.arange(half_size, dtype=jnp.float32) / half_size)
    angles = jnp.arange(row_count, dtype=jnp.float32)[:, None] * frequency[None, :]
    cosine = jnp.cos(angles)[:, None, :]
    sine_part = jnp.sin(angles)[:, None, :]
    first_half = values[..., :half_size]
    second = values[..., half_size:]
    return jnp.concatenate([first_half * cosine - second * sine_part, second * cosine + first_half * sine_part], axis=-1)

def dispatch_table(route, priority):
    flat_route = route.reshape(-1)
    onehot = (flat_route[:, None] == jnp.arange(EXPERTS, dtype=jnp.int32)[None, :]).astype(jnp.float32)
    before = (priority[None, :] < priority[:, None]).astype(jnp.float32)
    pair_rank = lax.optimization_barrier(jnp.sum(jnp.dot(before, onehot, precision=HIGHEST) * onehot, axis=1))
    column = flat_route * CAP + pair_rank.astype(jnp.int32)
    kept_pair = pair_rank < CAP
    slots_all = jnp.arange(EXPERTS * CAP, dtype=jnp.int32)
    chosen = kept_pair[:, None] & (column[:, None] == slots_all[None, :])
    return jnp.where(chosen, 1.0, 0.0).astype(jnp.float32)

def sequence(token_rows, length, route, priority, weights):
    attn_gain, query_weight, key_weight, value_weight, output_weight, query_gain, key_gain, ffn_gain, router_weight, gate_weight, up_weight, down_weight = weights
    row_count = token_rows.shape[0]
    normed = low(norm_rows(token_rows, attn_gain))
    query_raw = low_back(matmul(normed, query_weight)).reshape(row_count, HEADS, HD)
    key_raw = low_back(matmul(normed, key_weight)).reshape(row_count, HEADS, HD)
    value_heads = low(low_back(matmul(normed, value_weight))).reshape(row_count, HEADS, HD)
    query_heads = low(rotate(norm_rows(query_raw, query_gain)))
    key_heads = low(rotate(norm_rows(key_raw, key_gain)))
    valid_key = jnp.arange(row_count, dtype=jnp.int32) < length
    scores = jnp.einsum('qhd,khd->hqk', query_heads, key_heads, precision=HIGHEST) / math.sqrt(HD)
    scores = low_back(jnp.where(valid_key[None, None, :], scores, NEGATIVE))
    attention = jax.nn.softmax(scores, axis=-1)
    mixed_rows = jnp.einsum('hqk,khd->qhd', low(attention), value_heads, precision=HIGHEST).reshape(row_count, D)
    mixed_rows = low(low_back(mixed_rows))
    hidden = token_rows + low_back(matmul(mixed_rows, output_weight))
    routed_in = low(norm_rows(hidden, ffn_gain))
    gate_probs = jax.nn.softmax(low_back(matmul(routed_in, router_weight)), axis=-1)
    choose = (route[:, :, None] == jnp.arange(EXPERTS, dtype=jnp.int32)[None, None, :]).astype(jnp.float32)
    gate_values = lax.optimization_barrier(jnp.sum(choose * gate_probs[:, None, :], axis=-1))
    table = dispatch_table(route, priority).reshape(row_count, TOP, EXPERTS * CAP)
    sent_rows = low_back(jnp.einsum('tkc,td->cd', table, routed_in, precision=HIGHEST)).reshape(EXPERTS, CAP, D)
    gate_hidden = low_back(jnp.einsum('ecd,edf->ecf', sent_rows, gate_weight, precision=HIGHEST))
    up_hidden = low_back(jnp.einsum('ecd,edf->ecf', sent_rows, up_weight, precision=HIGHEST))
    active = low(jax.nn.silu(gate_hidden) * up_hidden)
    returned = low(low_back(jnp.einsum('ecf,efd->ecd', active, down_weight, precision=HIGHEST)))
    returned = returned.reshape(EXPERTS * CAP, D)
    picked = jnp.einsum('tkc,cd->tkd', table, returned, precision=HIGHEST)
    return hidden + lax.optimization_barrier(jnp.sum(gate_values[:, :, None] * picked, axis=1))

def reference(tokens, out_cotangent, lengths, routes, priority, attn_gain, query_weight, key_weight, value_weight, output_weight, query_gain, key_gain, ffn_gain, router_weight, gate_weight, up_weight, down_weight):
    params = tuple((item.astype(jnp.float32) for item in (attn_gain, query_weight, key_weight, value_weight, output_weight, query_gain, key_gain, ffn_gain, router_weight, gate_weight, up_weight, down_weight)))
    seq_total = MB * NSEQ
    group_size = math.gcd(seq_total, 8)

    def regroup(array):
        return array.reshape((seq_total // group_size, group_size) + array.shape[2:])

    def step(carry, pieces):
        token_rows, cotangent, length, route, order = pieces

        def forward(rows_in, weights):
            return jax.vmap(partial(sequence, weights=weights))(rows_in, length, route, order)
        results, pullback = jax.vjp(forward, token_rows.astype(jnp.float32), params)
        row_grad, weight_grad = pullback(cotangent.astype(jnp.float32))
        carry = jax.tree.map(jnp.add, carry, weight_grad)
        return (carry, (results.astype(jnp.bfloat16), row_grad))
    zeros = jax.tree.map(jnp.zeros_like, params)
    inputs = (regroup(tokens), regroup(out_cotangent), regroup(lengths), regroup(routes), regroup(priority))
    totals, (results, row_grads) = lax.scan(step, zeros, inputs)
    layer_out = results.reshape(MB, NSEQ, SEQ, D)
    tokens_grad = row_grads.reshape(MB, NSEQ, SEQ, D)
    return (layer_out, tokens_grad, totals[0], totals[1], totals[2], totals[3], totals[4], totals[5], totals[6], totals[7], totals[8], totals[9], totals[10], totals[11])
```

```python
import functools
import math

import jax
import jax.numpy as jnp
from jax import lax
from jax.experimental import pallas as pl
from jax.experimental.pallas import tpu as pltpu
from jax.sharding import Mesh
from jax.sharding import PartitionSpec as P

D = 2048
HEADS = 16
HD = 128
TOP = 8
EXTRA = 128

EPSILON = 1e-06
THETA = 50000.0
NEGATIVE = -1e30
BF = jnp.bfloat16
F32 = jnp.float32


def plain(left, right):
    return jnp.dot(left, right, preferred_element_type=F32)


def inner(left, right):
    return lax.dot_general(left, right, (((0,), (0,)), ((), ())), preferred_element_type=F32)


def times_t(left, right):
    return lax.dot_general(left, right, (((1,), (1,)), ((), ())), preferred_element_type=F32)


def shift(value, axis, step):
    size = lax.axis_size(axis)
    return lax.ppermute(value, axis, [(i, (i + step) % size) for i in range(size)])


def gather_blocks(block, order):
    held = {(): block}
    for axis in order:
        grown = {}
        for key, value in held.items():
            for k in range(lax.axis_size(axis)):
                if k:
                    value = shift(value, axis, 1)
                grown[key + (k,)] = value
        held = grown
    return held


def reduce_blocks(part, order):
    def reduce_from(key, depth):
        if depth == len(order):
            return part(key)
        axis = order[depth]
        size = lax.axis_size(axis)
        total = reduce_from(key + (size - 1,), depth + 1)
        for k in reversed(range(size - 1)):
            arrived = shift(total.astype(BF), axis, -1)
            total = reduce_from(key + (k,), depth + 1).astype(F32) + arrived.astype(F32)
        return total

    return reduce_from((), 0)


def place_kernel(count, row_axis, rows, offsets_ref, *refs):
    blocks, out, sems = refs[:count], refs[count], refs[count + 1]
    copies = []
    for i in range(count):
        start = pl.multiple_of(offsets_ref[i], 16)
        window = pl.ds(start, rows)
        target = out.at[window] if row_axis == 0 else out.at[:, window]
        copies.append(pltpu.make_async_copy(blocks[i], target, sems.at[i]))
    for copy in copies:
        copy.start()
    for copy in copies:
        copy.wait()


def place(blocks, offsets, row_axis):
    shape = list(blocks[0].shape)
    rows = shape[row_axis]
    shape[row_axis] = rows * len(blocks)
    return pl.pallas_call(
        functools.partial(place_kernel, len(blocks), row_axis, rows),
        out_shape=jax.ShapeDtypeStruct(tuple(shape), blocks[0].dtype),
        grid_spec=pltpu.PrefetchScalarGridSpec(
            num_scalar_prefetch=1,
            in_specs=[pl.BlockSpec(memory_space=pl.ANY)] * len(blocks),
            out_specs=pl.BlockSpec(memory_space=pl.ANY),
            scratch_shapes=[pltpu.SemaphoreType.DMA((len(blocks),))],
        ),
    )(jnp.stack(offsets).astype(jnp.int32), *blocks)


def rope_tables(row_count):
    half = HD // 2
    frequency = THETA ** (-jnp.arange(half, dtype=F32) / half)
    angles = jnp.arange(row_count, dtype=F32)[:, None] * frequency[None, :]
    cosine, sine = jnp.cos(angles), jnp.sin(angles)
    return jnp.concatenate([cosine, cosine], axis=1), jnp.concatenate([-sine, sine], axis=1)


def head_forward(raw, gain, cosine, sine):
    scale = lax.rsqrt(jnp.mean(raw * raw, axis=-1, keepdims=True) + EPSILON)
    unit = raw * scale
    value = unit * gain
    turned = value * cosine + pltpu.roll(value, HD // 2, 1) * sine
    return unit, scale, turned.astype(BF)


def head_backward(grad, unit, scale, gain, cosine, sine):
    grad = grad * cosine - pltpu.roll(grad, HD // 2, 1) * sine
    gain_grad = jnp.sum(grad * unit, axis=0, keepdims=True)
    grad = grad * gain
    grad = scale * (grad - unit * jnp.mean(grad * unit, axis=-1, keepdims=True))
    return grad.astype(BF), gain_grad


def attention_of(query, key, length):
    scores = times_t(query, key) * (1.0 / math.sqrt(HD))
    valid = lax.broadcasted_iota(jnp.int32, scores.shape, 1) < length
    scores = jnp.where(valid, scores, NEGATIVE)
    weight = jnp.exp(scores - jnp.max(scores, axis=-1, keepdims=True))
    return weight / jnp.sum(weight, axis=-1, keepdims=True)


def attend_kernel(heads, lengths_ref, qkv_ref, gains_ref, cosine_ref, sine_ref, mixed_ref):
    length = lengths_ref[pl.program_id(0)]
    cosine, sine = cosine_ref[...], sine_ref[...]
    query_gain, key_gain = gains_ref[0:1, :], gains_ref[1:2, :]
    width = heads * HD
    for h in range(heads):
        lo = h * HD
        query = head_forward(qkv_ref[:, lo : lo + HD], query_gain, cosine, sine)[2]
        key = head_forward(qkv_ref[:, width + lo : width + lo + HD], key_gain, cosine, sine)[2]
        value = qkv_ref[:, 2 * width + lo : 2 * width + lo + HD].astype(BF)
        attention = attention_of(query, key, length)
        mixed_ref[:, lo : lo + HD] = plain(attention.astype(BF), value).astype(BF)


def attend_back_kernel(
    heads, lengths_ref, qkv_ref, mixed_grad_ref, gains_ref, cosine_ref, sine_ref, out_ref, gain_ref
):
    @pl.when(pl.program_id(0) == 0)
    def _():
        gain_ref[...] = jnp.zeros_like(gain_ref)

    length = lengths_ref[pl.program_id(0)]
    cosine, sine = cosine_ref[...], sine_ref[...]
    query_gain, key_gain = gains_ref[0:1, :], gains_ref[1:2, :]
    width = heads * HD
    score_scale = 1.0 / math.sqrt(HD)
    for h in range(heads):
        lo = h * HD
        query_unit, query_scale, query = head_forward(
            qkv_ref[:, lo : lo + HD], query_gain, cosine, sine
        )
        key_unit, key_scale, key = head_forward(
            qkv_ref[:, width + lo : width + lo + HD], key_gain, cosine, sine
        )
        value = qkv_ref[:, 2 * width + lo : 2 * width + lo + HD].astype(BF)
        attention = attention_of(query, key, length)
        mixed_grad = mixed_grad_ref[:, lo : lo + HD]
        value_grad = inner(attention.astype(BF), mixed_grad)
        attention_grad = times_t(mixed_grad, value)
        score_grad = attention * (
            attention_grad - jnp.sum(attention * attention_grad, axis=-1, keepdims=True)
        )
        score_grad = score_grad.astype(BF)
        query_grad, query_gain_grad = head_backward(
            plain(score_grad, key) * score_scale, query_unit, query_scale, query_gain, cosine, sine
        )
        key_grad, key_gain_grad = head_backward(
            inner(score_grad, query) * score_scale, key_unit, key_scale, key_gain, cosine, sine
        )
        out_ref[:, lo : lo + HD] = query_grad
        out_ref[:, width + lo : width + lo + HD] = key_grad
        out_ref[:, 2 * width + lo : 2 * width + lo + HD] = value_grad.astype(BF)
        gain_ref[0:1, :] += query_gain_grad
        gain_ref[1:2, :] += key_gain_grad


def attend(qkv, lengths, gains, cosine, sine, rows, heads):
    sequences = qkv.shape[0] // rows
    width = heads * HD
    whole = pl.BlockSpec((2, HD), lambda s, n: (0, 0))
    table = pl.BlockSpec((rows, HD), lambda s, n: (0, 0))
    return pl.pallas_call(
        functools.partial(attend_kernel, heads),
        out_shape=jax.ShapeDtypeStruct((qkv.shape[0], width), BF),
        grid_spec=pltpu.PrefetchScalarGridSpec(
            num_scalar_prefetch=1,
            grid=(sequences,),
            in_specs=[
                pl.BlockSpec((rows, 3 * width), lambda s, n: (s, 0)),
                whole,
                table,
                table,
            ],
            out_specs=pl.BlockSpec((rows, width), lambda s, n: (s, 0)),
        ),
        compiler_params=pltpu.CompilerParams(vmem_limit_bytes=32 << 20),
    )(lengths, qkv, gains, cosine, sine)


def attend_back(qkv, mixed_grad, lengths, gains, cosine, sine, rows, heads):
    sequences = qkv.shape[0] // rows
    width = heads * HD
    whole = pl.BlockSpec((2, HD), lambda s, n: (0, 0))
    table = pl.BlockSpec((rows, HD), lambda s, n: (0, 0))
    return pl.pallas_call(
        functools.partial(attend_back_kernel, heads),
        out_shape=(
            jax.ShapeDtypeStruct((qkv.shape[0], 3 * width), BF),
            jax.ShapeDtypeStruct((2, HD), F32),
        ),
        grid_spec=pltpu.PrefetchScalarGridSpec(
            num_scalar_prefetch=1,
            grid=(sequences,),
            in_specs=[
                pl.BlockSpec((rows, 3 * width), lambda s, n: (s, 0)),
                pl.BlockSpec((rows, width), lambda s, n: (s, 0)),
                whole,
                table,
                table,
            ],
            out_specs=(
                pl.BlockSpec((rows, 3 * width), lambda s, n: (s, 0)),
                whole,
            ),
        ),
        compiler_params=pltpu.CompilerParams(vmem_limit_bytes=32 << 20),
    )(lengths, qkv, mixed_grad, gains, cosine, sine)


def norm_back(grad, unit, scale, gain):
    scaled = grad * gain
    values_grad = scale * (scaled - unit * jnp.mean(scaled * unit, axis=-1, keepdims=True))
    return values_grad, jnp.sum(grad * unit, axis=0)


def slot_ranks(route, priority, experts, capacity):
    rows = route.shape[0]
    expert = jnp.arange(experts, dtype=jnp.int32)
    chosen = route[:, :, None] == expert[None, None, :]
    order = jnp.sum(jnp.where(chosen, priority.reshape(rows, TOP)[:, :, None], 0), axis=1)
    routed = jnp.any(chosen, axis=1)
    order = jnp.where(routed, order, rows * TOP).T
    rank = jnp.sum((order[:, None, :] < order[:, :, None]).astype(jnp.int32), axis=2).T
    return jnp.where(routed & (rank < capacity), rank, -1)


def in_three(value):
    high = value.astype(BF)
    rest = value - high.astype(F32)
    middle = rest.astype(BF)
    low = (rest - middle.astype(F32)).astype(BF)
    return jnp.concatenate([high, middle, low], axis=-1)


def from_three(columns, count):
    return (
        columns[..., :count].astype(F32)
        + columns[..., count : 2 * count].astype(F32)
        + columns[..., 2 * count : 3 * count].astype(F32)
    )


def widen(columns, width):
    return jnp.pad(columns, ((0, 0), (0, width - columns.shape[-1])))


def shards(
    tokens,
    out_cotangent,
    lengths,
    routes,
    priority,
    attn_gain,
    query_weight,
    key_weight,
    value_weight,
    output_weight,
    query_gain,
    key_gain,
    ffn_gain,
    router_weight,
    gate_weight,
    up_weight,
    down_weight,
):
    batches, rows = tokens.shape[0], tokens.shape[2]
    own = batches * rows
    experts = router_weight.shape[1]
    capacity = 5 * rows * TOP // (4 * experts)
    local = gate_weight.shape[0]
    ys, zs, xs = lax.axis_size("y"), lax.axis_size("z"), lax.axis_size("x")
    y, c, z, x = (lax.axis_index(name) for name in ("y", "c", "z", "x"))
    shard_rows = query_weight.shape[0]
    head_shard = query_gain.shape[0]
    heads = HEADS // 2
    width = heads * HD
    chunk = D // (2 * ys)

    def swap(value):
        return lax.ppermute(value, "c", [(0, 1), (1, 0)])

    def half_columns(weight, core):
        return jnp.concatenate(
            [
                lax.dynamic_slice_in_dim(weight, (2 * i + core) * chunk, chunk, 1)
                for i in range(ys)
            ],
            axis=1,
        )

    token_rows = tokens.reshape(own, D)
    both_tokens = jnp.concatenate([token_rows, swap(token_rows)], axis=0)
    length = lengths.reshape(batches)
    both_lengths = jnp.concatenate([length, swap(length)])
    extra = jnp.concatenate(
        [
            attn_gain[:, None],
            ffn_gain[:, None],
            router_weight,
            jnp.pad(query_gain, (0, shard_rows - head_shard))[:, None],
            jnp.pad(key_gain, (0, shard_rows - head_shard))[:, None],
        ],
        axis=1,
    )
    extra = widen(extra, EXTRA)

    def packed(core):
        return jnp.concatenate(
            [half_columns(w, core) for w in (query_weight, key_weight, value_weight)] + [extra],
            axis=1,
        )

    mine, theirs = packed(c), swap(packed(1 - c))
    first = jnp.where(c == 0, mine, theirs)
    second = jnp.where(c == 0, theirs, mine)

    def row_block(key, order, core):
        at = dict(zip(order, key, strict=True))
        ky = jnp.mod(y - at["y"], ys)
        kz = jnp.mod(z - at["z"], zs)
        kx = jnp.mod(x - at["x"], xs)
        if core is None:
            return (ky * zs + kz) * xs + kx
        return ((ky * 2 + core) * zs + kz) * xs + kx

    ZXY, ZYX = ("z", "x", "y"), ("z", "y", "x")
    blocks, offsets = [], []
    for core, order, block in ((0, ZXY, first), (1, ZYX, second)):
        for key, value in gather_blocks(block, order).items():
            blocks.append(value)
            offsets.append(row_block(key, order, core) * shard_rows)
    qkv_weight = place(blocks, offsets, 0)
    blocks, offsets = [], []
    for key, value in gather_blocks(output_weight, ZYX).items():
        blocks.append(value)
        offsets.append(row_block(key, ZYX, None) * shard_rows)
    out_weight = place(blocks, offsets, 0)

    full_experts = []
    for weight in (gate_weight, up_weight, down_weight):
        blocks, offsets = [], []
        for key, value in gather_blocks(weight, ("y", "c")).items():
            blocks.append(value)
            offsets.append(
                (jnp.mod(y - key[0], ys) * 2 + jnp.mod(c - key[1], 2)) * weight.shape[1]
            )
        full_experts.append(place(blocks, offsets, 1))
    gate_full, up_full, down_full = full_experts

    ranks = jnp.concatenate(
        [
            slot_ranks(routes[b, 0], priority[b, 0], experts, capacity)
            for b in range(batches)
        ],
        axis=0,
    )
    cotangent = out_cotangent.reshape(own, D)
    ZX = ("z", "x")
    cot_blocks = gather_blocks(
        jnp.concatenate([cotangent, widen(ranks.astype(BF), EXTRA)], axis=1), ZX
    )

    small = qkv_weight[:, 3 * width :].astype(F32)
    qkv_weight = qkv_weight[:, : 3 * width]
    attn_gain_f = small[:, 0][None, :]
    ffn_gain_f = small[:, 1][None, :]
    router = small[:, 2 : 2 + experts].astype(BF)
    per_device = small.reshape(-1, shard_rows, EXTRA)[:, :head_shard]
    head_gains = jnp.stack(
        [per_device[:, :, 2 + experts].reshape(HD), per_device[:, :, 3 + experts].reshape(HD)]
    )
    tokens_f = both_tokens.astype(F32)
    token_scale = lax.rsqrt(jnp.mean(tokens_f * tokens_f, axis=-1, keepdims=True) + EPSILON)
    normed = (tokens_f * token_scale * attn_gain_f).astype(BF)
    qkv = plain(normed, qkv_weight)
    cosine, sine = rope_tables(rows)
    mixed = attend(qkv, both_lengths, head_gains, cosine, sine, rows, heads)
    partial = plain(mixed, out_weight)
    rows_f = token_rows.astype(F32)
    hidden = rows_f + (partial[:own] + swap(partial[own:]))
    hidden_scale = lax.rsqrt(jnp.mean(hidden * hidden, axis=-1, keepdims=True) + EPSILON)
    hidden_unit = hidden * hidden_scale
    routed_in = (hidden_unit * ffn_gain_f).astype(BF)
    gate_probs = jax.nn.softmax(plain(routed_in, router), axis=-1)

    row_blocks = gather_blocks(
        jnp.concatenate([routed_in, widen(in_three(gate_probs), EXTRA)], axis=1), ZX
    )
    keys = list(row_blocks)
    group = len(keys) * batches
    all_rows = jnp.concatenate([row_blocks[k] for k in keys], axis=0)
    all_cots = jnp.concatenate([cot_blocks[k] for k in keys], axis=0)
    first_expert = (z * xs + x) * local
    all_probs = from_three(all_rows[:, D:], experts)
    all_probs = lax.dynamic_slice_in_dim(all_probs, first_expert, local, 1)
    all_ranks = lax.dynamic_slice_in_dim(all_cots[:, D:], first_expert, local, 1).astype(F32)
    all_rows = all_rows[:, :D].reshape(group, rows, D)
    all_cots = all_cots[:, :D].reshape(group, rows, D)
    slot = jnp.arange(capacity, dtype=F32)[None, :, None]
    combined = 0.0
    routed_grad = 0.0
    probs_grad = []
    gate_grads, up_grads, down_grads = [], [], []
    dispatch = (((2,), (1,)), ((0,), (0,)))
    collect = (((1,), (1,)), ((0,), (0,)))
    for j in range(local):
        rank = all_ranks[:, j].reshape(group, 1, rows)
        probs = all_probs[:, j].reshape(group, 1, rows)
        chosen = rank == slot
        onehot = chosen.astype(BF)
        gated = jnp.where(chosen, probs, 0.0)
        gate_slot = jnp.sum(gated, axis=2, keepdims=True)
        sent = lax.dot_general(onehot, all_rows, dispatch, preferred_element_type=F32)
        sent = sent.astype(BF).reshape(group * capacity, D)
        cot = lax.dot_general(onehot, all_cots, dispatch, preferred_element_type=F32)
        returned_grad = (cot * gate_slot).astype(BF).reshape(group * capacity, D)
        gate_hidden = plain(sent, gate_full[j])
        up_hidden = plain(sent, up_full[j])
        sigmoid = jax.nn.sigmoid(gate_hidden)
        active = (gate_hidden * sigmoid * up_hidden).astype(BF)
        returned = plain(active, down_full[j]).astype(BF).reshape(group, capacity, D)
        combined = combined + lax.dot_general(
            gated.astype(BF), returned, collect, preferred_element_type=F32
        )
        gates_grad = jnp.sum(cot * returned.astype(F32), axis=2, keepdims=True)
        probs_grad.append(jnp.sum(jnp.where(chosen, gates_grad, 0.0), axis=1).reshape(-1, 1))
        active_grad = times_t(returned_grad, down_full[j])
        gate_hidden_grad = (
            active_grad * up_hidden * sigmoid * (1.0 + gate_hidden * (1.0 - sigmoid))
        ).astype(BF)
        up_hidden_grad = (active_grad * gate_hidden * sigmoid).astype(BF)
        sent_grad = times_t(gate_hidden_grad, gate_full[j]) + times_t(up_hidden_grad, up_full[j])
        sent_grad = sent_grad.astype(BF).reshape(group, capacity, D)
        routed_grad = routed_grad + lax.dot_general(
            onehot, sent_grad, collect, preferred_element_type=F32
        )
        down_grads.append(inner(active, returned_grad))
        gate_grads.append(inner(sent, gate_hidden_grad))
        up_grads.append(inner(sent, up_hidden_grad))
    expert_index = jnp.arange(experts)[None, :]
    probs_part = sum(
        jnp.where(expert_index == first_expert + j, probs_grad[j], 0.0) for j in range(local)
    )
    back = jnp.concatenate(
        [
            routed_grad.reshape(group * rows, D).astype(BF),
            widen(in_three(probs_part), EXTRA),
        ],
        axis=1,
    )
    combined = combined.reshape(group * rows, D).astype(BF)

    def part_of(array):
        return lambda key: array[keys.index(key) * own : (keys.index(key) + 1) * own]

    back = reduce_blocks(part_of(back), ZX)
    combined = reduce_blocks(part_of(combined), ZX)
    layer_out = (hidden + combined).astype(BF)

    probs_grad = from_three(back[:, D:], experts)
    logits_grad = (
        gate_probs * (probs_grad - jnp.sum(gate_probs * probs_grad, axis=-1, keepdims=True))
    ).astype(BF)
    router_grad = inner(routed_in, logits_grad)
    routed_grad = back[:, :D] + times_t(logits_grad, router)
    hidden_add, ffn_gain_grad = norm_back(routed_grad, hidden_unit, hidden_scale, ffn_gain_f)
    hidden_grad = cotangent.astype(F32) + hidden_add
    attn_out_grad = hidden_grad.astype(BF)

    both_grads = jnp.concatenate([attn_out_grad, swap(attn_out_grad)], axis=0)
    mixed_grad = times_t(both_grads, out_weight).astype(BF)
    output_grad = inner(mixed, both_grads).astype(BF)
    qkv_grad, head_gain_grads = attend_back(
        qkv, mixed_grad, both_lengths, head_gains, cosine, sine, rows, heads
    )
    qkv_weight_grad = inner(normed, qkv_grad)
    normed_part = times_t(qkv_grad, qkv_weight)
    normed_grad = normed_part[:own] + swap(normed_part[own:])
    token_unit = rows_f * token_scale[:own]
    tokens_add, attn_gain_grad = norm_back(normed_grad, token_unit, token_scale[:own], attn_gain_f)
    tokens_grad = hidden_grad + tokens_add

    small_grad = jnp.concatenate(
        [
            attn_gain_grad[:, None],
            ffn_gain_grad[:, None],
            router_grad,
            jnp.pad(
                head_gain_grads.reshape(2, -1, head_shard),
                ((0, 0), (0, 0), (0, shard_rows - head_shard)),
            )
            .reshape(2, D)
            .T,
        ],
        axis=1,
    )
    qkv_weight_grad = jnp.concatenate(
        [qkv_weight_grad.astype(BF), widen(small_grad, EXTRA).astype(BF)], axis=1
    )

    def rows_of(array, order, core):
        return lambda key: lax.dynamic_slice_in_dim(
            array, row_block(key, order, core) * shard_rows, shard_rows, 0
        )

    output_weight_grad = reduce_blocks(rows_of(output_grad, ZYX, None), ZYX)
    first = reduce_blocks(rows_of(qkv_weight_grad, ZXY, 0), ZXY)
    second = reduce_blocks(rows_of(qkv_weight_grad, ZYX, 1), ZYX)
    mine = jnp.where(c == 0, first, second)
    theirs = swap(jnp.where(c == 0, second, first).astype(BF)).astype(F32)
    small_total = mine[:, 3 * width :] + theirs[:, 3 * width :]

    def both_halves(at):
        low = jnp.where(c == 0, mine, theirs)[:, at * width : (at + 1) * width]
        high = jnp.where(c == 0, theirs, mine)[:, at * width : (at + 1) * width]
        return jnp.stack(
            [low.reshape(shard_rows, ys, chunk), high.reshape(shard_rows, ys, chunk)], axis=2
        ).reshape(shard_rows, D)

    def expert_total(parts):
        grad = jnp.stack(parts).astype(BF)
        depth = grad.shape[1] // (2 * ys)

        def part(key):
            at = jnp.mod(y - key[0], ys) * 2 + jnp.mod(c - key[1], 2)
            return lax.dynamic_slice_in_dim(grad, at * depth, depth, 1)

        return reduce_blocks(part, ("y", "c")).astype(F32)

    shape = (batches, 1, rows, D)
    return (
        layer_out.reshape(shape),
        tokens_grad.reshape(shape),
        small_total[:, 0],
        both_halves(0),
        both_halves(1),
        both_halves(2),
        output_weight_grad,
        small_total[:head_shard, 2 + experts],
        small_total[:head_shard, 3 + experts],
        small_total[:, 1],
        small_total[:, 2 : 2 + experts],
        expert_total(gate_grads),
        expert_total(up_grads),
        expert_total(down_grads),
    )


def solution(mesh):
    dp, expert = mesh.shape["dp"], mesh.shape["expert"]
    zs = math.gcd(expert, 4)
    grid = Mesh(
        mesh.devices.reshape(dp // 2, 2, zs, expert // zs),
        ("y", "c", "z", "x"),
    )
    every, dps, exps = ("y", "c", "z", "x"), ("y", "c"), ("z", "x")
    in_specs = (
        P(None, every, None, None),
        P(None, every, None, None),
        P(None, every),
        P(None, every, None, None),
        P(None, every, None),
        P(every),
        P(every, None),
        P(every, None),
        P(every, None),
        P(every, None),
        P(every),
        P(every),
        P(every),
        P(every, None),
        P(exps, dps, None),
        P(exps, dps, None),
        P(exps, dps, None),
    )
    out_specs = (
        P(None, every, None, None),
        P(None, every, None, None),
        P(every),
        P(every, None),
        P(every, None),
        P(every, None),
        P(every, None),
        P(every),
        P(every),
        P(every),
        P(every, None),
        P(exps, dps, None),
        P(exps, dps, None),
        P(exps, dps, None),
    )
    return jax.shard_map(shards, mesh=grid, in_specs=in_specs, out_specs=out_specs, check_vma=False)
```

```python
import functools
import math

import jax
import jax.numpy as jnp
from jax import lax
from jax.experimental import pallas as pl
from jax.experimental.pallas import tpu as pltpu
from jax.sharding import Mesh
from jax.sharding import PartitionSpec as P

D = 2048
HEADS = 16
HD = 128
TOP = 8
EXTRA = 128

EPSILON = 1e-06
THETA = 50000.0
NEGATIVE = -1e30
BF = jnp.bfloat16
F32 = jnp.float32


def plain(left, right):
    return jnp.dot(left, right, preferred_element_type=F32)


def inner(left, right):
    return lax.dot_general(left, right, (((0,), (0,)), ((), ())), preferred_element_type=F32)


def times_t(left, right):
    return lax.dot_general(left, right, (((1,), (1,)), ((), ())), preferred_element_type=F32)


def shift(value, axis, step):
    size = lax.axis_size(axis)
    return lax.ppermute(value, axis, [(i, (i + step) % size) for i in range(size)])


def gather_blocks(block, order):
    held = {(): block}
    for axis in order:
        grown = {}
        for key, value in held.items():
            for k in range(lax.axis_size(axis)):
                if k:
                    value = shift(value, axis, 1)
                grown[key + (k,)] = value
        held = grown
    return held


def reduce_blocks(part, order):
    def reduce_from(key, depth):
        if depth == len(order):
            return part(key)
        axis = order[depth]
        size = lax.axis_size(axis)
        total = reduce_from(key + (size - 1,), depth + 1)
        for k in reversed(range(size - 1)):
            arrived = shift(total.astype(BF), axis, -1)
            total = reduce_from(key + (k,), depth + 1).astype(F32) + arrived.astype(F32)
        return total

    return reduce_from((), 0)


def place_kernel(count, row_axis, rows, offsets_ref, *refs):
    blocks, out, sems = refs[:count], refs[count], refs[count + 1]
    copies = []
    for i in range(count):
        start = pl.multiple_of(offsets_ref[i], 16)
        window = pl.ds(start, rows)
        target = out.at[window] if row_axis == 0 else out.at[:, window]
        copies.append(pltpu.make_async_copy(blocks[i], target, sems.at[i]))
    for copy in copies:
        copy.start()
    for copy in copies:
        copy.wait()


def place(blocks, offsets, row_axis):
    shape = list(blocks[0].shape)
    rows = shape[row_axis]
    shape[row_axis] = rows * len(blocks)
    return pl.pallas_call(
        functools.partial(place_kernel, len(blocks), row_axis, rows),
        out_shape=jax.ShapeDtypeStruct(tuple(shape), blocks[0].dtype),
        grid_spec=pltpu.PrefetchScalarGridSpec(
            num_scalar_prefetch=1,
            in_specs=[pl.BlockSpec(memory_space=pl.ANY)] * len(blocks),
            out_specs=pl.BlockSpec(memory_space=pltpu.VMEM),
            scratch_shapes=[pltpu.SemaphoreType.DMA((len(blocks),))],
        ),
        compiler_params=pltpu.CompilerParams(vmem_limit_bytes=24 << 20),
    )(jnp.stack(offsets).astype(jnp.int32), *blocks)


def rope_tables(row_count):
    half = HD // 2
    frequency = THETA ** (-jnp.arange(half, dtype=F32) / half)
    angles = jnp.arange(row_count, dtype=F32)[:, None] * frequency[None, :]
    cosine, sine = jnp.cos(angles), jnp.sin(angles)
    return jnp.concatenate([cosine, cosine], axis=1), jnp.concatenate([-sine, sine], axis=1)


def head_forward(raw, gain, cosine, sine):
    scale = lax.rsqrt(jnp.mean(raw * raw, axis=-1, keepdims=True) + EPSILON)
    unit = raw * scale
    value = unit * gain
    turned = value * cosine + pltpu.roll(value, HD // 2, 1) * sine
    return unit, scale, turned.astype(BF)


def head_backward(grad, unit, scale, gain, cosine, sine):
    grad = grad * cosine - pltpu.roll(grad, HD // 2, 1) * sine
    gain_grad = jnp.sum(grad * unit, axis=0, keepdims=True)
    grad = grad * gain
    grad = scale * (grad - unit * jnp.mean(grad * unit, axis=-1, keepdims=True))
    return grad.astype(BF), gain_grad


def attention_of(query, key, length):
    scores = times_t(query, key) * (1.0 / math.sqrt(HD))
    valid = lax.broadcasted_iota(jnp.int32, scores.shape, 1) < length
    scores = jnp.where(valid, scores, NEGATIVE)
    weight = jnp.exp(scores - jnp.max(scores, axis=-1, keepdims=True))
    return weight / jnp.sum(weight, axis=-1, keepdims=True)


def attend_kernel(heads, lengths_ref, qkv_ref, gains_ref, cosine_ref, sine_ref, mixed_ref):
    length = lengths_ref[pl.program_id(0)]
    cosine, sine = cosine_ref[...], sine_ref[...]
    query_gain, key_gain = gains_ref[0:1, :], gains_ref[1:2, :]
    width = heads * HD
    for h in range(heads):
        lo = h * HD
        query = head_forward(qkv_ref[:, lo : lo + HD], query_gain, cosine, sine)[2]
        key = head_forward(qkv_ref[:, width + lo : width + lo + HD], key_gain, cosine, sine)[2]
        value = qkv_ref[:, 2 * width + lo : 2 * width + lo + HD].astype(BF)
        attention = attention_of(query, key, length)
        mixed_ref[:, lo : lo + HD] = plain(attention.astype(BF), value).astype(BF)


def attend_back_kernel(
    heads, lengths_ref, qkv_ref, mixed_grad_ref, gains_ref, cosine_ref, sine_ref, out_ref, gain_ref
):
    @pl.when(pl.program_id(0) == 0)
    def _():
        gain_ref[...] = jnp.zeros_like(gain_ref)

    length = lengths_ref[pl.program_id(0)]
    cosine, sine = cosine_ref[...], sine_ref[...]
    query_gain, key_gain = gains_ref[0:1, :], gains_ref[1:2, :]
    width = heads * HD
    score_scale = 1.0 / math.sqrt(HD)
    for h in range(heads):
        lo = h * HD
        query_unit, query_scale, query = head_forward(
            qkv_ref[:, lo : lo + HD], query_gain, cosine, sine
        )
        key_unit, key_scale, key = head_forward(
            qkv_ref[:, width + lo : width + lo + HD], key_gain, cosine, sine
        )
        value = qkv_ref[:, 2 * width + lo : 2 * width + lo + HD].astype(BF)
        attention = attention_of(query, key, length)
        mixed_grad = mixed_grad_ref[:, lo : lo + HD]
        value_grad = inner(attention.astype(BF), mixed_grad)
        attention_grad = times_t(mixed_grad, value)
        score_grad = attention * (
            attention_grad - jnp.sum(attention * attention_grad, axis=-1, keepdims=True)
        )
        score_grad = score_grad.astype(BF)
        query_grad, query_gain_grad = head_backward(
            plain(score_grad, key) * score_scale, query_unit, query_scale, query_gain, cosine, sine
        )
        key_grad, key_gain_grad = head_backward(
            inner(score_grad, query) * score_scale, key_unit, key_scale, key_gain, cosine, sine
        )
        out_ref[:, lo : lo + HD] = query_grad
        out_ref[:, width + lo : width + lo + HD] = key_grad
        out_ref[:, 2 * width + lo : 2 * width + lo + HD] = value_grad.astype(BF)
        gain_ref[0:1, :] += query_gain_grad
        gain_ref[1:2, :] += key_gain_grad


def attend(qkv, lengths, gains, cosine, sine, rows, heads):
    sequences = qkv.shape[0] // rows
    width = heads * HD
    whole = pl.BlockSpec((2, HD), lambda s, n: (0, 0))
    table = pl.BlockSpec((rows, HD), lambda s, n: (0, 0))
    return pl.pallas_call(
        functools.partial(attend_kernel, heads),
        out_shape=jax.ShapeDtypeStruct((qkv.shape[0], width), BF),
        grid_spec=pltpu.PrefetchScalarGridSpec(
            num_scalar_prefetch=1,
            grid=(sequences,),
            in_specs=[
                pl.BlockSpec((rows, 3 * width), lambda s, n: (s, 0)),
                whole,
                table,
                table,
            ],
            out_specs=pl.BlockSpec((rows, width), lambda s, n: (s, 0)),
        ),
        compiler_params=pltpu.CompilerParams(vmem_limit_bytes=32 << 20),
    )(lengths, qkv, gains, cosine, sine)


def attend_back(qkv, mixed_grad, lengths, gains, cosine, sine, rows, heads):
    sequences = qkv.shape[0] // rows
    width = heads * HD
    whole = pl.BlockSpec((2, HD), lambda s, n: (0, 0))
    table = pl.BlockSpec((rows, HD), lambda s, n: (0, 0))
    return pl.pallas_call(
        functools.partial(attend_back_kernel, heads),
        out_shape=(
            jax.ShapeDtypeStruct((qkv.shape[0], 3 * width), BF),
            jax.ShapeDtypeStruct((2, HD), F32),
        ),
        grid_spec=pltpu.PrefetchScalarGridSpec(
            num_scalar_prefetch=1,
            grid=(sequences,),
            in_specs=[
                pl.BlockSpec((rows, 3 * width), lambda s, n: (s, 0)),
                pl.BlockSpec((rows, width), lambda s, n: (s, 0)),
                whole,
                table,
                table,
            ],
            out_specs=(
                pl.BlockSpec((rows, 3 * width), lambda s, n: (s, 0)),
                whole,
            ),
        ),
        compiler_params=pltpu.CompilerParams(vmem_limit_bytes=32 << 20),
    )(lengths, qkv, mixed_grad, gains, cosine, sine)


def norm_back(grad, unit, scale, gain):
    scaled = grad * gain
    values_grad = scale * (scaled - unit * jnp.mean(scaled * unit, axis=-1, keepdims=True))
    return values_grad, jnp.sum(grad * unit, axis=0)


def slot_ranks(route, priority, experts, capacity):
    rows = route.shape[0]
    expert = jnp.arange(experts, dtype=jnp.int32)
    chosen = route[:, :, None] == expert[None, None, :]
    order = jnp.sum(jnp.where(chosen, priority.reshape(rows, TOP)[:, :, None], 0), axis=1)
    routed = jnp.any(chosen, axis=1)
    order = jnp.where(routed, order, rows * TOP).T
    rank = jnp.sum((order[:, None, :] < order[:, :, None]).astype(jnp.int32), axis=2).T
    return jnp.where(routed & (rank < capacity), rank, -1)


def in_three(value):
    high = value.astype(BF)
    rest = value - high.astype(F32)
    middle = rest.astype(BF)
    low = (rest - middle.astype(F32)).astype(BF)
    return jnp.concatenate([high, middle, low], axis=-1)


def from_three(columns, count):
    return (
        columns[..., :count].astype(F32)
        + columns[..., count : 2 * count].astype(F32)
        + columns[..., 2 * count : 3 * count].astype(F32)
    )


def widen(columns, width):
    return jnp.pad(columns, ((0, 0), (0, width - columns.shape[-1])))


def shards(
    tokens,
    out_cotangent,
    lengths,
    routes,
    priority,
    attn_gain,
    query_weight,
    key_weight,
    value_weight,
    output_weight,
    query_gain,
    key_gain,
    ffn_gain,
    router_weight,
    gate_weight,
    up_weight,
    down_weight,
):
    batches, rows = tokens.shape[0], tokens.shape[2]
    own = batches * rows
    experts = router_weight.shape[1]
    capacity = 5 * rows * TOP // (4 * experts)
    local = gate_weight.shape[0]
    ys, zs, xs = lax.axis_size("y"), lax.axis_size("z"), lax.axis_size("x")
    y, c, z, x = (lax.axis_index(name) for name in ("y", "c", "z", "x"))
    shard_rows = query_weight.shape[0]
    head_shard = query_gain.shape[0]
    heads = HEADS // 2
    width = heads * HD
    chunk = D // (2 * ys)

    def swap(value):
        return lax.ppermute(value, "c", [(0, 1), (1, 0)])

    def half_columns(weight, core):
        return jnp.concatenate(
            [
                lax.dynamic_slice_in_dim(weight, (2 * i + core) * chunk, chunk, 1)
                for i in range(ys)
            ],
            axis=1,
        )

    token_rows = tokens.reshape(own, D)
    both_tokens = jnp.concatenate([token_rows, swap(token_rows)], axis=0)
    length = lengths.reshape(batches)
    both_lengths = jnp.concatenate([length, swap(length)])
    extra = jnp.concatenate(
        [
            attn_gain[:, None],
            ffn_gain[:, None],
            router_weight,
            jnp.pad(query_gain, (0, shard_rows - head_shard))[:, None],
            jnp.pad(key_gain, (0, shard_rows - head_shard))[:, None],
        ],
        axis=1,
    )
    extra = widen(extra, EXTRA)

    def packed(core):
        return jnp.concatenate(
            [half_columns(w, core) for w in (query_weight, key_weight, value_weight)] + [extra],
            axis=1,
        )

    mine, theirs = packed(c), swap(packed(1 - c))
    first = jnp.where(c == 0, mine, theirs)
    second = jnp.where(c == 0, theirs, mine)

    def row_block(key, order, core):
        at = dict(zip(order, key, strict=True))
        ky = jnp.mod(y - at["y"], ys)
        kz = jnp.mod(z - at["z"], zs)
        kx = jnp.mod(x - at["x"], xs)
        if core is None:
            return (ky * zs + kz) * xs + kx
        return ((ky * 2 + core) * zs + kz) * xs + kx

    ZXY, ZYX = ("z", "x", "y"), ("z", "y", "x")
    blocks, offsets = [], []
    for core, order, block in ((0, ZXY, first), (1, ZYX, second)):
        for key, value in gather_blocks(block, order).items():
            blocks.append(value)
            offsets.append(row_block(key, order, core) * shard_rows)
    qkv_weight = place(blocks, offsets, 0)
    blocks, offsets = [], []
    for key, value in gather_blocks(output_weight, ZYX).items():
        blocks.append(value)
        offsets.append(row_block(key, ZYX, None) * shard_rows)
    out_weight = place(blocks, offsets, 0)

    full_experts = []
    for weight in (gate_weight, up_weight, down_weight):
        blocks, offsets = [], []
        for key, value in gather_blocks(weight, ("y", "c")).items():
            blocks.append(value)
            offsets.append(
                (jnp.mod(y - key[0], ys) * 2 + jnp.mod(c - key[1], 2)) * weight.shape[1]
            )
        full_experts.append(place(blocks, offsets, 1))
    gate_full, up_full, down_full = full_experts

    ranks = jnp.concatenate(
        [
            slot_ranks(routes[b, 0], priority[b, 0], experts, capacity)
            for b in range(batches)
        ],
        axis=0,
    )
    cotangent = out_cotangent.reshape(own, D)
    ZX = ("z", "x")
    cot_blocks = gather_blocks(
        jnp.concatenate([cotangent, widen(ranks.astype(BF), EXTRA)], axis=1), ZX
    )

    small = qkv_weight[:, 3 * width :].astype(F32)
    qkv_weight = qkv_weight[:, : 3 * width]
    attn_gain_f = small[:, 0][None, :]
    ffn_gain_f = small[:, 1][None, :]
    router = small[:, 2 : 2 + experts].astype(BF)
    per_device = small.reshape(-1, shard_rows, EXTRA)[:, :head_shard]
    head_gains = jnp.stack(
        [per_device[:, :, 2 + experts].reshape(HD), per_device[:, :, 3 + experts].reshape(HD)]
    )
    tokens_f = both_tokens.astype(F32)
    token_scale = lax.rsqrt(jnp.mean(tokens_f * tokens_f, axis=-1, keepdims=True) + EPSILON)
    normed = (tokens_f * token_scale * attn_gain_f).astype(BF)
    qkv = plain(normed, qkv_weight)
    cosine, sine = rope_tables(rows)
    mixed = attend(qkv, both_lengths, head_gains, cosine, sine, rows, heads)
    partial = plain(mixed, out_weight)
    rows_f = token_rows.astype(F32)
    hidden = rows_f + (partial[:own] + swap(partial[own:]))
    hidden_scale = lax.rsqrt(jnp.mean(hidden * hidden, axis=-1, keepdims=True) + EPSILON)
    hidden_unit = hidden * hidden_scale
    routed_in = (hidden_unit * ffn_gain_f).astype(BF)
    gate_probs = jax.nn.softmax(plain(routed_in, router), axis=-1)

    row_blocks = gather_blocks(
        jnp.concatenate([routed_in, widen(in_three(gate_probs), EXTRA)], axis=1), ZX
    )
    keys = list(row_blocks)
    group = len(keys) * batches
    all_rows = jnp.concatenate([row_blocks[k] for k in keys], axis=0)
    all_cots = jnp.concatenate([cot_blocks[k] for k in keys], axis=0)
    first_expert = (z * xs + x) * local
    all_probs = from_three(all_rows[:, D:], experts)
    all_probs = lax.dynamic_slice_in_dim(all_probs, first_expert, local, 1)
    all_ranks = lax.dynamic_slice_in_dim(all_cots[:, D:], first_expert, local, 1).astype(F32)
    all_rows = all_rows[:, :D].reshape(group, rows, D)
    all_cots = all_cots[:, :D].reshape(group, rows, D)
    slot = jnp.arange(capacity, dtype=F32)[None, :, None]
    combined = 0.0
    routed_grad = 0.0
    probs_grad = []
    gate_grads, up_grads, down_grads = [], [], []
    dispatch = (((2,), (1,)), ((0,), (0,)))
    collect = (((1,), (1,)), ((0,), (0,)))
    for j in range(local):
        rank = all_ranks[:, j].reshape(group, 1, rows)
        probs = all_probs[:, j].reshape(group, 1, rows)
        chosen = rank == slot
        onehot = chosen.astype(BF)
        gated = jnp.where(chosen, probs, 0.0)
        gate_slot = jnp.sum(gated, axis=2, keepdims=True)
        sent = lax.dot_general(onehot, all_rows, dispatch, preferred_element_type=F32)
        sent = sent.astype(BF).reshape(group * capacity, D)
        cot = lax.dot_general(onehot, all_cots, dispatch, preferred_element_type=F32)
        returned_grad = (cot * gate_slot).astype(BF).reshape(group * capacity, D)
        gate_hidden = plain(sent, gate_full[j])
        up_hidden = plain(sent, up_full[j])
        sigmoid = jax.nn.sigmoid(gate_hidden)
        active = (gate_hidden * sigmoid * up_hidden).astype(BF)
        returned = plain(active, down_full[j]).astype(BF).reshape(group, capacity, D)
        combined = combined + lax.dot_general(
            gated.astype(BF), returned, collect, preferred_element_type=F32
        )
        gates_grad = jnp.sum(cot * returned.astype(F32), axis=2, keepdims=True)
        probs_grad.append(jnp.sum(jnp.where(chosen, gates_grad, 0.0), axis=1).reshape(-1, 1))
        active_grad = times_t(returned_grad, down_full[j])
        gate_hidden_grad = (
            active_grad * up_hidden * sigmoid * (1.0 + gate_hidden * (1.0 - sigmoid))
        ).astype(BF)
        up_hidden_grad = (active_grad * gate_hidden * sigmoid).astype(BF)
        sent_grad = times_t(gate_hidden_grad, gate_full[j]) + times_t(up_hidden_grad, up_full[j])
        sent_grad = sent_grad.astype(BF).reshape(group, capacity, D)
        routed_grad = routed_grad + lax.dot_general(
            onehot, sent_grad, collect, preferred_element_type=F32
        )
        down_grads.append(inner(active, returned_grad))
        gate_grads.append(inner(sent, gate_hidden_grad))
        up_grads.append(inner(sent, up_hidden_grad))
    expert_index = jnp.arange(experts)[None, :]
    probs_part = sum(
        jnp.where(expert_index == first_expert + j, probs_grad[j], 0.0) for j in range(local)
    )
    back = jnp.concatenate(
        [
            routed_grad.reshape(group * rows, D).astype(BF),
            widen(in_three(probs_part), EXTRA),
        ],
        axis=1,
    )
    combined = combined.reshape(group * rows, D).astype(BF)

    def part_of(array):
        return lambda key: array[keys.index(key) * own : (keys.index(key) + 1) * own]

    back = reduce_blocks(part_of(back), ZX)
    combined = reduce_blocks(part_of(combined), ZX)
    layer_out = (hidden + combined).astype(BF)

    probs_grad = from_three(back[:, D:], experts)
    logits_grad = (
        gate_probs * (probs_grad - jnp.sum(gate_probs * probs_grad, axis=-1, keepdims=True))
    ).astype(BF)
    router_grad = inner(routed_in, logits_grad)
    routed_grad = back[:, :D] + times_t(logits_grad, router)
    hidden_add, ffn_gain_grad = norm_back(routed_grad, hidden_unit, hidden_scale, ffn_gain_f)
    hidden_grad = cotangent.astype(F32) + hidden_add
    attn_out_grad = hidden_grad.astype(BF)

    both_grads = jnp.concatenate([attn_out_grad, swap(attn_out_grad)], axis=0)
    mixed_grad = times_t(both_grads, out_weight).astype(BF)
    output_grad = inner(mixed, both_grads).astype(BF)
    qkv_grad, head_gain_grads = attend_back(
        qkv, mixed_grad, both_lengths, head_gains, cosine, sine, rows, heads
    )
    qkv_weight_grad = inner(normed, qkv_grad)
    normed_part = times_t(qkv_grad, qkv_weight)
    normed_grad = normed_part[:own] + swap(normed_part[own:])
    token_unit = rows_f * token_scale[:own]
    tokens_add, attn_gain_grad = norm_back(normed_grad, token_unit, token_scale[:own], attn_gain_f)
    tokens_grad = hidden_grad + tokens_add

    small_grad = jnp.concatenate(
        [
            attn_gain_grad[:, None],
            ffn_gain_grad[:, None],
            router_grad,
            jnp.pad(
                head_gain_grads.reshape(2, -1, head_shard),
                ((0, 0), (0, 0), (0, shard_rows - head_shard)),
            )
            .reshape(2, D)
            .T,
        ],
        axis=1,
    )
    qkv_weight_grad = jnp.concatenate(
        [qkv_weight_grad.astype(BF), widen(small_grad, EXTRA).astype(BF)], axis=1
    )

    def rows_of(array, order, core):
        return lambda key: lax.dynamic_slice_in_dim(
            array, row_block(key, order, core) * shard_rows, shard_rows, 0
        )

    output_weight_grad = reduce_blocks(rows_of(output_grad, ZYX, None), ZYX)
    first = reduce_blocks(rows_of(qkv_weight_grad, ZXY, 0), ZXY)
    second = reduce_blocks(rows_of(qkv_weight_grad, ZYX, 1), ZYX)
    mine = jnp.where(c == 0, first, second)
    theirs = swap(jnp.where(c == 0, second, first).astype(BF)).astype(F32)
    small_total = mine[:, 3 * width :] + theirs[:, 3 * width :]

    def both_halves(at):
        low = jnp.where(c == 0, mine, theirs)[:, at * width : (at + 1) * width]
        high = jnp.where(c == 0, theirs, mine)[:, at * width : (at + 1) * width]
        return jnp.stack(
            [low.reshape(shard_rows, ys, chunk), high.reshape(shard_rows, ys, chunk)], axis=2
        ).reshape(shard_rows, D)

    def expert_total(parts):
        grad = jnp.stack(parts).astype(BF)
        depth = grad.shape[1] // (2 * ys)

        def part(key):
            at = jnp.mod(y - key[0], ys) * 2 + jnp.mod(c - key[1], 2)
            return lax.dynamic_slice_in_dim(grad, at * depth, depth, 1)

        return reduce_blocks(part, ("y", "c")).astype(F32)

    shape = (batches, 1, rows, D)
    return (
        layer_out.reshape(shape),
        tokens_grad.reshape(shape),
        small_total[:, 0],
        both_halves(0),
        both_halves(1),
        both_halves(2),
        output_weight_grad,
        small_total[:head_shard, 2 + experts],
        small_total[:head_shard, 3 + experts],
        small_total[:, 1],
        small_total[:, 2 : 2 + experts],
        expert_total(gate_grads),
        expert_total(up_grads),
        expert_total(down_grads),
    )


def solution(mesh):
    dp, expert = mesh.shape["dp"], mesh.shape["expert"]
    zs = math.gcd(expert, 4)
    grid = Mesh(
        mesh.devices.reshape(dp // 2, 2, zs, expert // zs),
        ("y", "c", "z", "x"),
    )
    every, dps, exps = ("y", "c", "z", "x"), ("y", "c"), ("z", "x")
    in_specs = (
        P(None, every, None, None),
        P(None, every, None, None),
        P(None, every),
        P(None, every, None, None),
        P(None, every, None),
        P(every),
        P(every, None),
        P(every, None),
        P(every, None),
        P(every, None),
        P(every),
        P(every),
        P(every),
        P(every, None),
        P(exps, dps, None),
        P(exps, dps, None),
        P(exps, dps, None),
    )
    out_specs = (
        P(None, every, None, None),
        P(None, every, None, None),
        P(every),
        P(every, None),
        P(every, None),
        P(every, None),
        P(every, None),
        P(every),
        P(every),
        P(every),
        P(every, None),
        P(exps, dps, None),
        P(exps, dps, None),
        P(exps, dps, None),
    )
    return jax.shard_map(shards, mesh=grid, in_specs=in_specs, out_specs=out_specs, check_vma=False)
```

```python
import functools
import math

import jax
import jax.numpy as jnp
from jax import lax
from jax.experimental import pallas as pl
from jax.experimental.pallas import tpu as pltpu
from jax.sharding import Mesh
from jax.sharding import PartitionSpec as P

D = 2048
HEADS = 16
HD = 128
TOP = 8
EXTRA = 128

EPSILON = 1e-06
THETA = 50000.0
NEGATIVE = -1e30
BF = jnp.bfloat16
F32 = jnp.float32


def plain(left, right):
    return jnp.dot(left, right, preferred_element_type=F32)


def inner(left, right):
    return lax.dot_general(left, right, (((0,), (0,)), ((), ())), preferred_element_type=F32)


def times_t(left, right):
    return lax.dot_general(left, right, (((1,), (1,)), ((), ())), preferred_element_type=F32)


def tied(values, others):
    return lax.optimization_barrier((values, others))[0]


def ring_place(axis, at):
    return at ^ (at >> 1) if axis == "z" and lax.axis_size(axis) == 4 else at


def shift(value, axis, step):
    size = lax.axis_size(axis)
    pairs = [(ring_place(axis, i), ring_place(axis, (i + step) % size)) for i in range(size)]
    return lax.ppermute(value, axis, pairs)


def came_from(axis, k):
    at = ring_place(axis, lax.axis_index(axis))
    return ring_place(axis, jnp.mod(at - k, lax.axis_size(axis)))


def gather_blocks(block, order):
    held = {(): block}
    for axis in order:
        grown = {}
        for key, value in held.items():
            for k in range(lax.axis_size(axis)):
                if k:
                    value = shift(value, axis, 1)
                grown[key + (k,)] = value
        held = grown
    return held


def reduce_blocks(part, order):
    def reduce_from(key, depth):
        if depth == len(order):
            return part(key)
        axis = order[depth]
        size = lax.axis_size(axis)
        total = reduce_from(key + (1,), depth + 1)
        for k in [*range(2, size), 0]:
            arrived = shift(total.astype(BF), axis, 1)
            total = reduce_from(key + (k,), depth + 1).astype(F32) + arrived.astype(F32)
        return total

    return reduce_from((), 0)


def gather_pieces(block, order, merges):
    held = [(block, [()])]
    for depth, axis in enumerate(order):
        grown, level = [], held
        for k in range(lax.axis_size(axis)):
            if k:
                level = [(shift(value, axis, 1), keys) for value, keys in level]
            grown += [(value, [key + (k,) for key in keys]) for value, keys in level]
        if depth < len(merges):
            size = max(1, len(grown) // merges[depth])
            grown = [grown[i : i + size] for i in range(0, len(grown), size)]
            grown = [
                (
                    jnp.concatenate([value for value, _ in some], axis=0),
                    [key for _, keys in some for key in keys],
                )
                for some in grown
            ]
        held = grown
    return held


def reduce_axis(value, axis, dim):
    def part(k):
        return lax.dynamic_index_in_dim(value, came_from(axis, k), dim, keepdims=False)

    total = part(1)
    for k in [*range(2, lax.axis_size(axis)), 0]:
        arrived = shift(total.astype(BF), axis, 1)
        total = part(k).astype(F32) + arrived.astype(F32)
    return total


def place_kernel(plan, rows, offsets_ref, *refs):
    blocks, out, sems = refs[:-2], refs[-2], refs[-1]
    copies = []
    for i, (array, sub, column, width) in enumerate(plan):
        start = pl.multiple_of(offsets_ref[i], 16)
        copies.append(
            pltpu.make_async_copy(
                blocks[array].at[sub * rows : (sub + 1) * rows],
                out.at[pl.ds(start, rows), column : column + width],
                sems.at[i],
            )
        )
    for copy in copies:
        copy.start()
    for copy in copies:
        copy.wait()


def place(pieces, rows, shape):
    plan, offsets = [], []
    for array, (value, starts, column) in enumerate(pieces):
        for sub, start in enumerate(starts):
            plan.append((array, sub, column, value.shape[1]))
            offsets.append(start)
    return pl.pallas_call(
        functools.partial(place_kernel, plan, rows),
        out_shape=jax.ShapeDtypeStruct(shape, BF),
        grid_spec=pltpu.PrefetchScalarGridSpec(
            num_scalar_prefetch=1,
            in_specs=[pl.BlockSpec(memory_space=pl.ANY)] * len(pieces),
            out_specs=pl.BlockSpec(memory_space=pltpu.VMEM),
            scratch_shapes=[pltpu.SemaphoreType.DMA((len(plan),))],
        ),
        compiler_params=pltpu.CompilerParams(vmem_limit_bytes=24 << 20),
    )(jnp.stack(offsets).astype(jnp.int32), *[value for value, _, _ in pieces])


def rope_tables(row_count):
    half = HD // 2
    frequency = THETA ** (-jnp.arange(half, dtype=F32) / half)
    angles = jnp.arange(row_count, dtype=F32)[:, None] * frequency[None, :]
    cosine, sine = jnp.cos(angles), jnp.sin(angles)
    return jnp.concatenate([cosine, cosine], axis=1), jnp.concatenate([-sine, sine], axis=1)


def head_forward(raw, gain, cosine, sine):
    scale = lax.rsqrt(jnp.mean(raw * raw, axis=-1, keepdims=True) + EPSILON)
    unit = raw * scale
    value = unit * gain
    turned = value * cosine + pltpu.roll(value, HD // 2, 1) * sine
    return unit, scale, turned.astype(BF)


def head_backward(grad, unit, scale, gain, cosine, sine):
    grad = grad * cosine - pltpu.roll(grad, HD // 2, 1) * sine
    gain_grad = jnp.sum(grad * unit, axis=0, keepdims=True)
    grad = grad * gain
    grad = scale * (grad - unit * jnp.mean(grad * unit, axis=-1, keepdims=True))
    return grad.astype(BF), gain_grad


def attention_of(query, key, length):
    scores = times_t(query, key) * (1.0 / math.sqrt(HD))
    valid = lax.broadcasted_iota(jnp.int32, scores.shape, 1) < length
    scores = jnp.where(valid, scores, NEGATIVE)
    weight = jnp.exp(scores - jnp.max(scores, axis=-1, keepdims=True))
    return weight / jnp.sum(weight, axis=-1, keepdims=True)


def attend_kernel(heads, lengths_ref, qkv_ref, gains_ref, cosine_ref, sine_ref, mixed_ref):
    length = lengths_ref[pl.program_id(0)]
    cosine, sine = cosine_ref[...], sine_ref[...]
    query_gain, key_gain = gains_ref[0:1, :], gains_ref[1:2, :]
    width = heads * HD
    for h in range(heads):
        lo = h * HD
        query = head_forward(qkv_ref[:, lo : lo + HD], query_gain, cosine, sine)[2]
        key = head_forward(qkv_ref[:, width + lo : width + lo + HD], key_gain, cosine, sine)[2]
        value = qkv_ref[:, 2 * width + lo : 2 * width + lo + HD].astype(BF)
        attention = attention_of(query, key, length)
        mixed_ref[:, lo : lo + HD] = plain(attention.astype(BF), value).astype(BF)


def attend_back_kernel(
    heads, lengths_ref, qkv_ref, mixed_grad_ref, gains_ref, cosine_ref, sine_ref, out_ref, gain_ref
):
    @pl.when(pl.program_id(0) == 0)
    def _():
        gain_ref[...] = jnp.zeros_like(gain_ref)

    length = lengths_ref[pl.program_id(0)]
    cosine, sine = cosine_ref[...], sine_ref[...]
    query_gain, key_gain = gains_ref[0:1, :], gains_ref[1:2, :]
    width = heads * HD
    score_scale = 1.0 / math.sqrt(HD)
    for h in range(heads):
        lo = h * HD
        query_unit, query_scale, query = head_forward(
            qkv_ref[:, lo : lo + HD], query_gain, cosine, sine
        )
        key_unit, key_scale, key = head_forward(
            qkv_ref[:, width + lo : width + lo + HD], key_gain, cosine, sine
        )
        value = qkv_ref[:, 2 * width + lo : 2 * width + lo + HD].astype(BF)
        attention = attention_of(query, key, length)
        mixed_grad = mixed_grad_ref[:, lo : lo + HD]
        value_grad = inner(attention.astype(BF), mixed_grad)
        attention_grad = times_t(mixed_grad, value)
        score_grad = attention * (
            attention_grad - jnp.sum(attention * attention_grad, axis=-1, keepdims=True)
        )
        score_grad = score_grad.astype(BF)
        query_grad, query_gain_grad = head_backward(
            plain(score_grad, key) * score_scale, query_unit, query_scale, query_gain, cosine, sine
        )
        key_grad, key_gain_grad = head_backward(
            inner(score_grad, query) * score_scale, key_unit, key_scale, key_gain, cosine, sine
        )
        out_ref[:, lo : lo + HD] = query_grad
        out_ref[:, width + lo : width + lo + HD] = key_grad
        out_ref[:, 2 * width + lo : 2 * width + lo + HD] = value_grad.astype(BF)
        gain_ref[0:1, :] += query_gain_grad
        gain_ref[1:2, :] += key_gain_grad


def attend(qkv, lengths, gains, cosine, sine, rows, heads):
    sequences = qkv.shape[0] // rows
    width = heads * HD
    whole = pl.BlockSpec((2, HD), lambda s, n: (0, 0))
    table = pl.BlockSpec((rows, HD), lambda s, n: (0, 0))
    return pl.pallas_call(
        functools.partial(attend_kernel, heads),
        out_shape=jax.ShapeDtypeStruct((qkv.shape[0], width), BF),
        grid_spec=pltpu.PrefetchScalarGridSpec(
            num_scalar_prefetch=1,
            grid=(sequences,),
            in_specs=[
                pl.BlockSpec((rows, 3 * width), lambda s, n: (s, 0)),
                whole,
                table,
                table,
            ],
            out_specs=pl.BlockSpec((rows, width), lambda s, n: (s, 0)),
        ),
        compiler_params=pltpu.CompilerParams(vmem_limit_bytes=32 << 20),
        cost_estimate=pl.CostEstimate(flops=14 * 10**9, bytes_accessed=14 << 20, transcendentals=0),
    )(lengths, qkv, gains, cosine, sine)


def attend_back(qkv, mixed_grad, lengths, gains, cosine, sine, rows, heads):
    sequences = qkv.shape[0] // rows
    width = heads * HD
    whole = pl.BlockSpec((2, HD), lambda s, n: (0, 0))
    table = pl.BlockSpec((rows, HD), lambda s, n: (0, 0))
    return pl.pallas_call(
        functools.partial(attend_back_kernel, heads),
        out_shape=(
            jax.ShapeDtypeStruct((qkv.shape[0], 3 * width), BF),
            jax.ShapeDtypeStruct((2, HD), F32),
        ),
        grid_spec=pltpu.PrefetchScalarGridSpec(
            num_scalar_prefetch=1,
            grid=(sequences,),
            in_specs=[
                pl.BlockSpec((rows, 3 * width), lambda s, n: (s, 0)),
                pl.BlockSpec((rows, width), lambda s, n: (s, 0)),
                whole,
                table,
                table,
            ],
            out_specs=(
                pl.BlockSpec((rows, 3 * width), lambda s, n: (s, 0)),
                whole,
            ),
        ),
        compiler_params=pltpu.CompilerParams(vmem_limit_bytes=32 << 20),
        cost_estimate=pl.CostEstimate(flops=20 * 10**9, bytes_accessed=20 << 20, transcendentals=0),
    )(lengths, qkv, mixed_grad, gains, cosine, sine)


TILE = 256


def experts_kernel(sizes, places_ref, *refs):
    part, groups, rows, experts, slots, local, ff = sizes
    take = iter(refs)
    row_refs = [next(take) for _ in range(groups)]
    cots_ref = next(take)
    weight_refs = [next(take) for _ in range(3)]
    if part:
        for _ in range(5):
            next(take)
    combined_refs = [next(take) for _ in range(groups)]
    back_refs = [next(take) for _ in range(groups)]
    kept_refs = [next(take) for _ in range(5)]
    (rows_v, cots_v, gate_v, up_v, down_v, sent_v, grad_v, active_v, gate_grad_v, up_grad_v) = (
        next(take) for _ in range(10)
    )
    (cot_slots_v, returned_v, sent_grad_v, rank_v, prob_v, onehot_v, gated_v, sum_v) = (
        next(take) for _ in range(8)
    )
    in_sems, weight_sems, out_sems = (next(take) for _ in range(3))
    own = row_refs[0].shape[0]
    batches = own // rows
    sequences = groups * batches
    count = sequences * slots
    first = places_ref[0]

    loads = []
    for i in range(groups):
        loads.append(pltpu.make_async_copy(row_refs[i], rows_v.at[i], in_sems.at[2 * i]))
        start = pl.multiple_of(places_ref[1 + i], 16)
        loads.append(
            pltpu.make_async_copy(
                cots_ref.at[pl.ds(start, own)], cots_v.at[i], in_sems.at[2 * i + 1]
            )
        )
    for copy in loads:
        copy.start()
    weight_loads = [[] for _ in range(local)]
    for j in range(local):
        for w, target in enumerate((gate_v, up_v, down_v)):
            copy = pltpu.make_async_copy(
                weight_refs[w].at[j], target.at[j], weight_sems.at[j * 3 + w]
            )
            copy.start()
            weight_loads[j].append(copy)
    for copy in loads:
        copy.wait()

    slot = lax.broadcasted_iota(jnp.int32, (slots, rows), 0).astype(F32)
    for q in range(sequences):
        i, lo = q // batches, (q % batches) * rows
        rank_v[q] = cots_v[i, lo : lo + rows, D:].astype(F32).T
        prob_v[q] = rows_v[i, lo : lo + rows, D:].astype(F32).T
        onehots, gates = [], []
        for j in range(local):
            rank = rank_v[q, pl.ds(first + j, 1), :]
            prob = (
                prob_v[q, pl.ds(first + j, 1), :]
                + prob_v[q, pl.ds(experts + first + j, 1), :]
                + prob_v[q, pl.ds(2 * experts + first + j, 1), :]
            )
            chosen = rank == slot
            gated = jnp.where(chosen, prob, 0.0)
            onehot = jnp.where(chosen, 1.0, 0.0).astype(BF)
            onehot_v[q, j * slots : (j + 1) * slots, :] = onehot
            gated_v[q, j * slots : (j + 1) * slots, :] = gated.astype(BF)
            gates.append(jnp.sum(gated, axis=1, keepdims=True))
        gate_slots = jnp.concatenate(gates, axis=0)
        onehots = onehot_v[q]

        @pl.loop(0, D // TILE)
        def _(n):
            at = pl.ds(pl.multiple_of(n * TILE, TILE), TILE)
            sent = plain(onehots, rows_v[i, lo : lo + rows, at]).astype(BF)
            cots = plain(onehots, cots_v[i, lo : lo + rows, at])
            grads = (cots * gate_slots).astype(BF)
            cots = cots.astype(BF)
            for j in range(local):
                window = slice(j * slots, (j + 1) * slots)
                place = slice(q * slots, (q + 1) * slots)
                sent_v[j, place, at] = sent[window]
                cot_slots_v[j, place, at] = cots[window]
                grad_v[j, place, at] = grads[window]

    stores = []

    def store(index, source, j):
        target = kept_refs[index].at[j, pl.ds(part * count, count)]
        copy = pltpu.make_async_copy(source.at[j], target, out_sems.at[index * local + j])
        copy.start()
        stores.append(copy)

    for j in range(local):
        store(0, sent_v, j)
        store(1, grad_v, j)
    for j in range(local):
        for copy in weight_loads[j]:
            copy.wait()

        @pl.loop(0, ff // TILE)
        def _(n):
            at = pl.ds(pl.multiple_of(n * TILE, TILE), TILE)
            gate_hidden = plain(sent_v[j], gate_v[j, :, at])
            up_hidden = plain(sent_v[j], up_v[j, :, at])
            active_grad = times_t(grad_v[j], down_v[j, at, :])
            sigmoid = jax.nn.sigmoid(gate_hidden)
            silu = gate_hidden * sigmoid
            active_v[j, :, at] = (silu * up_hidden).astype(BF)
            gate_grad_v[j, :, at] = (
                active_grad * up_hidden * sigmoid * (1.0 + gate_hidden * (1.0 - sigmoid))
            ).astype(BF)
            up_grad_v[j, :, at] = (active_grad * silu).astype(BF)

        store(2, active_v, j)
        store(3, gate_grad_v, j)
        store(4, up_grad_v, j)
        sum_v[j] = jnp.zeros_like(sum_v[j])

        @pl.loop(0, D // TILE)
        def _(n):
            at = pl.ds(pl.multiple_of(n * TILE, TILE), TILE)
            returned = plain(active_v[j], down_v[j, :, at]).astype(BF)
            returned_v[j, :, at] = returned
            product = cot_slots_v[j, :, at].astype(F32) * returned.astype(F32)
            folded = product[:, :128]
            for m in range(1, TILE // 128):
                folded = folded + product[:, m * 128 : (m + 1) * 128]
            sum_v[j] += folded
            sent_grad = times_t(gate_grad_v[j], gate_v[j, at, :])
            sent_grad = sent_grad + times_t(up_grad_v[j], up_v[j, at, :])
            sent_grad_v[j, :, at] = sent_grad.astype(BF)

    column = lax.broadcasted_iota(jnp.int32, (EXTRA, rows), 0)
    for q in range(sequences):
        i, lo = q // batches, (q % batches) * rows
        place = slice(q * slots, (q + 1) * slots)
        table = jnp.zeros((EXTRA, rows), F32)
        for j in range(local):
            gates_grad = jnp.sum(sum_v[j, place, :], axis=1, keepdims=True)
            onehot = onehot_v[q, j * slots : (j + 1) * slots, :].astype(F32)
            value = jnp.sum(onehot * gates_grad, axis=0, keepdims=True)
            for m in range(3):
                high = value.astype(BF).astype(F32)
                table = table + jnp.where(column == m * experts + first + j, high, 0.0)
                value = value - high
        back_refs[i][lo : lo + rows, D:] = table.T.astype(BF)
        onehots, gates = onehot_v[q], gated_v[q]

        @pl.loop(0, D // TILE)
        def _(n):
            at = pl.ds(pl.multiple_of(n * TILE, TILE), TILE)
            returned = jnp.concatenate([returned_v[j, place, at] for j in range(local)], axis=0)
            sent_grad = jnp.concatenate([sent_grad_v[j, place, at] for j in range(local)], axis=0)
            combined_refs[i][lo : lo + rows, at] = inner(gates, returned).astype(BF)
            back_refs[i][lo : lo + rows, at] = inner(onehots, sent_grad).astype(BF)

    for copy in stores:
        copy.wait()


def run_experts(
    places, row_blocks, cots, weights, kept, part, parts, experts, rows, capacity
):
    groups = len(row_blocks)
    own = row_blocks[0].shape[0]
    sequences = groups * (own // rows)
    slots = (capacity + 15) // 16 * 16
    count = sequences * slots
    local, _, ff = weights[0].shape
    any_space = pl.BlockSpec(memory_space=pl.ANY)
    in_vmem = pl.BlockSpec(memory_space=pltpu.VMEM)
    widths = (D, D, ff, ff, ff)
    operands = [*row_blocks, cots, *weights]
    aliases = {}
    if kept is not None:
        aliases = {1 + len(operands) + i: 2 * groups + i for i in range(5)}
        operands = operands + list(kept)
    scratch = [
        pltpu.VMEM((groups, own, D + EXTRA), BF),
        pltpu.VMEM((groups, own, D + EXTRA), BF),
        *[pltpu.VMEM(w.shape, BF) for w in weights],
        *[pltpu.VMEM((local, count, w), BF) for w in widths],
        pltpu.VMEM((local, count, D), BF),
        pltpu.VMEM((local, count, D), BF),
        pltpu.VMEM((local, count, D), BF),
        pltpu.VMEM((sequences, EXTRA, rows), F32),
        pltpu.VMEM((sequences, EXTRA, rows), F32),
        pltpu.VMEM((sequences, local * slots, rows), BF),
        pltpu.VMEM((sequences, local * slots, rows), BF),
        pltpu.VMEM((local, count, 128), F32),
        pltpu.SemaphoreType.DMA((2 * groups,)),
        pltpu.SemaphoreType.DMA((3 * local,)),
        pltpu.SemaphoreType.DMA((5 * local,)),
    ]
    sizes = (part, groups, rows, experts, slots, local, ff)
    results = pl.pallas_call(
        functools.partial(experts_kernel, sizes),
        out_shape=(
            *[jax.ShapeDtypeStruct((own, D), BF)] * groups,
            *[jax.ShapeDtypeStruct((own, D + EXTRA), BF)] * groups,
            *[jax.ShapeDtypeStruct((local, parts * count, w), BF) for w in widths],
        ),
        grid_spec=pltpu.PrefetchScalarGridSpec(
            num_scalar_prefetch=1,
            in_specs=[any_space] * len(operands),
            out_specs=(*[in_vmem] * (2 * groups), *[any_space] * 5),
            scratch_shapes=scratch,
        ),
        input_output_aliases=aliases,
        compiler_params=pltpu.CompilerParams(vmem_limit_bytes=60 << 20),
        cost_estimate=pl.CostEstimate(
            flops=40 * local * count * D * ff, bytes_accessed=40 << 20, transcendentals=0
        ),
    )(places, *operands)
    return results[:groups], results[groups : 2 * groups], results[2 * groups :]


def norm_back(grad, unit, scale, gain):
    scaled = grad * gain
    values_grad = scale * (scaled - unit * jnp.mean(scaled * unit, axis=-1, keepdims=True))
    return values_grad, jnp.sum(grad * unit, axis=0)


def slot_ranks(route, priority, experts, capacity):
    rows = route.shape[0]
    expert = jnp.arange(experts, dtype=jnp.int32)
    chosen = route[:, :, None] == expert[None, None, :]
    order = jnp.sum(jnp.where(chosen, priority.reshape(rows, TOP)[:, :, None], 0), axis=1)
    routed = jnp.any(chosen, axis=1)
    order = jnp.where(routed, order, rows * TOP).T
    rank = jnp.sum((order[:, None, :] < order[:, :, None]).astype(jnp.int32), axis=2).T
    return jnp.where(routed & (rank < capacity), rank, -1)


def in_three(value):
    high = value.astype(BF)
    rest = value - high.astype(F32)
    middle = rest.astype(BF)
    low = (rest - middle.astype(F32)).astype(BF)
    return jnp.concatenate([high, middle, low], axis=-1)


def from_three(columns, count):
    return (
        columns[..., :count].astype(F32)
        + columns[..., count : 2 * count].astype(F32)
        + columns[..., 2 * count : 3 * count].astype(F32)
    )


def widen(columns, width):
    return jnp.pad(columns, ((0, 0), (0, width - columns.shape[-1])))


def shards(
    tokens,
    out_cotangent,
    lengths,
    routes,
    priority,
    attn_gain,
    query_weight,
    key_weight,
    value_weight,
    output_weight,
    query_gain,
    key_gain,
    ffn_gain,
    router_weight,
    gate_weight,
    up_weight,
    down_weight,
):
    batches, rows = tokens.shape[0], tokens.shape[2]
    own = batches * rows
    experts = router_weight.shape[1]
    capacity = 5 * rows * TOP // (4 * experts)
    local = gate_weight.shape[0]
    ys, zs, xs = lax.axis_size("y"), lax.axis_size("z"), lax.axis_size("x")
    y, c, z, x = (lax.axis_index(name) for name in ("y", "c", "z", "x"))
    shard_rows = query_weight.shape[0]
    head_shard = query_gain.shape[0]
    heads = HEADS // (2 * xs)
    width = heads * HD
    half_width = D // 2
    chunk = D // (2 * ys)

    def swap(value):
        return lax.ppermute(value, "c", [(0, 1), (1, 0)])

    def sent_along(axis, piece_for):
        at, size = lax.axis_index(axis), lax.axis_size(axis)
        return [
            shift(piece_for(jnp.mod(at + k, size)), axis, k) if k else piece_for(at)
            for k in range(size)
        ]

    token_rows = tokens.reshape(own, D)
    length = lengths.reshape(batches)
    group_keys = [(kx, kc) for kx in range(xs) for kc in range(2)]
    held = gather_blocks(token_rows, ("x", "c"))
    group_tokens = jnp.concatenate([held[key] for key in group_keys], axis=0)
    held = gather_blocks(length, ("x", "c"))
    group_lengths = jnp.concatenate([held[key] for key in group_keys])
    extra = jnp.concatenate(
        [
            attn_gain[:, None],
            ffn_gain[:, None],
            router_weight,
            jnp.pad(query_gain, (0, shard_rows - head_shard))[:, None],
            jnp.pad(key_gain, (0, shard_rows - head_shard))[:, None],
        ],
        axis=1,
    )
    extra = widen(extra, EXTRA)

    def row_offset(ky, kc, kz, kx):
        sources = (came_from("y", ky), came_from("c", kc), came_from("z", kz), came_from("x", kx))
        return (
            ((sources[0] * 2 + sources[1]) * zs + sources[2]) * xs + sources[3]
        ) * shard_rows

    def half_columns(weight, core):
        return jnp.concatenate(
            [
                lax.dynamic_slice_in_dim(weight, (2 * i + core) * chunk, chunk, 1)
                for i in range(ys)
            ],
            axis=1,
        )

    def packed(core):
        halves = [half_columns(w, core) for w in (query_weight, key_weight, value_weight)]
        return jnp.stack(
            [
                jnp.concatenate(
                    [half[:, i * width : (i + 1) * width] for half in halves] + [extra], axis=1
                )
                for i in range(xs)
            ]
        )

    block = jnp.concatenate(sent_along("c", packed), axis=1)
    block = jnp.concatenate(
        sent_along("x", lambda i: lax.dynamic_index_in_dim(block, i, 0, keepdims=False)), axis=0
    )
    block = jnp.concatenate(list(gather_blocks(block, ("y",)).values()), axis=0)
    out_blocks = gather_blocks(output_weight, ("z",))
    out_rows = jnp.concatenate(list(out_blocks.values()), axis=0)
    block = tied(block, out_rows)
    qkv_pieces, hops = [], []
    for (kz,), value in gather_blocks(block, ("z",)).items():
        starts = [
            row_offset(ky, kc, kz, kx)
            for ky in range(ys)
            for kx in range(xs)
            for kc in range(2)
        ]
        qkv_pieces.append((value, starts, 0))
        hops.append(value)
    qkv_weight = place(qkv_pieces, shard_rows, (D, 3 * width + EXTRA))
    out_rows = jnp.concatenate(list(gather_blocks(out_rows, ("y",)).values()), axis=0)
    out_pieces = []
    for (kx,), value in gather_blocks(out_rows, ("x",)).items():
        starts = [
            ((came_from("y", ky) * zs + came_from("z", kz)) * xs + came_from("x", kx)) * shard_rows
            for ky in range(ys)
            for kz in range(zs)
        ]
        out_pieces.append((value, starts, 0))
    out_weight = place(out_pieces, shard_rows, (half_width, D))
    ZX = ("z", "x")

    weights = [
        lax.all_gather(w, ("y", "c"), axis=1, tiled=True)
        for w in (gate_weight, up_weight, down_weight)
    ]

    ranks = jnp.concatenate(
        [
            slot_ranks(routes[b, 0], priority[b, 0], experts, capacity)
            for b in range(batches)
        ],
        axis=0,
    )
    cotangent = out_cotangent.reshape(own, D)
    cot_rows = jnp.concatenate([cotangent, widen(ranks.astype(BF), EXTRA)], axis=1)
    all_cots = lax.all_gather(tied(cot_rows, hops[1]), ZX, axis=0, tiled=True)

    small = qkv_weight[:, 3 * width :].astype(F32)
    qkv_weight = qkv_weight[:, : 3 * width]
    attn_gain_f = small[:, 0][None, :]
    ffn_gain_f = small[:, 1][None, :]
    router = small[:, 2 : 2 + experts].astype(BF)
    per_device = small.reshape(-1, shard_rows, EXTRA)[:, :head_shard]
    head_gains = jnp.stack(
        [per_device[:, :, 2 + experts].reshape(HD), per_device[:, :, 3 + experts].reshape(HD)]
    )
    tokens_f = group_tokens.astype(F32)
    token_scale = lax.rsqrt(jnp.mean(tokens_f * tokens_f, axis=-1, keepdims=True) + EPSILON)
    normed = (tokens_f * token_scale * attn_gain_f).astype(BF)
    qkv = plain(normed, qkv_weight)
    cosine, sine = rope_tables(rows)
    mixed = attend(qkv, group_lengths, head_gains, cosine, sine, rows, heads)
    chip_rows = 2 * own
    parts = [mixed[:chip_rows]]
    for k in range(1, xs):
        parts.append(shift(mixed[k * chip_rows : (k + 1) * chip_rows], "x", -k))
    mixed = jnp.zeros((chip_rows, half_width), BF)
    for k, part in enumerate(parts):
        place_at = jnp.mod(x + k, xs) * width
        mixed = lax.dynamic_update_slice(mixed, part, (0, place_at))
    partial = plain(mixed, out_weight)
    rows_f = token_rows.astype(F32)
    hidden = rows_f + (partial[:own] + swap(partial[own:]))
    hidden_scale = lax.rsqrt(jnp.mean(hidden * hidden, axis=-1, keepdims=True) + EPSILON)
    hidden_unit = hidden * hidden_scale
    routed_in = (hidden_unit * ffn_gain_f).astype(BF)
    gate_probs = jax.nn.softmax(plain(routed_in, router), axis=-1)

    row_blocks = gather_blocks(
        jnp.concatenate([routed_in, widen(in_three(gate_probs), EXTRA)], axis=1), ZX
    )
    first_expert = (z * xs + x) * local
    kept = None
    per_call = math.gcd(xs, 2)
    steps = [*range(1, zs), 0]
    chains = [[], []]
    arrived = [None, None]
    for n, kz in enumerate(steps):
        parts = [{}, {}]
        for some in range(0, xs, per_call):
            keys = [(kz, kx) for kx in range(some, some + per_call)]
            places = [(came_from("z", kz) * xs + came_from("x", kx)) * own for kz, kx in keys]
            places = [first_expert, *places]
            blocks = [row_blocks[key] for key in keys]
            if n >= 2:
                blocks = tied(blocks, [chain[n - 2] for chain in chains])
                if n >= 3:
                    blocks = tied(blocks, arrived)
            combined_part, back_part, kept = run_experts(
                jnp.stack(places).astype(jnp.int32),
                blocks,
                all_cots,
                weights,
                kept,
                (n * xs + some) // per_call,
                zs * xs // per_call,
                experts,
                rows,
                capacity,
            )
            parts[0].update(zip(keys, back_part, strict=True))
            parts[1].update(zip(keys, combined_part, strict=True))
        for i in range(2):
            if n:
                total = chains[i][n - 1]
                if arrived[i] is not None:
                    total = total + arrived[i].astype(F32)
                arrived[i] = shift(total.astype(BF), "z", 1)
            if kz == 0 and i == 1:
                back = chains[0][n] + arrived[0].astype(F32)
                parts[1] = tied(parts[1], back)
            part = {(kx,): value for (kz, kx), value in parts[i].items()}
            chains[i].append(reduce_blocks(part.get, ("x",)))
    combined = chains[1][-1] + arrived[1].astype(F32)
    layer_out = (hidden + combined).astype(BF)
    sent, returned_grad, active, gate_hidden_grad, up_hidden_grad = kept

    def weight_grads(left, right):
        return [inner(left[j], right[j]) for j in range(local)]

    down_grads = weight_grads(active, returned_grad)
    gate_grads = weight_grads(sent, gate_hidden_grad)
    up_grads = weight_grads(sent, up_hidden_grad)

    probs_grad = from_three(back[:, D:], experts)
    logits_grad = (
        gate_probs * (probs_grad - jnp.sum(gate_probs * probs_grad, axis=-1, keepdims=True))
    ).astype(BF)
    router_grad = inner(routed_in, logits_grad)
    routed_grad = back[:, :D] + times_t(logits_grad, router)
    hidden_add, ffn_gain_grad = norm_back(routed_grad, hidden_unit, hidden_scale, ffn_gain_f)
    hidden_grad = cotangent.astype(F32) + hidden_add
    attn_out_grad = hidden_grad.astype(BF)

    both_grads = jnp.concatenate([attn_out_grad, swap(attn_out_grad)], axis=0)
    mixed_grad = times_t(both_grads, out_weight).astype(BF)
    output_grad = inner(mixed, both_grads).astype(BF)
    mixed_grad = jnp.concatenate(
        sent_along("x", lambda i: lax.dynamic_slice_in_dim(mixed_grad, i * width, width, 1)), axis=0
    )
    qkv_grad, head_gain_grads = attend_back(
        qkv, mixed_grad, group_lengths, head_gains, cosine, sine, rows, heads
    )
    normed_part = times_t(qkv_grad, qkv_weight)
    normed_grad = reduce_blocks(
        lambda key: normed_part[(key[0] * 2 + key[1]) * own :][:own], ("x", "c")
    )
    token_unit = rows_f * token_scale[:own]
    tokens_add, attn_gain_grad = norm_back(normed_grad, token_unit, token_scale[:own], attn_gain_f)
    tokens_grad = hidden_grad + tokens_add

    small_grad = jnp.concatenate(
        [
            attn_gain_grad[:, None],
            ffn_gain_grad[:, None],
            router_grad,
            jnp.pad(
                head_gain_grads.reshape(2, -1, head_shard),
                ((0, 0), (0, 0), (0, shard_rows - head_shard)),
            )
            .reshape(2, D)
            .T,
        ],
        axis=1,
    )
    qkv_weight_grad = jnp.concatenate(
        [inner(normed, qkv_grad).astype(BF), widen(small_grad, EXTRA).astype(BF)], axis=1
    )
    output_grad = output_grad.reshape(ys, zs, xs, shard_rows, D)
    output_weight_grad = reduce_axis(output_grad, "x", 2).astype(BF)
    output_weight_grad = reduce_axis(output_weight_grad, "y", 0).astype(BF)
    output_weight_grad = reduce_axis(output_weight_grad, "z", 0)
    total = qkv_weight_grad.reshape(ys, 2, zs, xs, shard_rows, -1)
    total = reduce_axis(total, "z", 2).astype(BF)
    total = reduce_axis(total, "y", 0).astype(BF)
    columns = sent_along("x", lambda i: lax.dynamic_index_in_dim(total, i, 1, keepdims=False))
    columns = jnp.stack(columns)
    columns = sent_along("c", lambda i: lax.dynamic_index_in_dim(columns, i, 1, keepdims=False))
    small_total = sum(jnp.sum(some[:, :, 3 * width :].astype(F32), axis=0) for some in columns)

    def all_heads(at):
        halves = []
        for some in columns:
            half = jnp.zeros((shard_rows, half_width), BF)
            for k in range(xs):
                part = some[k][:, at * width : (at + 1) * width]
                half = lax.dynamic_update_slice(half, part, (0, jnp.mod(x - k, xs) * width))
            halves.append(half)
        low = jnp.where(c == 0, halves[0], halves[1]).reshape(shard_rows, ys, chunk)
        high = jnp.where(c == 0, halves[1], halves[0]).reshape(shard_rows, ys, chunk)
        return jnp.stack([low, high], axis=2).reshape(shard_rows, D).astype(F32)

    def expert_total(parts):
        grad = jnp.stack(parts).astype(BF)
        return lax.psum_scatter(grad, ("y", "c"), scatter_dimension=1, tiled=True).astype(F32)

    shape = (batches, 1, rows, D)
    return (
        layer_out.reshape(shape),
        tokens_grad.reshape(shape),
        small_total[:, 0],
        all_heads(0),
        all_heads(1),
        all_heads(2),
        output_weight_grad,
        small_total[:head_shard, 2 + experts],
        small_total[:head_shard, 3 + experts],
        small_total[:, 1],
        small_total[:, 2 : 2 + experts],
        expert_total(gate_grads),
        expert_total(up_grads),
        expert_total(down_grads),
    )


def solution(mesh):
    dp, expert = mesh.shape["dp"], mesh.shape["expert"]
    zs = math.gcd(expert, 4)
    grid = Mesh(
        mesh.devices.reshape(dp // 2, 2, zs, expert // zs),
        ("y", "c", "z", "x"),
    )
    every, dps, exps = ("y", "c", "z", "x"), ("y", "c"), ("z", "x")
    in_specs = (
        P(None, every, None, None),
        P(None, every, None, None),
        P(None, every),
        P(None, every, None, None),
        P(None, every, None),
        P(every),
        P(every, None),
        P(every, None),
        P(every, None),
        P(every, None),
        P(every),
        P(every),
        P(every),
        P(every, None),
        P(exps, dps, None),
        P(exps, dps, None),
        P(exps, dps, None),
    )
    out_specs = (
        P(None, every, None, None),
        P(None, every, None, None),
        P(every),
        P(every, None),
        P(every, None),
        P(every, None),
        P(every, None),
        P(every),
        P(every),
        P(every),
        P(every, None),
        P(exps, dps, None),
        P(exps, dps, None),
        P(exps, dps, None),
    )
    return jax.shard_map(shards, mesh=grid, in_specs=in_specs, out_specs=out_specs, check_vma=False)
```

```python
import functools
import math

import jax
import jax.numpy as jnp
from jax import lax
from jax.experimental import pallas as pl
from jax.experimental.pallas import tpu as pltpu
from jax.sharding import Mesh
from jax.sharding import PartitionSpec as P

D = 2048
HEADS = 16
HD = 128
TOP = 8
EXTRA = 128

EPSILON = 1e-06
THETA = 50000.0
NEGATIVE = -1e30
BF = jnp.bfloat16
F32 = jnp.float32


def plain(left, right):
    return jnp.dot(left, right, preferred_element_type=F32)


def inner(left, right):
    return lax.dot_general(left, right, (((0,), (0,)), ((), ())), preferred_element_type=F32)


def times_t(left, right):
    return lax.dot_general(left, right, (((1,), (1,)), ((), ())), preferred_element_type=F32)


def tied(values, others):
    return lax.optimization_barrier((values, others))[0]


def ring_place(axis, at):
    return at ^ (at >> 1) if axis == "z" and lax.axis_size(axis) == 4 else at


def shift(value, axis, step):
    size = lax.axis_size(axis)
    pairs = [(ring_place(axis, i), ring_place(axis, (i + step) % size)) for i in range(size)]
    return lax.ppermute(value, axis, pairs)


def came_from(axis, k):
    at = ring_place(axis, lax.axis_index(axis))
    return ring_place(axis, jnp.mod(at - k, lax.axis_size(axis)))


def gather_blocks(block, order):
    held = {(): block}
    for axis in order:
        grown = {}
        for key, value in held.items():
            for k in range(lax.axis_size(axis)):
                if k:
                    value = shift(value, axis, 1)
                grown[key + (k,)] = value
        held = grown
    return held


def reduce_blocks(part, order):
    def reduce_from(key, depth):
        if depth == len(order):
            return part(key)
        axis = order[depth]
        size = lax.axis_size(axis)
        total = reduce_from(key + (1,), depth + 1)
        for k in [*range(2, size), 0]:
            arrived = shift(total.astype(BF), axis, 1)
            total = reduce_from(key + (k,), depth + 1).astype(F32) + arrived.astype(F32)
        return total

    return reduce_from((), 0)


def gather_pieces(block, order, merges):
    held = [(block, [()])]
    for depth, axis in enumerate(order):
        grown, level = [], held
        for k in range(lax.axis_size(axis)):
            if k:
                level = [(shift(value, axis, 1), keys) for value, keys in level]
            grown += [(value, [key + (k,) for key in keys]) for value, keys in level]
        if depth < len(merges):
            size = max(1, len(grown) // merges[depth])
            grown = [grown[i : i + size] for i in range(0, len(grown), size)]
            grown = [
                (
                    jnp.concatenate([value for value, _ in some], axis=0),
                    [key for _, keys in some for key in keys],
                )
                for some in grown
            ]
        held = grown
    return held


def reduce_axis(value, axis, dim):
    def part(k):
        return lax.dynamic_index_in_dim(value, came_from(axis, k), dim, keepdims=False)

    total = part(1)
    for k in [*range(2, lax.axis_size(axis)), 0]:
        arrived = shift(total.astype(BF), axis, 1)
        total = part(k).astype(F32) + arrived.astype(F32)
    return total


def place_kernel(plan, rows, offsets_ref, *refs):
    blocks, out, sems = refs[:-2], refs[-2], refs[-1]
    copies = []
    for i, (array, sub, column, width) in enumerate(plan):
        start = pl.multiple_of(offsets_ref[i], 16)
        copies.append(
            pltpu.make_async_copy(
                blocks[array].at[sub * rows : (sub + 1) * rows],
                out.at[pl.ds(start, rows), column : column + width],
                sems.at[i],
            )
        )
    for copy in copies:
        copy.start()
    for copy in copies:
        copy.wait()


def place(pieces, rows, shape):
    plan, offsets = [], []
    for array, (value, starts, column) in enumerate(pieces):
        for sub, start in enumerate(starts):
            plan.append((array, sub, column, value.shape[1]))
            offsets.append(start)
    return pl.pallas_call(
        functools.partial(place_kernel, plan, rows),
        out_shape=jax.ShapeDtypeStruct(shape, BF),
        grid_spec=pltpu.PrefetchScalarGridSpec(
            num_scalar_prefetch=1,
            in_specs=[pl.BlockSpec(memory_space=pl.ANY)] * len(pieces),
            out_specs=pl.BlockSpec(memory_space=pltpu.VMEM),
            scratch_shapes=[pltpu.SemaphoreType.DMA((len(plan),))],
        ),
        compiler_params=pltpu.CompilerParams(vmem_limit_bytes=24 << 20),
    )(jnp.stack(offsets).astype(jnp.int32), *[value for value, _, _ in pieces])


def rope_tables(row_count):
    half = HD // 2
    frequency = THETA ** (-jnp.arange(half, dtype=F32) / half)
    angles = jnp.arange(row_count, dtype=F32)[:, None] * frequency[None, :]
    cosine, sine = jnp.cos(angles), jnp.sin(angles)
    return jnp.concatenate([cosine, cosine], axis=1), jnp.concatenate([-sine, sine], axis=1)


def head_forward(raw, gain, cosine, sine):
    scale = lax.rsqrt(jnp.mean(raw * raw, axis=-1, keepdims=True) + EPSILON)
    unit = raw * scale
    value = unit * gain
    turned = value * cosine + pltpu.roll(value, HD // 2, 1) * sine
    return unit, scale, turned.astype(BF)


def head_backward(grad, unit, scale, gain, cosine, sine):
    grad = grad * cosine - pltpu.roll(grad, HD // 2, 1) * sine
    gain_grad = jnp.sum(grad * unit, axis=0, keepdims=True)
    grad = grad * gain
    grad = scale * (grad - unit * jnp.mean(grad * unit, axis=-1, keepdims=True))
    return grad.astype(BF), gain_grad


def attention_of(query, key, length):
    scores = times_t(query, key) * (1.0 / math.sqrt(HD))
    valid = lax.broadcasted_iota(jnp.int32, scores.shape, 1) < length
    scores = jnp.where(valid, scores, NEGATIVE)
    weight = jnp.exp(scores - jnp.max(scores, axis=-1, keepdims=True))
    return weight / jnp.sum(weight, axis=-1, keepdims=True)


def attend_kernel(heads, lengths_ref, qkv_ref, gains_ref, cosine_ref, sine_ref, mixed_ref):
    length = lengths_ref[pl.program_id(0)]
    cosine, sine = cosine_ref[...], sine_ref[...]
    query_gain, key_gain = gains_ref[0:1, :], gains_ref[1:2, :]
    width = heads * HD
    for h in range(heads):
        lo = h * HD
        query = head_forward(qkv_ref[:, lo : lo + HD], query_gain, cosine, sine)[2]
        key = head_forward(qkv_ref[:, width + lo : width + lo + HD], key_gain, cosine, sine)[2]
        value = qkv_ref[:, 2 * width + lo : 2 * width + lo + HD].astype(BF)
        attention = attention_of(query, key, length)
        mixed_ref[:, lo : lo + HD] = plain(attention.astype(BF), value).astype(BF)


def attend_back_kernel(
    heads, lengths_ref, qkv_ref, mixed_grad_ref, gains_ref, cosine_ref, sine_ref, out_ref, gain_ref
):
    @pl.when(pl.program_id(0) == 0)
    def _():
        gain_ref[...] = jnp.zeros_like(gain_ref)

    length = lengths_ref[pl.program_id(0)]
    cosine, sine = cosine_ref[...], sine_ref[...]
    query_gain, key_gain = gains_ref[0:1, :], gains_ref[1:2, :]
    width = heads * HD
    score_scale = 1.0 / math.sqrt(HD)
    for h in range(heads):
        lo = h * HD
        query_unit, query_scale, query = head_forward(
            qkv_ref[:, lo : lo + HD], query_gain, cosine, sine
        )
        key_unit, key_scale, key = head_forward(
            qkv_ref[:, width + lo : width + lo + HD], key_gain, cosine, sine
        )
        value = qkv_ref[:, 2 * width + lo : 2 * width + lo + HD].astype(BF)
        attention = attention_of(query, key, length)
        mixed_grad = mixed_grad_ref[:, lo : lo + HD]
        value_grad = inner(attention.astype(BF), mixed_grad)
        attention_grad = times_t(mixed_grad, value)
        score_grad = attention * (
            attention_grad - jnp.sum(attention * attention_grad, axis=-1, keepdims=True)
        )
        score_grad = score_grad.astype(BF)
        query_grad, query_gain_grad = head_backward(
            plain(score_grad, key) * score_scale, query_unit, query_scale, query_gain, cosine, sine
        )
        key_grad, key_gain_grad = head_backward(
            inner(score_grad, query) * score_scale, key_unit, key_scale, key_gain, cosine, sine
        )
        out_ref[:, lo : lo + HD] = query_grad
        out_ref[:, width + lo : width + lo + HD] = key_grad
        out_ref[:, 2 * width + lo : 2 * width + lo + HD] = value_grad.astype(BF)
        gain_ref[0:1, :] += query_gain_grad
        gain_ref[1:2, :] += key_gain_grad


def attend(qkv, lengths, gains, cosine, sine, rows, heads):
    sequences = qkv.shape[0] // rows
    width = heads * HD
    whole = pl.BlockSpec((2, HD), lambda s, n: (0, 0))
    table = pl.BlockSpec((rows, HD), lambda s, n: (0, 0))
    return pl.pallas_call(
        functools.partial(attend_kernel, heads),
        out_shape=jax.ShapeDtypeStruct((qkv.shape[0], width), BF),
        grid_spec=pltpu.PrefetchScalarGridSpec(
            num_scalar_prefetch=1,
            grid=(sequences,),
            in_specs=[
                pl.BlockSpec((rows, 3 * width), lambda s, n: (s, 0)),
                whole,
                table,
                table,
            ],
            out_specs=pl.BlockSpec((rows, width), lambda s, n: (s, 0)),
        ),
        compiler_params=pltpu.CompilerParams(vmem_limit_bytes=32 << 20),
        cost_estimate=pl.CostEstimate(flops=14 * 10**9, bytes_accessed=14 << 20, transcendentals=0),
    )(lengths, qkv, gains, cosine, sine)


def attend_back(qkv, mixed_grad, lengths, gains, cosine, sine, rows, heads):
    sequences = qkv.shape[0] // rows
    width = heads * HD
    whole = pl.BlockSpec((2, HD), lambda s, n: (0, 0))
    table = pl.BlockSpec((rows, HD), lambda s, n: (0, 0))
    return pl.pallas_call(
        functools.partial(attend_back_kernel, heads),
        out_shape=(
            jax.ShapeDtypeStruct((qkv.shape[0], 3 * width), BF),
            jax.ShapeDtypeStruct((2, HD), F32),
        ),
        grid_spec=pltpu.PrefetchScalarGridSpec(
            num_scalar_prefetch=1,
            grid=(sequences,),
            in_specs=[
                pl.BlockSpec((rows, 3 * width), lambda s, n: (s, 0)),
                pl.BlockSpec((rows, width), lambda s, n: (s, 0)),
                whole,
                table,
                table,
            ],
            out_specs=(
                pl.BlockSpec((rows, 3 * width), lambda s, n: (s, 0)),
                whole,
            ),
        ),
        compiler_params=pltpu.CompilerParams(vmem_limit_bytes=32 << 20),
        cost_estimate=pl.CostEstimate(flops=20 * 10**9, bytes_accessed=20 << 20, transcendentals=0),
    )(lengths, qkv, mixed_grad, gains, cosine, sine)


TILE = 256


def experts_kernel(sizes, places_ref, *refs):
    part, groups, rows, experts, slots, local, ff = sizes
    take = iter(refs)
    row_refs = [next(take) for _ in range(groups)]
    cot_refs = [next(take) for _ in range(groups)]
    weight_refs = [next(take) for _ in range(3)]
    if part:
        for _ in range(5):
            next(take)
    combined_refs = [next(take) for _ in range(groups)]
    back_refs = [next(take) for _ in range(groups)]
    kept_refs = [next(take) for _ in range(5)]
    (rows_v, cots_v, gate_v, up_v, down_v, sent_v, grad_v, active_v, gate_grad_v, up_grad_v) = (
        next(take) for _ in range(10)
    )
    (cot_slots_v, returned_v, sent_grad_v, rank_v, prob_v, onehot_v, gated_v, sum_v) = (
        next(take) for _ in range(8)
    )
    in_sems, weight_sems, out_sems = (next(take) for _ in range(3))
    own = row_refs[0].shape[0]
    batches = own // rows
    sequences = groups * batches
    count = sequences * slots
    first = places_ref[0]

    loads = []
    for i in range(groups):
        loads.append(pltpu.make_async_copy(row_refs[i], rows_v.at[i], in_sems.at[2 * i]))
        loads.append(pltpu.make_async_copy(cot_refs[i], cots_v.at[i], in_sems.at[2 * i + 1]))
    for copy in loads:
        copy.start()
    weight_loads = [[] for _ in range(local)]
    for j in range(local):
        for w, target in enumerate((gate_v, up_v, down_v)):
            copy = pltpu.make_async_copy(
                weight_refs[w].at[j], target.at[j], weight_sems.at[j * 3 + w]
            )
            copy.start()
            weight_loads[j].append(copy)
    for copy in loads:
        copy.wait()

    slot = lax.broadcasted_iota(jnp.int32, (slots, rows), 0).astype(F32)
    for q in range(sequences):
        i, lo = q // batches, (q % batches) * rows
        rank_v[q] = cots_v[i, lo : lo + rows, D:].astype(F32).T
        prob_v[q] = rows_v[i, lo : lo + rows, D:].astype(F32).T
        onehots, gates = [], []
        for j in range(local):
            rank = rank_v[q, pl.ds(first + j, 1), :]
            prob = (
                prob_v[q, pl.ds(first + j, 1), :]
                + prob_v[q, pl.ds(experts + first + j, 1), :]
                + prob_v[q, pl.ds(2 * experts + first + j, 1), :]
            )
            chosen = rank == slot
            gated = jnp.where(chosen, prob, 0.0)
            onehot = jnp.where(chosen, 1.0, 0.0).astype(BF)
            onehot_v[q, j * slots : (j + 1) * slots, :] = onehot
            gated_v[q, j * slots : (j + 1) * slots, :] = gated.astype(BF)
            gates.append(jnp.sum(gated, axis=1, keepdims=True))
        gate_slots = jnp.concatenate(gates, axis=0)
        onehots = onehot_v[q]

        @pl.loop(0, D // TILE)
        def _(n):
            at = pl.ds(pl.multiple_of(n * TILE, TILE), TILE)
            sent = plain(onehots, rows_v[i, lo : lo + rows, at]).astype(BF)
            cots = plain(onehots, cots_v[i, lo : lo + rows, at])
            grads = (cots * gate_slots).astype(BF)
            cots = cots.astype(BF)
            for j in range(local):
                window = slice(j * slots, (j + 1) * slots)
                place = slice(q * slots, (q + 1) * slots)
                sent_v[j, place, at] = sent[window]
                cot_slots_v[j, place, at] = cots[window]
                grad_v[j, place, at] = grads[window]

    stores = []

    def store(index, source, j):
        target = kept_refs[index].at[j, pl.ds(part * count, count)]
        copy = pltpu.make_async_copy(source.at[j], target, out_sems.at[index * local + j])
        copy.start()
        stores.append(copy)

    for j in range(local):
        store(0, sent_v, j)
        store(1, grad_v, j)
    for j in range(local):
        for copy in weight_loads[j]:
            copy.wait()

        @pl.loop(0, ff // TILE)
        def _(n):
            at = pl.ds(pl.multiple_of(n * TILE, TILE), TILE)
            gate_hidden = plain(sent_v[j], gate_v[j, :, at])
            up_hidden = plain(sent_v[j], up_v[j, :, at])
            active_grad = times_t(grad_v[j], down_v[j, at, :])
            sigmoid = jax.nn.sigmoid(gate_hidden)
            silu = gate_hidden * sigmoid
            active_v[j, :, at] = (silu * up_hidden).astype(BF)
            gate_grad_v[j, :, at] = (
                active_grad * up_hidden * sigmoid * (1.0 + gate_hidden * (1.0 - sigmoid))
            ).astype(BF)
            up_grad_v[j, :, at] = (active_grad * silu).astype(BF)

        store(2, active_v, j)
        store(3, gate_grad_v, j)
        store(4, up_grad_v, j)
        sum_v[j] = jnp.zeros_like(sum_v[j])

        @pl.loop(0, D // TILE)
        def _(n):
            at = pl.ds(pl.multiple_of(n * TILE, TILE), TILE)
            returned = plain(active_v[j], down_v[j, :, at]).astype(BF)
            returned_v[j, :, at] = returned
            product = cot_slots_v[j, :, at].astype(F32) * returned.astype(F32)
            folded = product[:, :128]
            for m in range(1, TILE // 128):
                folded = folded + product[:, m * 128 : (m + 1) * 128]
            sum_v[j] += folded
            sent_grad = times_t(gate_grad_v[j], gate_v[j, at, :])
            sent_grad = sent_grad + times_t(up_grad_v[j], up_v[j, at, :])
            sent_grad_v[j, :, at] = sent_grad.astype(BF)

    column = lax.broadcasted_iota(jnp.int32, (EXTRA, rows), 0)
    for q in range(sequences):
        i, lo = q // batches, (q % batches) * rows
        place = slice(q * slots, (q + 1) * slots)
        table = jnp.zeros((EXTRA, rows), F32)
        for j in range(local):
            gates_grad = jnp.sum(sum_v[j, place, :], axis=1, keepdims=True)
            onehot = onehot_v[q, j * slots : (j + 1) * slots, :].astype(F32)
            value = jnp.sum(onehot * gates_grad, axis=0, keepdims=True)
            for m in range(3):
                high = value.astype(BF).astype(F32)
                table = table + jnp.where(column == m * experts + first + j, high, 0.0)
                value = value - high
        back_refs[i][lo : lo + rows, D:] = table.T.astype(BF)
        onehots, gates = onehot_v[q], gated_v[q]

        @pl.loop(0, D // TILE)
        def _(n):
            at = pl.ds(pl.multiple_of(n * TILE, TILE), TILE)
            returned = jnp.concatenate([returned_v[j, place, at] for j in range(local)], axis=0)
            sent_grad = jnp.concatenate([sent_grad_v[j, place, at] for j in range(local)], axis=0)
            combined_refs[i][lo : lo + rows, at] = inner(gates, returned).astype(BF)
            back_refs[i][lo : lo + rows, at] = inner(onehots, sent_grad).astype(BF)

    for copy in stores:
        copy.wait()


def run_experts(
    places, row_blocks, cot_blocks, weights, kept, part, parts, experts, rows, capacity
):
    groups = len(row_blocks)
    own = row_blocks[0].shape[0]
    sequences = groups * (own // rows)
    slots = (capacity + 15) // 16 * 16
    count = sequences * slots
    local, _, ff = weights[0].shape
    any_space = pl.BlockSpec(memory_space=pl.ANY)
    in_vmem = pl.BlockSpec(memory_space=pltpu.VMEM)
    widths = (D, D, ff, ff, ff)
    operands = [*row_blocks, *cot_blocks, *weights]
    aliases = {}
    if kept is not None:
        aliases = {1 + len(operands) + i: 2 * groups + i for i in range(5)}
        operands = operands + list(kept)
    scratch = [
        pltpu.VMEM((groups, own, D + EXTRA), BF),
        pltpu.VMEM((groups, own, D + EXTRA), BF),
        *[pltpu.VMEM(w.shape, BF) for w in weights],
        *[pltpu.VMEM((local, count, w), BF) for w in widths],
        pltpu.VMEM((local, count, D), BF),
        pltpu.VMEM((local, count, D), BF),
        pltpu.VMEM((local, count, D), BF),
        pltpu.VMEM((sequences, EXTRA, rows), F32),
        pltpu.VMEM((sequences, EXTRA, rows), F32),
        pltpu.VMEM((sequences, local * slots, rows), BF),
        pltpu.VMEM((sequences, local * slots, rows), BF),
        pltpu.VMEM((local, count, 128), F32),
        pltpu.SemaphoreType.DMA((2 * groups,)),
        pltpu.SemaphoreType.DMA((3 * local,)),
        pltpu.SemaphoreType.DMA((5 * local,)),
    ]
    sizes = (part, groups, rows, experts, slots, local, ff)
    results = pl.pallas_call(
        functools.partial(experts_kernel, sizes),
        out_shape=(
            *[jax.ShapeDtypeStruct((own, D), BF)] * groups,
            *[jax.ShapeDtypeStruct((own, D + EXTRA), BF)] * groups,
            *[jax.ShapeDtypeStruct((local, parts * count, w), BF) for w in widths],
        ),
        grid_spec=pltpu.PrefetchScalarGridSpec(
            num_scalar_prefetch=1,
            in_specs=[any_space] * len(operands),
            out_specs=(*[in_vmem] * (2 * groups), *[any_space] * 5),
            scratch_shapes=scratch,
        ),
        input_output_aliases=aliases,
        compiler_params=pltpu.CompilerParams(vmem_limit_bytes=60 << 20),
        cost_estimate=pl.CostEstimate(
            flops=40 * local * count * D * ff, bytes_accessed=40 << 20, transcendentals=0
        ),
    )(places, *operands)
    return results[:groups], results[groups : 2 * groups], results[2 * groups :]


def norm_back(grad, unit, scale, gain):
    scaled = grad * gain
    values_grad = scale * (scaled - unit * jnp.mean(scaled * unit, axis=-1, keepdims=True))
    return values_grad, jnp.sum(grad * unit, axis=0)


def slot_ranks(route, priority, experts, capacity):
    rows = route.shape[0]
    expert = jnp.arange(experts, dtype=jnp.int32)
    chosen = route[:, :, None] == expert[None, None, :]
    order = jnp.sum(jnp.where(chosen, priority.reshape(rows, TOP)[:, :, None], 0), axis=1)
    routed = jnp.any(chosen, axis=1)
    order = jnp.where(routed, order, rows * TOP).T
    rank = jnp.sum((order[:, None, :] < order[:, :, None]).astype(jnp.int32), axis=2).T
    return jnp.where(routed & (rank < capacity), rank, -1)


def in_three(value):
    high = value.astype(BF)
    rest = value - high.astype(F32)
    middle = rest.astype(BF)
    low = (rest - middle.astype(F32)).astype(BF)
    return jnp.concatenate([high, middle, low], axis=-1)


def from_three(columns, count):
    return (
        columns[..., :count].astype(F32)
        + columns[..., count : 2 * count].astype(F32)
        + columns[..., 2 * count : 3 * count].astype(F32)
    )


def widen(columns, width):
    return jnp.pad(columns, ((0, 0), (0, width - columns.shape[-1])))


def shards(
    tokens,
    out_cotangent,
    lengths,
    routes,
    priority,
    attn_gain,
    query_weight,
    key_weight,
    value_weight,
    output_weight,
    query_gain,
    key_gain,
    ffn_gain,
    router_weight,
    gate_weight,
    up_weight,
    down_weight,
):
    batches, rows = tokens.shape[0], tokens.shape[2]
    own = batches * rows
    experts = router_weight.shape[1]
    capacity = 5 * rows * TOP // (4 * experts)
    local = gate_weight.shape[0]
    ys, zs, xs = lax.axis_size("y"), lax.axis_size("z"), lax.axis_size("x")
    y, c, z, x = (lax.axis_index(name) for name in ("y", "c", "z", "x"))
    shard_rows = query_weight.shape[0]
    head_shard = query_gain.shape[0]
    heads = HEADS // (2 * xs)
    width = heads * HD
    half_width = D // 2
    chunk = D // (2 * ys)

    def swap(value):
        return lax.ppermute(value, "c", [(0, 1), (1, 0)])

    def sent_along(axis, piece_for):
        at, size = lax.axis_index(axis), lax.axis_size(axis)
        return [
            shift(piece_for(jnp.mod(at + k, size)), axis, k) if k else piece_for(at)
            for k in range(size)
        ]

    token_rows = tokens.reshape(own, D)
    length = lengths.reshape(batches)
    group_keys = [(kx, kc) for kx in range(xs) for kc in range(2)]
    x_tokens = gather_blocks(token_rows, ("x",))
    held = gather_blocks(length, ("x", "c"))
    group_lengths = jnp.concatenate([held[key] for key in group_keys])
    extra = jnp.concatenate(
        [
            attn_gain[:, None],
            ffn_gain[:, None],
            router_weight,
            jnp.pad(query_gain, (0, shard_rows - head_shard))[:, None],
            jnp.pad(key_gain, (0, shard_rows - head_shard))[:, None],
        ],
        axis=1,
    )
    extra = widen(extra, EXTRA)

    def row_offset(ky, kc, kz, kx):
        sources = (came_from("y", ky), came_from("c", kc), came_from("z", kz), came_from("x", kx))
        return (
            ((sources[0] * 2 + sources[1]) * zs + sources[2]) * xs + sources[3]
        ) * shard_rows

    def half_columns(weight, core):
        return jnp.concatenate(
            [
                lax.dynamic_slice_in_dim(weight, (2 * i + core) * chunk, chunk, 1)
                for i in range(ys)
            ],
            axis=1,
        )

    def packed(core):
        halves = [half_columns(w, core) for w in (query_weight, key_weight, value_weight)]
        return jnp.stack(
            [
                jnp.concatenate(
                    [half[:, i * width : (i + 1) * width] for half in halves] + [extra], axis=1
                )
                for i in range(xs)
            ]
        )

    out_hops = [output_weight]
    for _ in range(1, zs):
        out_hops.append(shift(out_hops[-1], "z", 1))
    block = jnp.concatenate(sent_along("c", packed), axis=1)
    block = jnp.concatenate(
        sent_along("x", lambda i: lax.dynamic_index_in_dim(block, i, 0, keepdims=False)), axis=0
    )
    ZX = ("z", "x")
    ranks = jnp.concatenate(
        [
            slot_ranks(routes[b, 0], priority[b, 0], experts, capacity)
            for b in range(batches)
        ],
        axis=0,
    )
    cotangent = out_cotangent.reshape(own, D)
    cot_rows = jnp.concatenate([cotangent, widen(ranks.astype(BF), EXTRA)], axis=1)
    cot_blocks = {(0, kx): v for (kx,), v in gather_blocks(cot_rows, ("x",)).items()}
    block = tied(block, out_hops[1])
    late = list(gather_blocks(block, ("y",)).values())
    late = jnp.concatenate(late, axis=0)
    weight_shards = tied((gate_weight, up_weight, down_weight), late)
    late = tied(late, out_hops[2:3])

    def offsets_of(kz):
        return [
            row_offset(ky, kc, kz, kx)
            for ky in range(ys)
            for kx in range(xs)
            for kc in range(2)
        ]

    qkv_pieces = []
    hop = late
    for kz in range(zs):
        if kz:
            hop = shift(hop, "z", 1)
            if kz == 1:
                hop, out_hops, x_tokens = lax.optimization_barrier((hop, out_hops, x_tokens))
                out_rows = jnp.concatenate(out_hops, axis=0)
                out_rows = list(gather_blocks(out_rows, ("y",)).values())
            if kz == 2:
                hop, out_rows, cot_blocks = lax.optimization_barrier((hop, out_rows, cot_blocks))
        qkv_pieces.append((hop, offsets_of(kz), 0))
    qkv_weight = place(qkv_pieces, shard_rows, (D, 3 * width + EXTRA))
    out_pieces = []
    out_rows = jnp.concatenate(out_rows, axis=0)
    for (kx,), value in gather_blocks(out_rows, ("x",)).items():
        starts = [
            ((came_from("y", ky) * zs + came_from("z", kz)) * xs + came_from("x", kx)) * shard_rows
            for ky in range(ys)
            for kz in range(zs)
        ]
        out_pieces.append((value, starts, 0))
    cot_hops = [tied(cot_rows, hop)]
    for _ in range(1, zs):
        cot_hops.append(shift(cot_hops[-1], "z", 1))
    for kz in range(1, zs):
        for (kx,), value in gather_blocks(cot_hops[kz], ("x",)).items():
            cot_blocks[(kz, kx)] = value

    weights = [
        lax.all_gather(w, ("y", "c"), axis=1, tiled=True)
        for w in weight_shards
    ]

    small = qkv_weight[:, 3 * width :].astype(F32)
    qkv_weight = qkv_weight[:, : 3 * width]
    attn_gain_f = small[:, 0][None, :]
    ffn_gain_f = small[:, 1][None, :]
    router = small[:, 2 : 2 + experts].astype(BF)
    per_device = small.reshape(-1, shard_rows, EXTRA)[:, :head_shard]
    head_gains = jnp.stack(
        [per_device[:, :, 2 + experts].reshape(HD), per_device[:, :, 3 + experts].reshape(HD)]
    )
    held = [value for kx in range(xs) for value in (x_tokens[(kx,)], swap(x_tokens[(kx,)]))]
    group_tokens = jnp.concatenate(held, axis=0)
    tokens_f = group_tokens.astype(F32)
    token_scale = lax.rsqrt(jnp.mean(tokens_f * tokens_f, axis=-1, keepdims=True) + EPSILON)
    normed = (tokens_f * token_scale * attn_gain_f).astype(BF)
    qkv = plain(normed, qkv_weight)
    qkv = tied(qkv, (cot_hops[1], [value for value, _, _ in out_pieces]))
    out_weight = place(out_pieces, shard_rows, (half_width, D))
    cosine, sine = rope_tables(rows)
    mixed = attend(qkv, group_lengths, head_gains, cosine, sine, rows, heads)
    chip_rows = 2 * own
    parts = [mixed[:chip_rows]]
    for k in range(1, xs):
        parts.append(shift(mixed[k * chip_rows : (k + 1) * chip_rows], "x", -k))
    mixed = jnp.zeros((chip_rows, half_width), BF)
    for k, part in enumerate(parts):
        place_at = jnp.mod(x + k, xs) * width
        mixed = lax.dynamic_update_slice(mixed, part, (0, place_at))
    early_swaps = [cot_blocks[(1, kx)] for kx in range(xs)]
    mixed = tied(mixed, (cot_hops[min(2, zs - 1)], early_swaps))
    partial = plain(mixed, out_weight)
    rows_f = token_rows.astype(F32)
    hidden = rows_f + (partial[:own] + swap(partial[own:]))
    hidden_scale = lax.rsqrt(jnp.mean(hidden * hidden, axis=-1, keepdims=True) + EPSILON)
    hidden_unit = hidden * hidden_scale
    routed_in = (hidden_unit * ffn_gain_f).astype(BF)
    gate_probs = jax.nn.softmax(plain(routed_in, router), axis=-1)

    routed_rows = jnp.concatenate([routed_in, widen(in_three(gate_probs), EXTRA)], axis=1)
    swaps = [[cot_blocks[(kz, kx)] for kx in range(xs)] for kz in range(zs)]
    hop = tied(routed_rows, (cot_hops[-1], swaps[: max(2, zs - 1)]))
    first_expert = ((z * xs + x) * local).astype(jnp.int32).reshape(1)
    per_call = math.gcd(xs, 2)
    back_parts, combined_parts, kept = {}, {}, None

    def call_experts(kz, swapped, kept):
        for some in range(0, xs, per_call):
            keys = [(kz, kx) for kx in range(some, some + per_call)]
            combined_part, back_part, kept = run_experts(
                first_expert,
                [swapped[(kx,)] for _, kx in keys],
                [cot_blocks[key] for key in keys],
                weights,
                kept,
                (kz * xs + some) // per_call,
                zs * xs // per_call,
                experts,
                rows,
                capacity,
            )
            back_parts.update(zip(keys, back_part, strict=True))
            combined_parts.update(zip(keys, combined_part, strict=True))
        return kept

    def moves(chain, parts, given):
        started = {}
        done = len(chain["sums"])
        if done < given:
            kz = chain["order"][done]
            total = parts[(kz, 1)]
            for kx in range(2, xs):
                total = parts[(kz, kx)].astype(F32) + shift(total.astype(BF), "x", 1).astype(F32)
            started["x"] = shift(total.astype(BF), "x", 1)
        if chain["hops"] < min(zs, done + chain["order"][0]):
            total = chain["sums"][chain["hops"] - chain["order"][0]]
            if chain["arrived"] is not None:
                total = total + chain["arrived"].astype(F32)
            started["z"] = shift(total.astype(BF), "z", 1)
        return started

    def settle(chain, parts, started):
        if "x" in started:
            kz = chain["order"][len(chain["sums"])]
            chain["sums"].append(parts[(kz, 0)].astype(F32) + started["x"].astype(F32))
        if "z" in started:
            chain["arrived"] = started["z"]
            chain["hops"] += 1

    def final(chain):
        return chain["sums"][chain["order"].index(0)] + chain["arrived"].astype(F32)

    back_chain = {"sums": [], "hops": 1, "arrived": None, "order": [*range(zs)]}
    combined_chain = {"sums": [], "hops": 1, "arrived": None, "order": [*range(1, zs), 0]}

    swapped = gather_blocks(hop, ("x",))
    hop = shift(hop, "z", 1)
    ready, hop = lax.optimization_barrier((swapped, hop))
    for kz in range(zs):
        coming = []
        if kz < zs - 1:
            coming = [gather_blocks(hop, ("x",))]
        if kz < zs - 2:
            hop = shift(hop, "z", 1)
        back_moves = moves(back_chain, back_parts, kz)
        kept = call_experts(kz, ready, kept)
        coming, hop, kept, back_moves = lax.optimization_barrier((coming, hop, kept, back_moves))
        settle(back_chain, back_parts, back_moves)
        ready = coming[0] if coming else None

    def weight_grads(left, right):
        return lax.dot_general(
            kept[left], kept[right], (((1,), (1,)), ((0,), (0,))), preferred_element_type=F32
        ).astype(BF)

    expert_grads, waiting = [], [(2, 1), (0, 3), (0, 4)]
    while back_chain["hops"] < zs or waiting:
        back_moves = moves(back_chain, back_parts, zs)
        last = back_chain["hops"] == zs - 1 and len(back_chain["sums"]) == zs
        combined_moves = moves(combined_chain, combined_parts, zs) if last else {}
        some, waiting = (waiting, []) if last else (waiting[:1], waiting[1:])
        some = [weight_grads(*pair) for pair in some]
        some, kept, back_moves, combined_moves = lax.optimization_barrier(
            (some, kept, back_moves, combined_moves)
        )
        expert_grads += some
        settle(back_chain, back_parts, back_moves)
        settle(combined_chain, combined_parts, combined_moves)
    down_grads, gate_grads, up_grads = expert_grads
    back = final(back_chain)

    def beside(value, others):
        parts = tied(combined_parts, others)
        started = moves(combined_chain, parts, zs)
        value, started = lax.optimization_barrier((value, started))
        settle(combined_chain, combined_parts, started)
        return value

    probs_grad = from_three(back[:, D:], experts)
    logits_grad = (
        gate_probs * (probs_grad - jnp.sum(gate_probs * probs_grad, axis=-1, keepdims=True))
    ).astype(BF)
    router_grad = inner(routed_in, logits_grad)
    routed_grad = back[:, :D] + times_t(logits_grad, router)
    hidden_add, ffn_gain_grad = norm_back(routed_grad, hidden_unit, hidden_scale, ffn_gain_f)
    hidden_grad = cotangent.astype(F32) + hidden_add
    attn_out_grad = hidden_grad.astype(BF)

    both_grads = jnp.concatenate([attn_out_grad, swap(attn_out_grad)], axis=0)
    mixed_grad = times_t(both_grads, out_weight).astype(BF)
    output_grad = inner(mixed, both_grads).astype(BF)
    mixed_grad = jnp.concatenate(
        sent_along("x", lambda i: lax.dynamic_slice_in_dim(mixed_grad, i * width, width, 1)), axis=0
    )
    qkv_grad, head_gain_grads = attend_back(
        qkv, mixed_grad, group_lengths, head_gains, cosine, sine, rows, heads
    )
    output_grad = output_grad.reshape(ys, zs, xs, shard_rows, D)
    qkv_grad = beside(qkv_grad, mixed_grad)
    normed_part = times_t(qkv_grad, qkv_weight)
    qkv_weight_grad = inner(normed, tied(qkv_grad, normed_part)).astype(BF)
    normed_sums = [
        reduce_blocks(lambda key: normed_part[(kx * 2 + key[0]) * own :][:own], ("c",)).astype(BF)
        for kx in range(xs)
    ]
    qkv_weight_grad, normed_sums = beside((qkv_weight_grad, normed_sums), qkv_grad)
    late = qkv_weight_grad.reshape(ys, 2, zs, xs, shard_rows, -1)

    def finish(normed_grad):
        token_unit = rows_f * token_scale[:own]
        tokens_add, attn_gain_grad = norm_back(
            normed_grad, token_unit, token_scale[:own], attn_gain_f
        )
        small_grad = jnp.concatenate(
            [
                attn_gain_grad[:, None],
                ffn_gain_grad[:, None],
                router_grad,
                jnp.pad(
                    head_gain_grads.reshape(2, -1, head_shard),
                    ((0, 0), (0, 0), (0, shard_rows - head_shard)),
                )
                .reshape(2, D)
                .T,
            ],
            axis=1,
        )
        small = widen(small_grad, EXTRA).astype(BF)
        return hidden_grad + tokens_add, small.reshape(ys, 2, zs, xs, shard_rows, EXTRA)

    def part_of(value, axis, dim, k):
        return lax.dynamic_index_in_dim(value, came_from(axis, k), dim, keepdims=False)

    ring = [*range(2, zs), 0]
    late_total = part_of(late, "z", 2, 1)
    output_x = output_y = output_total = None
    small_hops, output_hops = 0, 0
    for n, k in enumerate(ring):
        arrived = {"late": shift(late_total.astype(BF), "z", 1)}
        if n == 0:
            combined_parts = tied(combined_parts, late)
            arrived["combined"] = moves(combined_chain, combined_parts, zs)
            arrived["normed"] = reduce_blocks(lambda key: normed_sums[key[0]], ("x",))
        if n == 1:
            arrived["x"] = reduce_axis(tied(output_grad, late_total), "x", 2).astype(BF)
        if n == 2:
            arrived["y"] = reduce_axis(output_x, "y", 0).astype(BF)
        if n >= 1:
            arrived["small"] = shift(small_total.astype(BF), "z", 1)
        arrived = lax.optimization_barrier(arrived)
        late_total = part_of(late, "z", 2, k) + arrived["late"].astype(F32)
        if n == 0:
            settle(combined_chain, combined_parts, arrived["combined"])
            tokens_grad, small = finish(arrived["normed"])
            small_total = part_of(small, "z", 2, 1)
        if n == 1:
            output_x = arrived["x"]
        if n == 2:
            output_y = arrived["y"]
            output_total = part_of(output_y, "z", 0, 1)
        if n >= 1:
            part = part_of(small, "z", 2, ring[small_hops])
            small_total = part + arrived["small"].astype(F32)
            small_hops += 1
    combined = final(combined_chain)
    layer_out = (hidden + combined).astype(BF)
    expert_totals = [
        lax.psum_scatter(grad, ("y", "c"), scatter_dimension=1, tiled=True).astype(F32)
        for grad in (down_grads, gate_grads, up_grads)
    ]
    late = reduce_axis(late_total.astype(BF), "y", 0).astype(BF)
    arrived = [shift(small_total.astype(BF), "z", 1), shift(output_total.astype(BF), "z", 1)]
    late, arrived, expert_totals = lax.optimization_barrier((late, arrived, expert_totals))
    small = part_of(small, "z", 2, 0) + arrived[0].astype(F32)
    small = reduce_axis(small.astype(BF), "y", 0).astype(BF)
    output_total = part_of(output_y, "z", 0, ring[output_hops]) + arrived[1].astype(F32)
    output_hops += 1
    while output_hops < zs - 1:
        output_total = shift(output_total.astype(BF), "z", 1).astype(F32)
        output_total = part_of(output_y, "z", 0, ring[output_hops]) + output_total
        output_hops += 1
    output_weight_grad = output_total
    total = jnp.concatenate([late, small], axis=-1)
    columns = sent_along("x", lambda i: lax.dynamic_index_in_dim(total, i, 1, keepdims=False))
    columns = jnp.stack(columns)
    columns = sent_along("c", lambda i: lax.dynamic_index_in_dim(columns, i, 1, keepdims=False))
    small_total = sum(jnp.sum(some[:, :, 3 * width :].astype(F32), axis=0) for some in columns)

    def all_heads(at):
        halves = []
        for some in columns:
            half = jnp.zeros((shard_rows, half_width), BF)
            for k in range(xs):
                part = some[k][:, at * width : (at + 1) * width]
                half = lax.dynamic_update_slice(half, part, (0, jnp.mod(x - k, xs) * width))
            halves.append(half)
        low = jnp.where(c == 0, halves[0], halves[1]).reshape(shard_rows, ys, chunk)
        high = jnp.where(c == 0, halves[1], halves[0]).reshape(shard_rows, ys, chunk)
        return jnp.stack([low, high], axis=2).reshape(shard_rows, D).astype(F32)

    shape = (batches, 1, rows, D)
    return (
        layer_out.reshape(shape),
        tokens_grad.reshape(shape),
        small_total[:, 0],
        all_heads(0),
        all_heads(1),
        all_heads(2),
        output_weight_grad,
        small_total[:head_shard, 2 + experts],
        small_total[:head_shard, 3 + experts],
        small_total[:, 1],
        small_total[:, 2 : 2 + experts],
        expert_totals[1],
        expert_totals[2],
        expert_totals[0],
    )


def solution(mesh):
    dp, expert = mesh.shape["dp"], mesh.shape["expert"]
    zs = math.gcd(expert, 4)
    grid = Mesh(
        mesh.devices.reshape(dp // 2, 2, zs, expert // zs),
        ("y", "c", "z", "x"),
    )
    every, dps, exps = ("y", "c", "z", "x"), ("y", "c"), ("z", "x")
    in_specs = (
        P(None, every, None, None),
        P(None, every, None, None),
        P(None, every),
        P(None, every, None, None),
        P(None, every, None),
        P(every),
        P(every, None),
        P(every, None),
        P(every, None),
        P(every, None),
        P(every),
        P(every),
        P(every),
        P(every, None),
        P(exps, dps, None),
        P(exps, dps, None),
        P(exps, dps, None),
    )
    out_specs = (
        P(None, every, None, None),
        P(None, every, None, None),
        P(every),
        P(every, None),
        P(every, None),
        P(every, None),
        P(every, None),
        P(every),
        P(every),
        P(every),
        P(every, None),
        P(exps, dps, None),
        P(exps, dps, None),
        P(exps, dps, None),
    )
    return jax.shard_map(shards, mesh=grid, in_specs=in_specs, out_specs=out_specs, check_vma=False)
```

```python
import functools
import math

import jax
import jax.numpy as jnp
from jax import lax
from jax.experimental import pallas as pl
from jax.experimental.pallas import tpu as pltpu
from jax.sharding import Mesh
from jax.sharding import PartitionSpec as P

D = 2048
HEADS = 16
HD = 128
TOP = 8
EXTRA = 128

EPSILON = 1e-06
THETA = 50000.0
NEGATIVE = -1e30
BF = jnp.bfloat16
F32 = jnp.float32


def plain(left, right):
    return jnp.dot(left, right, preferred_element_type=F32)


def inner(left, right):
    return lax.dot_general(left, right, (((0,), (0,)), ((), ())), preferred_element_type=F32)


def times_t(left, right):
    return lax.dot_general(left, right, (((1,), (1,)), ((), ())), preferred_element_type=F32)


def tied(values, others):
    return lax.optimization_barrier((values, others))[0]


def ring_place(axis, at):
    return at ^ (at >> 1) if axis == "z" and lax.axis_size(axis) == 4 else at


def shift(value, axis, step):
    size = lax.axis_size(axis)
    pairs = [(ring_place(axis, i), ring_place(axis, (i + step) % size)) for i in range(size)]
    return lax.ppermute(value, axis, pairs)


def came_from(axis, k):
    at = ring_place(axis, lax.axis_index(axis))
    return ring_place(axis, jnp.mod(at - k, lax.axis_size(axis)))


def gather_blocks(block, order):
    held = {(): block}
    for axis in order:
        grown = {}
        for key, value in held.items():
            for k in range(lax.axis_size(axis)):
                if k:
                    value = shift(value, axis, 1)
                grown[key + (k,)] = value
        held = grown
    return held


def reduce_blocks(part, order):
    def reduce_from(key, depth):
        if depth == len(order):
            return part(key)
        axis = order[depth]
        size = lax.axis_size(axis)
        total = reduce_from(key + (1,), depth + 1)
        for k in [*range(2, size), 0]:
            arrived = shift(total.astype(BF), axis, 1)
            total = reduce_from(key + (k,), depth + 1).astype(F32) + arrived.astype(F32)
        return total

    return reduce_from((), 0)


def gather_pieces(block, order, merges):
    held = [(block, [()])]
    for depth, axis in enumerate(order):
        grown, level = [], held
        for k in range(lax.axis_size(axis)):
            if k:
                level = [(shift(value, axis, 1), keys) for value, keys in level]
            grown += [(value, [key + (k,) for key in keys]) for value, keys in level]
        if depth < len(merges):
            size = max(1, len(grown) // merges[depth])
            grown = [grown[i : i + size] for i in range(0, len(grown), size)]
            grown = [
                (
                    jnp.concatenate([value for value, _ in some], axis=0),
                    [key for _, keys in some for key in keys],
                )
                for some in grown
            ]
        held = grown
    return held


def reduce_axis(value, axis, dim):
    def part(k):
        return lax.dynamic_index_in_dim(value, came_from(axis, k), dim, keepdims=False)

    total = part(1)
    for k in [*range(2, lax.axis_size(axis)), 0]:
        arrived = shift(total.astype(BF), axis, 1)
        total = part(k).astype(F32) + arrived.astype(F32)
    return total


def place_kernel(plan, rows, offsets_ref, *refs):
    blocks, out, sems = refs[:-2], refs[-2], refs[-1]
    copies = []
    for i, (array, sub, column, width) in enumerate(plan):
        start = pl.multiple_of(offsets_ref[i], 16)
        copies.append(
            pltpu.make_async_copy(
                blocks[array].at[sub * rows : (sub + 1) * rows],
                out.at[pl.ds(start, rows), column : column + width],
                sems.at[i],
            )
        )
    for copy in copies:
        copy.start()
    for copy in copies:
        copy.wait()


def place(pieces, rows, shape):
    plan, offsets = [], []
    for array, (value, starts, column) in enumerate(pieces):
        for sub, start in enumerate(starts):
            plan.append((array, sub, column, value.shape[1]))
            offsets.append(start)
    return pl.pallas_call(
        functools.partial(place_kernel, plan, rows),
        out_shape=jax.ShapeDtypeStruct(shape, BF),
        grid_spec=pltpu.PrefetchScalarGridSpec(
            num_scalar_prefetch=1,
            in_specs=[pl.BlockSpec(memory_space=pl.ANY)] * len(pieces),
            out_specs=pl.BlockSpec(memory_space=pltpu.VMEM),
            scratch_shapes=[pltpu.SemaphoreType.DMA((len(plan),))],
        ),
        compiler_params=pltpu.CompilerParams(vmem_limit_bytes=24 << 20),
    )(jnp.stack(offsets).astype(jnp.int32), *[value for value, _, _ in pieces])


def rope_tables(row_count):
    half = HD // 2
    frequency = THETA ** (-jnp.arange(half, dtype=F32) / half)
    angles = jnp.arange(row_count, dtype=F32)[:, None] * frequency[None, :]
    cosine, sine = jnp.cos(angles), jnp.sin(angles)
    return jnp.concatenate([cosine, cosine], axis=1), jnp.concatenate([-sine, sine], axis=1)


def head_forward(raw, gain, cosine, sine):
    scale = lax.rsqrt(jnp.mean(raw * raw, axis=-1, keepdims=True) + EPSILON)
    unit = raw * scale
    value = unit * gain
    turned = value * cosine + pltpu.roll(value, HD // 2, 1) * sine
    return unit, scale, turned.astype(BF)


def head_backward(grad, unit, scale, gain, cosine, sine):
    grad = grad * cosine - pltpu.roll(grad, HD // 2, 1) * sine
    gain_grad = jnp.sum(grad * unit, axis=0, keepdims=True)
    grad = grad * gain
    grad = scale * (grad - unit * jnp.mean(grad * unit, axis=-1, keepdims=True))
    return grad.astype(BF), gain_grad


def attention_of(query, key, length):
    scores = times_t(query, key) * (1.0 / math.sqrt(HD))
    valid = lax.broadcasted_iota(jnp.int32, scores.shape, 1) < length
    scores = jnp.where(valid, scores, NEGATIVE)
    weight = jnp.exp(scores - jnp.max(scores, axis=-1, keepdims=True))
    return weight / jnp.sum(weight, axis=-1, keepdims=True)


def attend_kernel(heads, lengths_ref, qkv_ref, gains_ref, cosine_ref, sine_ref, mixed_ref):
    length = lengths_ref[pl.program_id(0)]
    cosine, sine = cosine_ref[...], sine_ref[...]
    query_gain, key_gain = gains_ref[0:1, :], gains_ref[1:2, :]
    width = heads * HD
    for h in range(heads):
        lo = h * HD
        query = head_forward(qkv_ref[:, lo : lo + HD], query_gain, cosine, sine)[2]
        key = head_forward(qkv_ref[:, width + lo : width + lo + HD], key_gain, cosine, sine)[2]
        value = qkv_ref[:, 2 * width + lo : 2 * width + lo + HD].astype(BF)
        attention = attention_of(query, key, length)
        mixed_ref[:, lo : lo + HD] = plain(attention.astype(BF), value).astype(BF)


def attend_back_kernel(
    heads, lengths_ref, qkv_ref, mixed_grad_ref, gains_ref, cosine_ref, sine_ref, out_ref, gain_ref
):
    @pl.when(pl.program_id(0) == 0)
    def _():
        gain_ref[...] = jnp.zeros_like(gain_ref)

    length = lengths_ref[pl.program_id(0)]
    cosine, sine = cosine_ref[...], sine_ref[...]
    query_gain, key_gain = gains_ref[0:1, :], gains_ref[1:2, :]
    width = heads * HD
    score_scale = 1.0 / math.sqrt(HD)
    for h in range(heads):
        lo = h * HD
        query_unit, query_scale, query = head_forward(
            qkv_ref[:, lo : lo + HD], query_gain, cosine, sine
        )
        key_unit, key_scale, key = head_forward(
            qkv_ref[:, width + lo : width + lo + HD], key_gain, cosine, sine
        )
        value = qkv_ref[:, 2 * width + lo : 2 * width + lo + HD].astype(BF)
        attention = attention_of(query, key, length)
        mixed_grad = mixed_grad_ref[:, lo : lo + HD]
        value_grad = inner(attention.astype(BF), mixed_grad)
        attention_grad = times_t(mixed_grad, value)
        score_grad = attention * (
            attention_grad - jnp.sum(attention * attention_grad, axis=-1, keepdims=True)
        )
        score_grad = score_grad.astype(BF)
        query_grad, query_gain_grad = head_backward(
            plain(score_grad, key) * score_scale, query_unit, query_scale, query_gain, cosine, sine
        )
        key_grad, key_gain_grad = head_backward(
            inner(score_grad, query) * score_scale, key_unit, key_scale, key_gain, cosine, sine
        )
        out_ref[:, lo : lo + HD] = query_grad
        out_ref[:, width + lo : width + lo + HD] = key_grad
        out_ref[:, 2 * width + lo : 2 * width + lo + HD] = value_grad.astype(BF)
        gain_ref[0:1, :] += query_gain_grad
        gain_ref[1:2, :] += key_gain_grad


def attend(qkv, lengths, gains, cosine, sine, rows, heads):
    sequences = qkv.shape[0] // rows
    width = heads * HD
    whole = pl.BlockSpec((2, HD), lambda s, n: (0, 0))
    table = pl.BlockSpec((rows, HD), lambda s, n: (0, 0))
    return pl.pallas_call(
        functools.partial(attend_kernel, heads),
        out_shape=jax.ShapeDtypeStruct((qkv.shape[0], width), BF),
        grid_spec=pltpu.PrefetchScalarGridSpec(
            num_scalar_prefetch=1,
            grid=(sequences,),
            in_specs=[
                pl.BlockSpec((rows, 3 * width), lambda s, n: (s, 0)),
                whole,
                table,
                table,
            ],
            out_specs=pl.BlockSpec((rows, width), lambda s, n: (s, 0)),
        ),
        compiler_params=pltpu.CompilerParams(vmem_limit_bytes=32 << 20),
        cost_estimate=pl.CostEstimate(flops=14 * 10**9, bytes_accessed=14 << 20, transcendentals=0),
    )(lengths, qkv, gains, cosine, sine)


def attend_back(qkv, mixed_grad, lengths, gains, cosine, sine, rows, heads):
    sequences = qkv.shape[0] // rows
    width = heads * HD
    whole = pl.BlockSpec((2, HD), lambda s, n: (0, 0))
    table = pl.BlockSpec((rows, HD), lambda s, n: (0, 0))
    return pl.pallas_call(
        functools.partial(attend_back_kernel, heads),
        out_shape=(
            jax.ShapeDtypeStruct((qkv.shape[0], 3 * width), BF),
            jax.ShapeDtypeStruct((2, HD), F32),
        ),
        grid_spec=pltpu.PrefetchScalarGridSpec(
            num_scalar_prefetch=1,
            grid=(sequences,),
            in_specs=[
                pl.BlockSpec((rows, 3 * width), lambda s, n: (s, 0)),
                pl.BlockSpec((rows, width), lambda s, n: (s, 0)),
                whole,
                table,
                table,
            ],
            out_specs=(
                pl.BlockSpec((rows, 3 * width), lambda s, n: (s, 0)),
                whole,
            ),
        ),
        compiler_params=pltpu.CompilerParams(vmem_limit_bytes=32 << 20),
        cost_estimate=pl.CostEstimate(flops=20 * 10**9, bytes_accessed=20 << 20, transcendentals=0),
    )(lengths, qkv, mixed_grad, gains, cosine, sine)


def experts_kernel(sizes, places_ref, *refs):
    part, groups, rows, experts, slots, local, ff = sizes
    take = iter(refs)
    row_refs = [next(take) for _ in range(groups)]
    cot_refs = [next(take) for _ in range(groups)]
    weight_refs = [next(take) for _ in range(3)]
    if part:
        for _ in range(5):
            next(take)
    combined_refs = [next(take) for _ in range(groups)]
    back_refs = [next(take) for _ in range(groups)]
    kept_refs = [next(take) for _ in range(5)]
    (rows_v, cots_v, gate_v, up_v, down_v, sent_v, grad_v, active_v, gate_grad_v, up_grad_v) = (
        next(take) for _ in range(10)
    )
    (cot_slots_v, returned_v, sent_grad_v, rank_v, prob_v, onehot_v, gated_v, sum_v) = (
        next(take) for _ in range(8)
    )
    in_sems, weight_sems, out_sems = (next(take) for _ in range(3))
    own = row_refs[0].shape[0]
    batches = own // rows
    sequences = groups * batches
    count = sequences * slots
    first = places_ref[0]

    loads = []
    for i in range(groups):
        loads.append(pltpu.make_async_copy(row_refs[i], rows_v.at[i], in_sems.at[2 * i]))
        loads.append(pltpu.make_async_copy(cot_refs[i], cots_v.at[i], in_sems.at[2 * i + 1]))
    for copy in loads:
        copy.start()
    weight_loads = [[] for _ in range(local)]
    for j in range(local):
        for w, target in enumerate((gate_v, up_v, down_v)):
            copy = pltpu.make_async_copy(
                weight_refs[w].at[j], target.at[j], weight_sems.at[j * 3 + w]
            )
            copy.start()
            weight_loads[j].append(copy)
    for copy in loads:
        copy.wait()

    slot = lax.broadcasted_iota(jnp.int32, (slots, rows), 0).astype(F32)
    for q in range(sequences):
        i, lo = q // batches, (q % batches) * rows
        rank_v[q] = cots_v[i, lo : lo + rows, D:].astype(F32).T
        prob_v[q] = rows_v[i, lo : lo + rows, D:].astype(F32).T
        onehots, gates = [], []
        for j in range(local):
            rank = rank_v[q, pl.ds(first + j, 1), :]
            prob = (
                prob_v[q, pl.ds(first + j, 1), :]
                + prob_v[q, pl.ds(experts + first + j, 1), :]
                + prob_v[q, pl.ds(2 * experts + first + j, 1), :]
            )
            chosen = rank == slot
            gated = jnp.where(chosen, prob, 0.0)
            onehot = jnp.where(chosen, 1.0, 0.0).astype(BF)
            onehot_v[q, j * slots : (j + 1) * slots, :] = onehot
            gated_v[q, j * slots : (j + 1) * slots, :] = gated.astype(BF)
            gates.append(jnp.sum(gated, axis=1, keepdims=True))
        gate_slots = jnp.concatenate(gates, axis=0)
        onehots = onehot_v[q]

        sent = plain(onehots, rows_v[i, lo : lo + rows, :D]).astype(BF)
        cots = plain(onehots, cots_v[i, lo : lo + rows, :D])
        grads = (cots * gate_slots).astype(BF)
        cots = cots.astype(BF)
        for j in range(local):
            window = slice(j * slots, (j + 1) * slots)
            place = slice(q * slots, (q + 1) * slots)
            sent_v[j, place, :] = sent[window]
            cot_slots_v[j, place, :] = cots[window]
            grad_v[j, place, :] = grads[window]

    stores = []

    def store(index, source, j):
        target = kept_refs[index].at[j, pl.ds(part * count, count)]
        copy = pltpu.make_async_copy(source.at[j], target, out_sems.at[index * local + j])
        copy.start()
        stores.append(copy)

    for j in range(local):
        store(0, sent_v, j)
        store(1, grad_v, j)
    for j in range(local):
        for copy in weight_loads[j]:
            copy.wait()

        @pl.loop(0, ff // 512)
        def _(n):
            at = pl.ds(pl.multiple_of(n * 512, 512), 512)
            gate_hidden = plain(sent_v[j], gate_v[j, :, at])
            up_hidden = plain(sent_v[j], up_v[j, :, at])
            active_grad = times_t(grad_v[j], down_v[j, at, :])
            sigmoid = jax.nn.sigmoid(gate_hidden)
            silu = gate_hidden * sigmoid
            active_v[j, :, at] = (silu * up_hidden).astype(BF)
            gate_grad_v[j, :, at] = (
                active_grad * up_hidden * sigmoid * (1.0 + gate_hidden * (1.0 - sigmoid))
            ).astype(BF)
            up_grad_v[j, :, at] = (active_grad * silu).astype(BF)

        store(2, active_v, j)
        store(3, gate_grad_v, j)
        store(4, up_grad_v, j)

        sum_v[j] = jnp.zeros_like(sum_v[j])

        @pl.loop(0, D // 1024)
        def _(n):
            at = pl.ds(pl.multiple_of(n * 1024, 1024), 1024)
            returned = plain(active_v[j], down_v[j, :, at]).astype(BF)
            returned_v[j, :, at] = returned
            product = cot_slots_v[j, :, at].astype(F32) * returned.astype(F32)
            folded = product[:, :128]
            for m in range(1, 1024 // 128):
                folded = folded + product[:, m * 128 : (m + 1) * 128]
            sum_v[j] += folded
            sent_grad = times_t(gate_grad_v[j], gate_v[j, at, :])
            sent_grad = sent_grad + times_t(up_grad_v[j], up_v[j, at, :])
            sent_grad_v[j, :, at] = sent_grad.astype(BF)

    column = lax.broadcasted_iota(jnp.int32, (EXTRA, rows), 0)
    for q in range(sequences):
        i, lo = q // batches, (q % batches) * rows
        place = slice(q * slots, (q + 1) * slots)
        table = jnp.zeros((EXTRA, rows), F32)
        for j in range(local):
            gates_grad = jnp.sum(sum_v[j, place, :], axis=1, keepdims=True)
            onehot = onehot_v[q, j * slots : (j + 1) * slots, :].astype(F32)
            value = jnp.sum(onehot * gates_grad, axis=0, keepdims=True)
            for m in range(3):
                high = value.astype(BF).astype(F32)
                table = table + jnp.where(column == m * experts + first + j, high, 0.0)
                value = value - high
        back_refs[i][lo : lo + rows, D:] = table.T.astype(BF)
        onehots, gates = onehot_v[q], gated_v[q]

        returned = jnp.concatenate([returned_v[j, place, :] for j in range(local)], axis=0)
        sent_grad = jnp.concatenate([sent_grad_v[j, place, :] for j in range(local)], axis=0)
        combined_refs[i][lo : lo + rows, :] = inner(gates, returned).astype(BF)
        back_refs[i][lo : lo + rows, :D] = inner(onehots, sent_grad).astype(BF)

    for copy in stores:
        copy.wait()


def run_experts(
    places, row_blocks, cot_blocks, weights, kept, part, parts, experts, rows, capacity
):
    groups = len(row_blocks)
    own = row_blocks[0].shape[0]
    sequences = groups * (own // rows)
    slots = (capacity + 15) // 16 * 16
    count = sequences * slots
    local, _, ff = weights[0].shape
    any_space = pl.BlockSpec(memory_space=pl.ANY)
    in_vmem = pl.BlockSpec(memory_space=pltpu.VMEM)
    widths = (D, D, ff, ff, ff)
    operands = [*row_blocks, *cot_blocks, *weights]
    aliases = {}
    if kept is not None:
        aliases = {1 + len(operands) + i: 2 * groups + i for i in range(5)}
        operands = operands + list(kept)
    scratch = [
        pltpu.VMEM((groups, own, D + EXTRA), BF),
        pltpu.VMEM((groups, own, D + EXTRA), BF),
        *[pltpu.VMEM(w.shape, BF) for w in weights],
        *[pltpu.VMEM((local, count, w), BF) for w in widths],
        pltpu.VMEM((local, count, D), BF),
        pltpu.VMEM((local, count, D), BF),
        pltpu.VMEM((local, count, D), BF),
        pltpu.VMEM((sequences, EXTRA, rows), F32),
        pltpu.VMEM((sequences, EXTRA, rows), F32),
        pltpu.VMEM((sequences, local * slots, rows), BF),
        pltpu.VMEM((sequences, local * slots, rows), BF),
        pltpu.VMEM((local, count, 128), F32),
        pltpu.SemaphoreType.DMA((2 * groups,)),
        pltpu.SemaphoreType.DMA((3 * local,)),
        pltpu.SemaphoreType.DMA((5 * local,)),
    ]
    sizes = (part, groups, rows, experts, slots, local, ff)
    results = pl.pallas_call(
        functools.partial(experts_kernel, sizes),
        out_shape=(
            *[jax.ShapeDtypeStruct((own, D), BF)] * groups,
            *[jax.ShapeDtypeStruct((own, D + EXTRA), BF)] * groups,
            *[jax.ShapeDtypeStruct((local, parts * count, w), BF) for w in widths],
        ),
        grid_spec=pltpu.PrefetchScalarGridSpec(
            num_scalar_prefetch=1,
            in_specs=[any_space] * len(operands),
            out_specs=(*[in_vmem] * (2 * groups), *[any_space] * 5),
            scratch_shapes=scratch,
        ),
        input_output_aliases=aliases,
        compiler_params=pltpu.CompilerParams(vmem_limit_bytes=60 << 20),
        cost_estimate=pl.CostEstimate(
            flops=40 * local * count * D * ff, bytes_accessed=40 << 20, transcendentals=0
        ),
    )(places, *operands)
    return results[:groups], results[groups : 2 * groups], results[2 * groups :]


def norm_back(grad, unit, scale, gain):
    scaled = grad * gain
    values_grad = scale * (scaled - unit * jnp.mean(scaled * unit, axis=-1, keepdims=True))
    return values_grad, jnp.sum(grad * unit, axis=0)


def slot_ranks(route, priority, experts, capacity):
    rows = route.shape[0]
    expert = jnp.arange(experts, dtype=jnp.int32)
    chosen = route[:, :, None] == expert[None, None, :]
    order = jnp.sum(jnp.where(chosen, priority.reshape(rows, TOP)[:, :, None], 0), axis=1)
    routed = jnp.any(chosen, axis=1)
    order = jnp.where(routed, order, rows * TOP).T
    rank = jnp.sum((order[:, None, :] < order[:, :, None]).astype(jnp.int32), axis=2).T
    return jnp.where(routed & (rank < capacity), rank, -1)


def in_three(value):
    high = value.astype(BF)
    rest = value - high.astype(F32)
    middle = rest.astype(BF)
    low = (rest - middle.astype(F32)).astype(BF)
    return jnp.concatenate([high, middle, low], axis=-1)


def from_three(columns, count):
    return (
        columns[..., :count].astype(F32)
        + columns[..., count : 2 * count].astype(F32)
        + columns[..., 2 * count : 3 * count].astype(F32)
    )


def widen(columns, width):
    return jnp.pad(columns, ((0, 0), (0, width - columns.shape[-1])))


def shards(
    tokens,
    out_cotangent,
    lengths,
    routes,
    priority,
    attn_gain,
    query_weight,
    key_weight,
    value_weight,
    output_weight,
    query_gain,
    key_gain,
    ffn_gain,
    router_weight,
    gate_weight,
    up_weight,
    down_weight,
):
    batches, rows = tokens.shape[0], tokens.shape[2]
    own = batches * rows
    experts = router_weight.shape[1]
    capacity = 5 * rows * TOP // (4 * experts)
    local = gate_weight.shape[0]
    ys, zs, xs = lax.axis_size("y"), lax.axis_size("z"), lax.axis_size("x")
    y, c, z, x = (lax.axis_index(name) for name in ("y", "c", "z", "x"))
    shard_rows = query_weight.shape[0]
    head_shard = query_gain.shape[0]
    heads = HEADS // (2 * xs)
    width = heads * HD
    half_width = D // 2
    chunk = D // (2 * ys)

    def swap(value):
        return lax.ppermute(value, "c", [(0, 1), (1, 0)])

    def sent_along(axis, piece_for):
        at, size = lax.axis_index(axis), lax.axis_size(axis)
        return [
            shift(piece_for(jnp.mod(at + k, size)), axis, k) if k else piece_for(at)
            for k in range(size)
        ]

    token_rows = tokens.reshape(own, D)
    length = lengths.reshape(batches)
    group_keys = [(kx, kc) for kx in range(xs) for kc in range(2)]
    x_tokens = gather_blocks(token_rows, ("x",))
    held = gather_blocks(length, ("x", "c"))
    group_lengths = jnp.concatenate([held[key] for key in group_keys])
    extra = jnp.concatenate(
        [
            attn_gain[:, None],
            ffn_gain[:, None],
            router_weight,
            jnp.pad(query_gain, (0, shard_rows - head_shard))[:, None],
            jnp.pad(key_gain, (0, shard_rows - head_shard))[:, None],
        ],
        axis=1,
    )
    extra = widen(extra, EXTRA)

    def row_offset(ky, kc, kz, kx):
        sources = (came_from("y", ky), came_from("c", kc), came_from("z", kz), came_from("x", kx))
        return (
            ((sources[0] * 2 + sources[1]) * zs + sources[2]) * xs + sources[3]
        ) * shard_rows

    def half_columns(weight, core):
        return jnp.concatenate(
            [
                lax.dynamic_slice_in_dim(weight, (2 * i + core) * chunk, chunk, 1)
                for i in range(ys)
            ],
            axis=1,
        )

    def packed(core):
        halves = [half_columns(w, core) for w in (query_weight, key_weight, value_weight)]
        return jnp.stack(
            [
                jnp.concatenate(
                    [half[:, i * width : (i + 1) * width] for half in halves] + [extra], axis=1
                )
                for i in range(xs)
            ]
        )

    out_hops = [output_weight]
    for _ in range(1, zs):
        out_hops.append(shift(out_hops[-1], "z", 1))
    block = jnp.concatenate(sent_along("c", packed), axis=1)
    block = jnp.concatenate(
        sent_along("x", lambda i: lax.dynamic_index_in_dim(block, i, 0, keepdims=False)), axis=0
    )
    ZX = ("z", "x")
    ranks = jnp.concatenate(
        [
            slot_ranks(routes[b, 0], priority[b, 0], experts, capacity)
            for b in range(batches)
        ],
        axis=0,
    )
    cotangent = out_cotangent.reshape(own, D)
    cot_rows = jnp.concatenate([cotangent, widen(ranks.astype(BF), EXTRA)], axis=1)
    cot_blocks = {(0, kx): v for (kx,), v in gather_blocks(cot_rows, ("x",)).items()}
    block = tied(block, out_hops[1])
    late = list(gather_blocks(block, ("y",)).values())
    late = jnp.concatenate(tied(late, out_hops[2:3]), axis=0)
    weight_shards = tied((gate_weight, up_weight, down_weight), late)

    def offsets_of(kz):
        return [
            row_offset(ky, kc, kz, kx)
            for ky in range(ys)
            for kx in range(xs)
            for kc in range(2)
        ]

    qkv_pieces = []
    hop = late
    for kz in range(zs):
        if kz:
            hop = shift(hop, "z", 1)
            if kz == 1:
                hop, out_hops, x_tokens = lax.optimization_barrier((hop, out_hops, x_tokens))
                out_rows = jnp.concatenate(out_hops, axis=0)
                out_rows = list(gather_blocks(out_rows, ("y",)).values())
            if kz == 2:
                hop, out_rows, cot_blocks = lax.optimization_barrier((hop, out_rows, cot_blocks))
        qkv_pieces.append((hop, offsets_of(kz), 0))
    qkv_weight = place(qkv_pieces, shard_rows, (D, 3 * width + EXTRA))
    out_pieces = []
    out_rows = jnp.concatenate(out_rows, axis=0)
    for (kx,), value in gather_blocks(out_rows, ("x",)).items():
        starts = [
            ((came_from("y", ky) * zs + came_from("z", kz)) * xs + came_from("x", kx)) * shard_rows
            for ky in range(ys)
            for kz in range(zs)
        ]
        out_pieces.append((value, starts, 0))
    cot_hops = [tied(cot_rows, hop)]
    for _ in range(1, zs):
        cot_hops.append(shift(cot_hops[-1], "z", 1))
    for kz in range(1, zs):
        for (kx,), value in gather_blocks(cot_hops[kz], ("x",)).items():
            cot_blocks[(kz, kx)] = value

    weights = [
        lax.all_gather(w, ("y", "c"), axis=1, tiled=True)
        for w in weight_shards
    ]

    small = qkv_weight[:, 3 * width :].astype(F32)
    qkv_weight = qkv_weight[:, : 3 * width]
    attn_gain_f = small[:, 0][None, :]
    ffn_gain_f = small[:, 1][None, :]
    router = small[:, 2 : 2 + experts].astype(BF)
    per_device = small.reshape(-1, shard_rows, EXTRA)[:, :head_shard]
    head_gains = jnp.stack(
        [per_device[:, :, 2 + experts].reshape(HD), per_device[:, :, 3 + experts].reshape(HD)]
    )
    held = [value for kx in range(xs) for value in (x_tokens[(kx,)], swap(x_tokens[(kx,)]))]
    group_tokens = jnp.concatenate(held, axis=0)
    tokens_f = group_tokens.astype(F32)
    token_scale = lax.rsqrt(jnp.mean(tokens_f * tokens_f, axis=-1, keepdims=True) + EPSILON)
    normed = (tokens_f * token_scale * attn_gain_f).astype(BF)
    qkv = plain(normed, qkv_weight)
    qkv = tied(qkv, (cot_hops[1], [value for value, _, _ in out_pieces]))
    out_weight = place(out_pieces, shard_rows, (half_width, D))
    cosine, sine = rope_tables(rows)
    mixed = attend(qkv, group_lengths, head_gains, cosine, sine, rows, heads)
    chip_rows = 2 * own
    parts = [mixed[:chip_rows]]
    for k in range(1, xs):
        parts.append(shift(mixed[k * chip_rows : (k + 1) * chip_rows], "x", -k))
    mixed = jnp.zeros((chip_rows, half_width), BF)
    for k, part in enumerate(parts):
        place_at = jnp.mod(x + k, xs) * width
        mixed = lax.dynamic_update_slice(mixed, part, (0, place_at))
    early_swaps = [cot_blocks[(1, kx)] for kx in range(xs)]
    mixed = tied(mixed, (cot_hops[min(2, zs - 1)], early_swaps))
    partial = plain(mixed, out_weight)
    rows_f = token_rows.astype(F32)
    hidden = rows_f + (partial[:own] + swap(partial[own:]))
    hidden_scale = lax.rsqrt(jnp.mean(hidden * hidden, axis=-1, keepdims=True) + EPSILON)
    hidden_unit = hidden * hidden_scale
    routed_in = (hidden_unit * ffn_gain_f).astype(BF)
    gate_probs = jax.nn.softmax(plain(routed_in, router), axis=-1)

    routed_rows = jnp.concatenate([routed_in, widen(in_three(gate_probs), EXTRA)], axis=1)
    swaps = [[cot_blocks[(kz, kx)] for kx in range(xs)] for kz in range(zs)]
    hop = tied(routed_rows, (cot_hops[-1], swaps[: max(2, zs - 1)]))
    first_expert = ((z * xs + x) * local).astype(jnp.int32).reshape(1)
    per_call = math.gcd(xs, 2)
    back_parts, combined_parts, kept = {}, {}, None

    def call_experts(kz, swapped, kept):
        for some in range(0, xs, per_call):
            keys = [(kz, kx) for kx in range(some, some + per_call)]
            combined_part, back_part, kept = run_experts(
                first_expert,
                [swapped[(kx,)] for _, kx in keys],
                [cot_blocks[key] for key in keys],
                weights,
                kept,
                (kz * xs + some) // per_call,
                zs * xs // per_call,
                experts,
                rows,
                capacity,
            )
            back_parts.update(zip(keys, back_part, strict=True))
            combined_parts.update(zip(keys, combined_part, strict=True))
        return kept

    def moves(chain, parts, given):
        started = {}
        done = len(chain["sums"])
        if done < given:
            kz = chain["order"][done]
            total = parts[(kz, 1)]
            for kx in range(2, xs):
                total = parts[(kz, kx)].astype(F32) + shift(total.astype(BF), "x", 1).astype(F32)
            started["x"] = shift(total.astype(BF), "x", 1)
        if chain["hops"] < min(zs, done + chain["order"][0]):
            total = chain["sums"][chain["hops"] - chain["order"][0]]
            if chain["arrived"] is not None:
                total = total + chain["arrived"].astype(F32)
            started["z"] = shift(total.astype(BF), "z", 1)
        return started

    def settle(chain, parts, started):
        if "x" in started:
            kz = chain["order"][len(chain["sums"])]
            chain["sums"].append(parts[(kz, 0)].astype(F32) + started["x"].astype(F32))
        if "z" in started:
            chain["arrived"] = started["z"]
            chain["hops"] += 1

    def final(chain):
        return chain["sums"][chain["order"].index(0)] + chain["arrived"].astype(F32)

    back_chain = {"sums": [], "hops": 1, "arrived": None, "order": [*range(zs)]}
    combined_chain = {"sums": [], "hops": 1, "arrived": None, "order": [*range(1, zs), 0]}

    swapped = gather_blocks(hop, ("x",))
    hop = shift(hop, "z", 1)
    ready, hop = lax.optimization_barrier((swapped, hop))
    for kz in range(zs):
        coming = []
        if kz < zs - 1:
            coming = [gather_blocks(hop, ("x",))]
        if kz < zs - 2:
            hop = shift(hop, "z", 1)
        back_moves = moves(back_chain, back_parts, kz)
        kept = call_experts(kz, ready, kept)
        coming, hop, kept, back_moves = lax.optimization_barrier((coming, hop, kept, back_moves))
        settle(back_chain, back_parts, back_moves)
        ready = coming[0] if coming else None

    def weight_grads(left, right):
        return lax.dot_general(
            kept[left], kept[right], (((1,), (1,)), ((0,), (0,))), preferred_element_type=F32
        ).astype(BF)

    expert_grads, waiting = [], [(2, 1), (0, 3), (0, 4)]
    while back_chain["hops"] < zs or waiting:
        back_moves = moves(back_chain, back_parts, zs)
        last = back_chain["hops"] == zs - 1 and len(back_chain["sums"]) == zs
        combined_moves = moves(combined_chain, combined_parts, zs) if last else {}
        some, waiting = (waiting, []) if last else (waiting[:1], waiting[1:])
        some = [weight_grads(*pair) for pair in some]
        some, kept, back_moves, combined_moves = lax.optimization_barrier(
            (some, kept, back_moves, combined_moves)
        )
        expert_grads += some
        settle(back_chain, back_parts, back_moves)
        settle(combined_chain, combined_parts, combined_moves)
    down_grads, gate_grads, up_grads = expert_grads
    back = final(back_chain)

    def beside(value, others):
        parts = tied(combined_parts, others)
        started = moves(combined_chain, parts, zs)
        value, started = lax.optimization_barrier((value, started))
        settle(combined_chain, combined_parts, started)
        return value

    probs_grad = from_three(back[:, D:], experts)
    logits_grad = (
        gate_probs * (probs_grad - jnp.sum(gate_probs * probs_grad, axis=-1, keepdims=True))
    ).astype(BF)
    router_grad = inner(routed_in, logits_grad)
    routed_grad = back[:, :D] + times_t(logits_grad, router)
    hidden_add, ffn_gain_grad = norm_back(routed_grad, hidden_unit, hidden_scale, ffn_gain_f)
    hidden_grad = cotangent.astype(F32) + hidden_add
    attn_out_grad = hidden_grad.astype(BF)

    both_grads = jnp.concatenate([attn_out_grad, swap(attn_out_grad)], axis=0)
    mixed_grad = times_t(both_grads, out_weight).astype(BF)
    output_grad = inner(mixed, both_grads).astype(BF)
    mixed_grad = jnp.concatenate(
        sent_along("x", lambda i: lax.dynamic_slice_in_dim(mixed_grad, i * width, width, 1)), axis=0
    )
    qkv_grad, head_gain_grads = attend_back(
        qkv, mixed_grad, group_lengths, head_gains, cosine, sine, rows, heads
    )
    output_grad = output_grad.reshape(ys, zs, xs, shard_rows, D)
    qkv_grad = beside(qkv_grad, mixed_grad)
    normed_part = times_t(qkv_grad, qkv_weight)
    qkv_weight_grad = inner(normed, tied(qkv_grad, normed_part)).astype(BF)
    normed_sums = [
        reduce_blocks(lambda key: normed_part[(kx * 2 + key[0]) * own :][:own], ("c",)).astype(BF)
        for kx in range(xs)
    ]
    qkv_weight_grad, normed_sums = beside((qkv_weight_grad, normed_sums), qkv_grad)
    late = qkv_weight_grad.reshape(ys, 2, zs, xs, shard_rows, -1)

    def finish(normed_grad):
        token_unit = rows_f * token_scale[:own]
        tokens_add, attn_gain_grad = norm_back(
            normed_grad, token_unit, token_scale[:own], attn_gain_f
        )
        small_grad = jnp.concatenate(
            [
                attn_gain_grad[:, None],
                ffn_gain_grad[:, None],
                router_grad,
                jnp.pad(
                    head_gain_grads.reshape(2, -1, head_shard),
                    ((0, 0), (0, 0), (0, shard_rows - head_shard)),
                )
                .reshape(2, D)
                .T,
            ],
            axis=1,
        )
        small = widen(small_grad, EXTRA).astype(BF)
        return hidden_grad + tokens_add, small.reshape(ys, 2, zs, xs, shard_rows, EXTRA)

    def part_of(value, axis, dim, k):
        return lax.dynamic_index_in_dim(value, came_from(axis, k), dim, keepdims=False)

    ring = [*range(2, zs), 0]
    late_total = part_of(late, "z", 2, 1)
    output_x = output_y = output_total = None
    small_hops, output_hops = 0, 0
    expert_totals = [
        lax.psum_scatter(grad, ("y", "c"), scatter_dimension=1, tiled=True).astype(F32)
        for grad in (down_grads, gate_grads, up_grads)
    ]
    for n, k in enumerate(ring):
        arrived = {"late": shift(late_total.astype(BF), "z", 1)}
        if n == 0:
            combined_parts = tied(combined_parts, late)
            arrived["combined"] = moves(combined_chain, combined_parts, zs)
            arrived["normed"] = reduce_blocks(lambda key: normed_sums[key[0]], ("x",))
        if n == 1:
            arrived["x"] = reduce_axis(tied(output_grad, late_total), "x", 2).astype(BF)
        if n == 2:
            arrived["y"] = reduce_axis(output_x, "y", 0).astype(BF)
            arrived["experts"] = expert_totals
        if n >= 1:
            arrived["small"] = shift(small_total.astype(BF), "z", 1)
        arrived = lax.optimization_barrier(arrived)
        late_total = part_of(late, "z", 2, k) + arrived["late"].astype(F32)
        if n == 0:
            settle(combined_chain, combined_parts, arrived["combined"])
            tokens_grad, small = finish(arrived["normed"])
            small_total = part_of(small, "z", 2, 1)
        if n == 1:
            output_x = arrived["x"]
        if n == 2:
            output_y = arrived["y"]
            expert_totals = arrived["experts"]
            output_total = part_of(output_y, "z", 0, 1)
        if n >= 1:
            part = part_of(small, "z", 2, ring[small_hops])
            small_total = part + arrived["small"].astype(F32)
            small_hops += 1
    combined = final(combined_chain)
    layer_out = (hidden + combined).astype(BF)
    late = reduce_axis(late_total.astype(BF), "y", 0).astype(BF)
    arrived = [shift(small_total.astype(BF), "z", 1), shift(output_total.astype(BF), "z", 1)]
    late, arrived = lax.optimization_barrier((late, arrived))
    small = part_of(small, "z", 2, 0) + arrived[0].astype(F32)
    small = reduce_axis(small.astype(BF), "y", 0).astype(BF)
    output_total = part_of(output_y, "z", 0, ring[output_hops]) + arrived[1].astype(F32)
    output_hops += 1
    while output_hops < zs - 1:
        output_total = shift(output_total.astype(BF), "z", 1).astype(F32)
        output_total = part_of(output_y, "z", 0, ring[output_hops]) + output_total
        output_hops += 1
    output_weight_grad = output_total
    total = jnp.concatenate([late, small], axis=-1)
    columns = sent_along("x", lambda i: lax.dynamic_index_in_dim(total, i, 1, keepdims=False))
    columns = jnp.stack(columns)
    columns = sent_along("c", lambda i: lax.dynamic_index_in_dim(columns, i, 1, keepdims=False))
    small_total = sum(jnp.sum(some[:, :, 3 * width :].astype(F32), axis=0) for some in columns)

    def all_heads(at):
        halves = []
        for some in columns:
            half = jnp.zeros((shard_rows, half_width), BF)
            for k in range(xs):
                part = some[k][:, at * width : (at + 1) * width]
                half = lax.dynamic_update_slice(half, part, (0, jnp.mod(x - k, xs) * width))
            halves.append(half)
        low = jnp.where(c == 0, halves[0], halves[1]).reshape(shard_rows, ys, chunk)
        high = jnp.where(c == 0, halves[1], halves[0]).reshape(shard_rows, ys, chunk)
        return jnp.stack([low, high], axis=2).reshape(shard_rows, D).astype(F32)

    shape = (batches, 1, rows, D)
    return (
        layer_out.reshape(shape),
        tokens_grad.reshape(shape),
        small_total[:, 0],
        all_heads(0),
        all_heads(1),
        all_heads(2),
        output_weight_grad,
        small_total[:head_shard, 2 + experts],
        small_total[:head_shard, 3 + experts],
        small_total[:, 1],
        small_total[:, 2 : 2 + experts],
        expert_totals[1],
        expert_totals[2],
        expert_totals[0],
    )


def solution(mesh):
    dp, expert = mesh.shape["dp"], mesh.shape["expert"]
    zs = math.gcd(expert, 4)
    grid = Mesh(
        mesh.devices.reshape(dp // 2, 2, zs, expert // zs),
        ("y", "c", "z", "x"),
    )
    every, dps, exps = ("y", "c", "z", "x"), ("y", "c"), ("z", "x")
    in_specs = (
        P(None, every, None, None),
        P(None, every, None, None),
        P(None, every),
        P(None, every, None, None),
        P(None, every, None),
        P(every),
        P(every, None),
        P(every, None),
        P(every, None),
        P(every, None),
        P(every),
        P(every),
        P(every),
        P(every, None),
        P(exps, dps, None),
        P(exps, dps, None),
        P(exps, dps, None),
    )
    out_specs = (
        P(None, every, None, None),
        P(None, every, None, None),
        P(every),
        P(every, None),
        P(every, None),
        P(every, None),
        P(every, None),
        P(every),
        P(every),
        P(every),
        P(every, None),
        P(exps, dps, None),
        P(exps, dps, None),
        P(exps, dps, None),
    )
    return jax.shard_map(shards, mesh=grid, in_specs=in_specs, out_specs=out_specs, check_vma=False)
```

```python
import functools
import math

import jax
import jax.numpy as jnp
from jax import lax
from jax.experimental import pallas as pl
from jax.experimental.pallas import tpu as pltpu
from jax.sharding import Mesh
from jax.sharding import PartitionSpec as P

D = 2048
HEADS = 16
HD = 128
TOP = 8
EXTRA = 128

EPSILON = 1e-06
THETA = 50000.0
NEGATIVE = -1e30
BF = jnp.bfloat16
F32 = jnp.float32


def plain(left, right):
    return jnp.dot(left, right, preferred_element_type=F32)


def inner(left, right):
    return lax.dot_general(left, right, (((0,), (0,)), ((), ())), preferred_element_type=F32)


def times_t(left, right):
    return lax.dot_general(left, right, (((1,), (1,)), ((), ())), preferred_element_type=F32)


def tied(values, others):
    return lax.optimization_barrier((values, others))[0]


def ring_place(axis, at):
    return at ^ (at >> 1) if axis == "z" and lax.axis_size(axis) == 4 else at


def shift(value, axis, step):
    size = lax.axis_size(axis)
    pairs = [(ring_place(axis, i), ring_place(axis, (i + step) % size)) for i in range(size)]
    return lax.ppermute(value, axis, pairs)


def came_from(axis, k):
    at = ring_place(axis, lax.axis_index(axis))
    return ring_place(axis, jnp.mod(at - k, lax.axis_size(axis)))


def gather_blocks(block, order):
    held = {(): block}
    for axis in order:
        grown = {}
        for key, value in held.items():
            for k in range(lax.axis_size(axis)):
                if k:
                    value = shift(value, axis, 1)
                grown[key + (k,)] = value
        held = grown
    return held


def reduce_blocks(part, order):
    def reduce_from(key, depth):
        if depth == len(order):
            return part(key)
        axis = order[depth]
        size = lax.axis_size(axis)
        total = reduce_from(key + (1,), depth + 1)
        for k in [*range(2, size), 0]:
            arrived = shift(total.astype(BF), axis, 1)
            total = reduce_from(key + (k,), depth + 1).astype(F32) + arrived.astype(F32)
        return total

    return reduce_from((), 0)


def gather_pieces(block, order, merges):
    held = [(block, [()])]
    for depth, axis in enumerate(order):
        grown, level = [], held
        for k in range(lax.axis_size(axis)):
            if k:
                level = [(shift(value, axis, 1), keys) for value, keys in level]
            grown += [(value, [key + (k,) for key in keys]) for value, keys in level]
        if depth < len(merges):
            size = max(1, len(grown) // merges[depth])
            grown = [grown[i : i + size] for i in range(0, len(grown), size)]
            grown = [
                (
                    jnp.concatenate([value for value, _ in some], axis=0),
                    [key for _, keys in some for key in keys],
                )
                for some in grown
            ]
        held = grown
    return held


def reduce_axis(value, axis, dim):
    def part(k):
        return lax.dynamic_index_in_dim(value, came_from(axis, k), dim, keepdims=False)

    total = part(1)
    for k in [*range(2, lax.axis_size(axis)), 0]:
        arrived = shift(total.astype(BF), axis, 1)
        total = part(k).astype(F32) + arrived.astype(F32)
    return total


def place_kernel(plan, rows, offsets_ref, *refs):
    blocks, out, sems = refs[:-2], refs[-2], refs[-1]
    copies = []
    for i, (array, sub, column, width) in enumerate(plan):
        start = pl.multiple_of(offsets_ref[i], 16)
        copies.append(
            pltpu.make_async_copy(
                blocks[array].at[sub * rows : (sub + 1) * rows],
                out.at[pl.ds(start, rows), column : column + width],
                sems.at[i],
            )
        )
    for copy in copies:
        copy.start()
    for copy in copies:
        copy.wait()


def place(pieces, rows, shape):
    plan, offsets = [], []
    for array, (value, starts, column) in enumerate(pieces):
        for sub, start in enumerate(starts):
            plan.append((array, sub, column, value.shape[1]))
            offsets.append(start)
    return pl.pallas_call(
        functools.partial(place_kernel, plan, rows),
        out_shape=jax.ShapeDtypeStruct(shape, BF),
        grid_spec=pltpu.PrefetchScalarGridSpec(
            num_scalar_prefetch=1,
            in_specs=[pl.BlockSpec(memory_space=pl.ANY)] * len(pieces),
            out_specs=pl.BlockSpec(memory_space=pltpu.VMEM),
            scratch_shapes=[pltpu.SemaphoreType.DMA((len(plan),))],
        ),
        compiler_params=pltpu.CompilerParams(vmem_limit_bytes=24 << 20),
    )(jnp.stack(offsets).astype(jnp.int32), *[value for value, _, _ in pieces])


def rope_tables(row_count):
    half = HD // 2
    frequency = THETA ** (-jnp.arange(half, dtype=F32) / half)
    angles = jnp.arange(row_count, dtype=F32)[:, None] * frequency[None, :]
    cosine, sine = jnp.cos(angles), jnp.sin(angles)
    return jnp.concatenate([cosine, cosine], axis=1), jnp.concatenate([-sine, sine], axis=1)


def head_forward(raw, gain, cosine, sine):
    scale = lax.rsqrt(jnp.mean(raw * raw, axis=-1, keepdims=True) + EPSILON)
    unit = raw * scale
    value = unit * gain
    turned = value * cosine + pltpu.roll(value, HD // 2, 1) * sine
    return unit, scale, turned.astype(BF)


def head_backward(grad, unit, scale, gain, cosine, sine):
    grad = grad * cosine - pltpu.roll(grad, HD // 2, 1) * sine
    gain_grad = jnp.sum(grad * unit, axis=0, keepdims=True)
    grad = grad * gain
    grad = scale * (grad - unit * jnp.mean(grad * unit, axis=-1, keepdims=True))
    return grad.astype(BF), gain_grad


def attention_of(query, key, length):
    scores = times_t(query, key) * (1.0 / math.sqrt(HD))
    valid = lax.broadcasted_iota(jnp.int32, scores.shape, 1) < length
    scores = jnp.where(valid, scores, NEGATIVE)
    weight = jnp.exp(scores - jnp.max(scores, axis=-1, keepdims=True))
    return weight / jnp.sum(weight, axis=-1, keepdims=True)


def attend_kernel(heads, lengths_ref, qkv_ref, gains_ref, cosine_ref, sine_ref, mixed_ref):
    length = lengths_ref[pl.program_id(0)]
    cosine, sine = cosine_ref[...], sine_ref[...]
    query_gain, key_gain = gains_ref[0:1, :], gains_ref[1:2, :]
    width = heads * HD
    for h in range(heads):
        lo = h * HD
        query = head_forward(qkv_ref[:, lo : lo + HD], query_gain, cosine, sine)[2]
        key = head_forward(qkv_ref[:, width + lo : width + lo + HD], key_gain, cosine, sine)[2]
        value = qkv_ref[:, 2 * width + lo : 2 * width + lo + HD].astype(BF)
        attention = attention_of(query, key, length)
        mixed_ref[:, lo : lo + HD] = plain(attention.astype(BF), value).astype(BF)


def attend_back_kernel(
    heads, lengths_ref, qkv_ref, mixed_grad_ref, gains_ref, cosine_ref, sine_ref, out_ref, gain_ref
):
    @pl.when(pl.program_id(0) == 0)
    def _():
        gain_ref[...] = jnp.zeros_like(gain_ref)

    length = lengths_ref[pl.program_id(0)]
    cosine, sine = cosine_ref[...], sine_ref[...]
    query_gain, key_gain = gains_ref[0:1, :], gains_ref[1:2, :]
    width = heads * HD
    score_scale = 1.0 / math.sqrt(HD)
    for h in range(heads):
        lo = h * HD
        query_unit, query_scale, query = head_forward(
            qkv_ref[:, lo : lo + HD], query_gain, cosine, sine
        )
        key_unit, key_scale, key = head_forward(
            qkv_ref[:, width + lo : width + lo + HD], key_gain, cosine, sine
        )
        value = qkv_ref[:, 2 * width + lo : 2 * width + lo + HD].astype(BF)
        attention = attention_of(query, key, length)
        mixed_grad = mixed_grad_ref[:, lo : lo + HD]
        value_grad = inner(attention.astype(BF), mixed_grad)
        attention_grad = times_t(mixed_grad, value)
        score_grad = attention * (
            attention_grad - jnp.sum(attention * attention_grad, axis=-1, keepdims=True)
        )
        score_grad = score_grad.astype(BF)
        query_grad, query_gain_grad = head_backward(
            plain(score_grad, key) * score_scale, query_unit, query_scale, query_gain, cosine, sine
        )
        key_grad, key_gain_grad = head_backward(
            inner(score_grad, query) * score_scale, key_unit, key_scale, key_gain, cosine, sine
        )
        out_ref[:, lo : lo + HD] = query_grad
        out_ref[:, width + lo : width + lo + HD] = key_grad
        out_ref[:, 2 * width + lo : 2 * width + lo + HD] = value_grad.astype(BF)
        gain_ref[0:1, :] += query_gain_grad
        gain_ref[1:2, :] += key_gain_grad


def attend(qkv, lengths, gains, cosine, sine, rows, heads):
    sequences = qkv.shape[0] // rows
    width = heads * HD
    whole = pl.BlockSpec((2, HD), lambda s, n: (0, 0))
    table = pl.BlockSpec((rows, HD), lambda s, n: (0, 0))
    return pl.pallas_call(
        functools.partial(attend_kernel, heads),
        out_shape=jax.ShapeDtypeStruct((qkv.shape[0], width), BF),
        grid_spec=pltpu.PrefetchScalarGridSpec(
            num_scalar_prefetch=1,
            grid=(sequences,),
            in_specs=[
                pl.BlockSpec((rows, 3 * width), lambda s, n: (s, 0)),
                whole,
                table,
                table,
            ],
            out_specs=pl.BlockSpec((rows, width), lambda s, n: (s, 0)),
        ),
        compiler_params=pltpu.CompilerParams(vmem_limit_bytes=32 << 20),
        cost_estimate=pl.CostEstimate(flops=14 * 10**9, bytes_accessed=14 << 20, transcendentals=0),
    )(lengths, qkv, gains, cosine, sine)


def attend_back(qkv, mixed_grad, lengths, gains, cosine, sine, rows, heads):
    sequences = qkv.shape[0] // rows
    width = heads * HD
    whole = pl.BlockSpec((2, HD), lambda s, n: (0, 0))
    table = pl.BlockSpec((rows, HD), lambda s, n: (0, 0))
    return pl.pallas_call(
        functools.partial(attend_back_kernel, heads),
        out_shape=(
            jax.ShapeDtypeStruct((qkv.shape[0], 3 * width), BF),
            jax.ShapeDtypeStruct((2, HD), F32),
        ),
        grid_spec=pltpu.PrefetchScalarGridSpec(
            num_scalar_prefetch=1,
            grid=(sequences,),
            in_specs=[
                pl.BlockSpec((rows, 3 * width), lambda s, n: (s, 0)),
                pl.BlockSpec((rows, width), lambda s, n: (s, 0)),
                whole,
                table,
                table,
            ],
            out_specs=(
                pl.BlockSpec((rows, 3 * width), lambda s, n: (s, 0)),
                whole,
            ),
        ),
        compiler_params=pltpu.CompilerParams(vmem_limit_bytes=32 << 20),
        cost_estimate=pl.CostEstimate(flops=20 * 10**9, bytes_accessed=20 << 20, transcendentals=0),
    )(lengths, qkv, mixed_grad, gains, cosine, sine)


def experts_kernel(sizes, places_ref, *refs):
    part, groups, rows, experts, slots, local, ff = sizes
    take = iter(refs)
    row_refs = [next(take) for _ in range(groups)]
    cot_refs = [next(take) for _ in range(groups)]
    weight_refs = [next(take) for _ in range(3)]
    if part:
        for _ in range(5):
            next(take)
    combined_refs = [next(take) for _ in range(groups)]
    back_refs = [next(take) for _ in range(groups)]
    kept_refs = [next(take) for _ in range(5)]
    (rows_v, cots_v, gate_v, up_v, down_v, sent_v, grad_v, active_v, gate_grad_v, up_grad_v) = (
        next(take) for _ in range(10)
    )
    (cot_slots_v, returned_v, sent_grad_v, rank_v, prob_v, onehot_v, gated_v, sum_v) = (
        next(take) for _ in range(8)
    )
    in_sems, weight_sems, out_sems = (next(take) for _ in range(3))
    own = row_refs[0].shape[0]
    batches = own // rows
    sequences = groups * batches
    count = sequences * slots
    first = places_ref[0]

    loads = []
    for i in range(groups):
        loads.append(pltpu.make_async_copy(row_refs[i], rows_v.at[i], in_sems.at[2 * i]))
        loads.append(pltpu.make_async_copy(cot_refs[i], cots_v.at[i], in_sems.at[2 * i + 1]))
    for copy in loads:
        copy.start()
    weight_loads = [[] for _ in range(local)]
    for j in range(local):
        for w, target in enumerate((gate_v, up_v, down_v)):
            copy = pltpu.make_async_copy(
                weight_refs[w].at[j], target.at[j], weight_sems.at[j * 3 + w]
            )
            copy.start()
            weight_loads[j].append(copy)
    for copy in loads:
        copy.wait()

    slot = lax.broadcasted_iota(jnp.int32, (slots, rows), 0).astype(F32)
    for q in range(sequences):
        i, lo = q // batches, (q % batches) * rows
        rank_v[q] = cots_v[i, lo : lo + rows, D:].astype(F32).T
        prob_v[q] = rows_v[i, lo : lo + rows, D:].astype(F32).T
        onehots, gates = [], []
        for j in range(local):
            rank = rank_v[q, pl.ds(first + j, 1), :]
            prob = (
                prob_v[q, pl.ds(first + j, 1), :]
                + prob_v[q, pl.ds(experts + first + j, 1), :]
                + prob_v[q, pl.ds(2 * experts + first + j, 1), :]
            )
            chosen = rank == slot
            gated = jnp.where(chosen, prob, 0.0)
            onehot = jnp.where(chosen, 1.0, 0.0).astype(BF)
            onehot_v[q, j * slots : (j + 1) * slots, :] = onehot
            gated_v[q, j * slots : (j + 1) * slots, :] = gated.astype(BF)
            gates.append(jnp.sum(gated, axis=1, keepdims=True))
        gate_slots = jnp.concatenate(gates, axis=0)
        onehots = onehot_v[q]

        sent = plain(onehots, rows_v[i, lo : lo + rows, :D]).astype(BF)
        cots = plain(onehots, cots_v[i, lo : lo + rows, :D])
        grads = (cots * gate_slots).astype(BF)
        cots = cots.astype(BF)
        for j in range(local):
            window = slice(j * slots, (j + 1) * slots)
            place = slice(q * slots, (q + 1) * slots)
            sent_v[j, place, :] = sent[window]
            cot_slots_v[j, place, :] = cots[window]
            grad_v[j, place, :] = grads[window]

    stores = []

    def store(index, source, j):
        target = kept_refs[index].at[j, pl.ds(part * count, count)]
        copy = pltpu.make_async_copy(source.at[j], target, out_sems.at[index * local + j])
        copy.start()
        stores.append(copy)

    for j in range(local):
        store(0, sent_v, j)
        store(1, grad_v, j)
    for j in range(local):
        for copy in weight_loads[j]:
            copy.wait()

        @pl.loop(0, ff // 512)
        def _(n):
            at = pl.ds(pl.multiple_of(n * 512, 512), 512)
            gate_hidden = plain(sent_v[j], gate_v[j, :, at])
            up_hidden = plain(sent_v[j], up_v[j, :, at])
            active_grad = times_t(grad_v[j], down_v[j, at, :])
            sigmoid = jax.nn.sigmoid(gate_hidden)
            silu = gate_hidden * sigmoid
            active_v[j, :, at] = (silu * up_hidden).astype(BF)
            gate_grad_v[j, :, at] = (
                active_grad * up_hidden * sigmoid * (1.0 + gate_hidden * (1.0 - sigmoid))
            ).astype(BF)
            up_grad_v[j, :, at] = (active_grad * silu).astype(BF)

        store(2, active_v, j)
        store(3, gate_grad_v, j)
        store(4, up_grad_v, j)

        sum_v[j] = jnp.zeros_like(sum_v[j])

        @pl.loop(0, D // 1024)
        def _(n):
            at = pl.ds(pl.multiple_of(n * 1024, 1024), 1024)
            returned = plain(active_v[j], down_v[j, :, at]).astype(BF)
            returned_v[j, :, at] = returned
            product = cot_slots_v[j, :, at].astype(F32) * returned.astype(F32)
            folded = product[:, :128]
            for m in range(1, 1024 // 128):
                folded = folded + product[:, m * 128 : (m + 1) * 128]
            sum_v[j] += folded
            sent_grad = times_t(gate_grad_v[j], gate_v[j, at, :])
            sent_grad = sent_grad + times_t(up_grad_v[j], up_v[j, at, :])
            sent_grad_v[j, :, at] = sent_grad.astype(BF)

    column = lax.broadcasted_iota(jnp.int32, (EXTRA, rows), 0)
    for q in range(sequences):
        i, lo = q // batches, (q % batches) * rows
        place = slice(q * slots, (q + 1) * slots)
        table = jnp.zeros((EXTRA, rows), F32)
        for j in range(local):
            gates_grad = jnp.sum(sum_v[j, place, :], axis=1, keepdims=True)
            onehot = onehot_v[q, j * slots : (j + 1) * slots, :].astype(F32)
            value = jnp.sum(onehot * gates_grad, axis=0, keepdims=True)
            for m in range(3):
                high = value.astype(BF).astype(F32)
                table = table + jnp.where(column == m * experts + first + j, high, 0.0)
                value = value - high
        back_refs[i][lo : lo + rows, D:] = table.T.astype(BF)
        onehots, gates = onehot_v[q], gated_v[q]

        returned = jnp.concatenate([returned_v[j, place, :] for j in range(local)], axis=0)
        sent_grad = jnp.concatenate([sent_grad_v[j, place, :] for j in range(local)], axis=0)
        combined_refs[i][lo : lo + rows, :] = inner(gates, returned).astype(BF)
        back_refs[i][lo : lo + rows, :D] = inner(onehots, sent_grad).astype(BF)

    for copy in stores:
        copy.wait()


def run_experts(
    places, row_blocks, cot_blocks, weights, kept, part, parts, experts, rows, capacity
):
    groups = len(row_blocks)
    own = row_blocks[0].shape[0]
    sequences = groups * (own // rows)
    slots = (capacity + 15) // 16 * 16
    count = sequences * slots
    local, _, ff = weights[0].shape
    any_space = pl.BlockSpec(memory_space=pl.ANY)
    in_vmem = pl.BlockSpec(memory_space=pltpu.VMEM)
    widths = (D, D, ff, ff, ff)
    operands = [*row_blocks, *cot_blocks, *weights]
    aliases = {}
    if kept is not None:
        aliases = {1 + len(operands) + i: 2 * groups + i for i in range(5)}
        operands = operands + list(kept)
    scratch = [
        pltpu.VMEM((groups, own, D + EXTRA), BF),
        pltpu.VMEM((groups, own, D + EXTRA), BF),
        *[pltpu.VMEM(w.shape, BF) for w in weights],
        *[pltpu.VMEM((local, count, w), BF) for w in widths],
        pltpu.VMEM((local, count, D), BF),
        pltpu.VMEM((local, count, D), BF),
        pltpu.VMEM((local, count, D), BF),
        pltpu.VMEM((sequences, EXTRA, rows), F32),
        pltpu.VMEM((sequences, EXTRA, rows), F32),
        pltpu.VMEM((sequences, local * slots, rows), BF),
        pltpu.VMEM((sequences, local * slots, rows), BF),
        pltpu.VMEM((local, count, 128), F32),
        pltpu.SemaphoreType.DMA((2 * groups,)),
        pltpu.SemaphoreType.DMA((3 * local,)),
        pltpu.SemaphoreType.DMA((5 * local,)),
    ]
    sizes = (part, groups, rows, experts, slots, local, ff)
    results = pl.pallas_call(
        functools.partial(experts_kernel, sizes),
        out_shape=(
            *[jax.ShapeDtypeStruct((own, D), BF)] * groups,
            *[jax.ShapeDtypeStruct((own, D + EXTRA), BF)] * groups,
            *[jax.ShapeDtypeStruct((local, parts * count, w), BF) for w in widths],
        ),
        grid_spec=pltpu.PrefetchScalarGridSpec(
            num_scalar_prefetch=1,
            in_specs=[any_space] * len(operands),
            out_specs=(*[in_vmem] * (2 * groups), *[any_space] * 5),
            scratch_shapes=scratch,
        ),
        input_output_aliases=aliases,
        compiler_params=pltpu.CompilerParams(vmem_limit_bytes=60 << 20),
        cost_estimate=pl.CostEstimate(
            flops=40 * local * count * D * ff, bytes_accessed=40 << 20, transcendentals=0
        ),
    )(places, *operands)
    return results[:groups], results[groups : 2 * groups], results[2 * groups :]


def norm_back(grad, unit, scale, gain):
    scaled = grad * gain
    values_grad = scale * (scaled - unit * jnp.mean(scaled * unit, axis=-1, keepdims=True))
    return values_grad, jnp.sum(grad * unit, axis=0)


def slot_ranks(route, priority, experts, capacity):
    rows = route.shape[0]
    expert = jnp.arange(experts, dtype=jnp.int32)
    chosen = route[:, :, None] == expert[None, None, :]
    order = jnp.sum(jnp.where(chosen, priority.reshape(rows, TOP)[:, :, None], 0), axis=1)
    routed = jnp.any(chosen, axis=1)
    order = jnp.where(routed, order, rows * TOP).T
    rank = jnp.sum((order[:, None, :] < order[:, :, None]).astype(jnp.int32), axis=2).T
    return jnp.where(routed & (rank < capacity), rank, -1)


def in_three(value):
    high = value.astype(BF)
    rest = value - high.astype(F32)
    middle = rest.astype(BF)
    low = (rest - middle.astype(F32)).astype(BF)
    return jnp.concatenate([high, middle, low], axis=-1)


def from_three(columns, count):
    return (
        columns[..., :count].astype(F32)
        + columns[..., count : 2 * count].astype(F32)
        + columns[..., 2 * count : 3 * count].astype(F32)
    )


def widen(columns, width):
    return jnp.pad(columns, ((0, 0), (0, width - columns.shape[-1])))


def shards(
    tokens,
    out_cotangent,
    lengths,
    routes,
    priority,
    attn_gain,
    query_weight,
    key_weight,
    value_weight,
    output_weight,
    query_gain,
    key_gain,
    ffn_gain,
    router_weight,
    gate_weight,
    up_weight,
    down_weight,
):
    batches, rows = tokens.shape[0], tokens.shape[2]
    own = batches * rows
    experts = router_weight.shape[1]
    capacity = 5 * rows * TOP // (4 * experts)
    local = gate_weight.shape[0]
    ys, zs, xs = lax.axis_size("y"), lax.axis_size("z"), lax.axis_size("x")
    y, c, z, x = (lax.axis_index(name) for name in ("y", "c", "z", "x"))
    shard_rows = query_weight.shape[0]
    head_shard = query_gain.shape[0]
    heads = HEADS // (2 * xs)
    width = heads * HD
    half_width = D // 2
    chunk = D // (2 * ys)

    def swap(value):
        return lax.ppermute(value, "c", [(0, 1), (1, 0)])

    def sent_along(axis, piece_for):
        at, size = lax.axis_index(axis), lax.axis_size(axis)
        return [
            shift(piece_for(jnp.mod(at + k, size)), axis, k) if k else piece_for(at)
            for k in range(size)
        ]

    token_rows = tokens.reshape(own, D)
    length = lengths.reshape(batches)
    group_keys = [(kx, kc) for kx in range(xs) for kc in range(2)]
    x_tokens = gather_blocks(token_rows, ("x",))
    held = gather_blocks(length, ("x", "c"))
    group_lengths = jnp.concatenate([held[key] for key in group_keys])
    extra = jnp.concatenate(
        [
            attn_gain[:, None],
            ffn_gain[:, None],
            router_weight,
            jnp.pad(query_gain, (0, shard_rows - head_shard))[:, None],
            jnp.pad(key_gain, (0, shard_rows - head_shard))[:, None],
        ],
        axis=1,
    )
    extra = widen(extra, EXTRA)

    def row_offset(ky, kc, kz, kx):
        sources = (came_from("y", ky), came_from("c", kc), came_from("z", kz), came_from("x", kx))
        return (
            ((sources[0] * 2 + sources[1]) * zs + sources[2]) * xs + sources[3]
        ) * shard_rows

    def half_columns(weight, core):
        return jnp.concatenate(
            [
                lax.dynamic_slice_in_dim(weight, (2 * i + core) * chunk, chunk, 1)
                for i in range(ys)
            ],
            axis=1,
        )

    def packed(core):
        halves = [half_columns(w, core) for w in (query_weight, key_weight, value_weight)]
        return jnp.stack(
            [
                jnp.concatenate(
                    [half[:, i * width : (i + 1) * width] for half in halves] + [extra], axis=1
                )
                for i in range(xs)
            ]
        )

    out_hops = [output_weight]
    for _ in range(1, zs):
        out_hops.append(shift(out_hops[-1], "z", 1))
    block = jnp.concatenate(sent_along("c", packed), axis=1)
    block = jnp.concatenate(
        sent_along("x", lambda i: lax.dynamic_index_in_dim(block, i, 0, keepdims=False)), axis=0
    )
    ZX = ("z", "x")
    ranks = jnp.concatenate(
        [
            slot_ranks(routes[b, 0], priority[b, 0], experts, capacity)
            for b in range(batches)
        ],
        axis=0,
    )
    cotangent = out_cotangent.reshape(own, D)
    cot_rows = jnp.concatenate([cotangent, widen(ranks.astype(BF), EXTRA)], axis=1)
    cot_blocks = {(0, kx): v for (kx,), v in gather_blocks(cot_rows, ("x",)).items()}
    block = tied(block, out_hops[1])
    late = list(gather_blocks(block, ("y",)).values())
    late = jnp.concatenate(tied(late, out_hops[2:3]), axis=0)
    weight_shards = tied((gate_weight, up_weight, down_weight), late)

    def offsets_of(kz):
        return [
            row_offset(ky, kc, kz, kx)
            for ky in range(ys)
            for kx in range(xs)
            for kc in range(2)
        ]

    qkv_pieces = []
    hop = late
    for kz in range(zs):
        if kz:
            hop = shift(hop, "z", 1)
            if kz == 1:
                hop, out_hops, x_tokens = lax.optimization_barrier((hop, out_hops, x_tokens))
                out_rows = jnp.concatenate(out_hops, axis=0)
                out_rows = list(gather_blocks(out_rows, ("y",)).values())
            if kz == 2:
                hop, out_rows, cot_blocks = lax.optimization_barrier((hop, out_rows, cot_blocks))
        qkv_pieces.append((hop, offsets_of(kz), 0))
    qkv_weight = place(qkv_pieces, shard_rows, (D, 3 * width + EXTRA))
    out_pieces = []
    out_rows = jnp.concatenate(out_rows, axis=0)
    for (kx,), value in gather_blocks(out_rows, ("x",)).items():
        starts = [
            ((came_from("y", ky) * zs + came_from("z", kz)) * xs + came_from("x", kx)) * shard_rows
            for ky in range(ys)
            for kz in range(zs)
        ]
        out_pieces.append((value, starts, 0))
    cot_hops = [tied(cot_rows, hop)]
    for _ in range(1, zs):
        cot_hops.append(shift(cot_hops[-1], "z", 1))
    for kz in range(1, zs):
        for (kx,), value in gather_blocks(cot_hops[kz], ("x",)).items():
            cot_blocks[(kz, kx)] = value

    weights = [
        lax.all_gather(w, ("y", "c"), axis=1, tiled=True)
        for w in weight_shards
    ]

    small = qkv_weight[:, 3 * width :].astype(F32)
    qkv_weight = qkv_weight[:, : 3 * width]
    attn_gain_f = small[:, 0][None, :]
    ffn_gain_f = small[:, 1][None, :]
    router = small[:, 2 : 2 + experts].astype(BF)
    per_device = small.reshape(-1, shard_rows, EXTRA)[:, :head_shard]
    head_gains = jnp.stack(
        [per_device[:, :, 2 + experts].reshape(HD), per_device[:, :, 3 + experts].reshape(HD)]
    )
    held = [value for kx in range(xs) for value in (x_tokens[(kx,)], swap(x_tokens[(kx,)]))]
    group_tokens = jnp.concatenate(held, axis=0)
    tokens_f = group_tokens.astype(F32)
    token_scale = lax.rsqrt(jnp.mean(tokens_f * tokens_f, axis=-1, keepdims=True) + EPSILON)
    normed = (tokens_f * token_scale * attn_gain_f).astype(BF)
    qkv = plain(normed, qkv_weight)
    qkv = tied(qkv, (cot_hops[1], [value for value, _, _ in out_pieces]))
    out_weight = place(out_pieces, shard_rows, (half_width, D))
    cosine, sine = rope_tables(rows)
    mixed = attend(qkv, group_lengths, head_gains, cosine, sine, rows, heads)
    chip_rows = 2 * own
    parts = [mixed[:chip_rows]]
    for k in range(1, xs):
        parts.append(shift(mixed[k * chip_rows : (k + 1) * chip_rows], "x", -k))
    mixed = jnp.zeros((chip_rows, half_width), BF)
    for k, part in enumerate(parts):
        place_at = jnp.mod(x + k, xs) * width
        mixed = lax.dynamic_update_slice(mixed, part, (0, place_at))
    early_swaps = [cot_blocks[(1, kx)] for kx in range(xs)]
    mixed = tied(mixed, (cot_hops[min(2, zs - 1)], early_swaps))
    partial = plain(mixed, out_weight)
    rows_f = token_rows.astype(F32)
    hidden = rows_f + (partial[:own] + swap(partial[own:]))
    hidden_scale = lax.rsqrt(jnp.mean(hidden * hidden, axis=-1, keepdims=True) + EPSILON)
    hidden_unit = hidden * hidden_scale
    routed_in = (hidden_unit * ffn_gain_f).astype(BF)
    gate_probs = jax.nn.softmax(plain(routed_in, router), axis=-1)

    routed_rows = jnp.concatenate([routed_in, widen(in_three(gate_probs), EXTRA)], axis=1)
    swaps = [[cot_blocks[(kz, kx)] for kx in range(xs)] for kz in range(zs)]
    hop = tied(routed_rows, (cot_hops[-1], swaps[: max(2, zs - 1)]))
    first_expert = ((z * xs + x) * local).astype(jnp.int32).reshape(1)
    per_call = math.gcd(xs, 2)
    back_parts, combined_parts, kept = {}, {}, None

    def call_experts(kz, swapped, kept):
        for some in range(0, xs, per_call):
            keys = [(kz, kx) for kx in range(some, some + per_call)]
            combined_part, back_part, kept = run_experts(
                first_expert,
                [swapped[(kx,)] for _, kx in keys],
                [cot_blocks[key] for key in keys],
                weights,
                kept,
                (kz * xs + some) // per_call,
                zs * xs // per_call,
                experts,
                rows,
                capacity,
            )
            back_parts.update(zip(keys, back_part, strict=True))
            combined_parts.update(zip(keys, combined_part, strict=True))
        return kept

    def moves(chain, parts, given):
        started = {}
        done = len(chain["sums"])
        if done < given:
            kz = chain["order"][done]
            total = parts[(kz, 1)]
            for kx in range(2, xs):
                total = parts[(kz, kx)].astype(F32) + shift(total.astype(BF), "x", 1).astype(F32)
            started["x"] = shift(total.astype(BF), "x", 1)
        if chain["hops"] < min(zs, done + chain["order"][0]):
            total = chain["sums"][chain["hops"] - chain["order"][0]]
            if chain["arrived"] is not None:
                total = total + chain["arrived"].astype(F32)
            started["z"] = shift(total.astype(BF), "z", 1)
        return started

    def settle(chain, parts, started):
        if "x" in started:
            kz = chain["order"][len(chain["sums"])]
            chain["sums"].append(parts[(kz, 0)].astype(F32) + started["x"].astype(F32))
        if "z" in started:
            chain["arrived"] = started["z"]
            chain["hops"] += 1

    def final(chain):
        return chain["sums"][chain["order"].index(0)] + chain["arrived"].astype(F32)

    back_chain = {"sums": [], "hops": 1, "arrived": None, "order": [*range(zs)]}
    combined_chain = {"sums": [], "hops": 1, "arrived": None, "order": [*range(1, zs), 0]}

    swapped = gather_blocks(hop, ("x",))
    hop = shift(hop, "z", 1)
    ready, hop = lax.optimization_barrier((swapped, hop))
    for kz in range(zs):
        coming = []
        if kz < zs - 1:
            coming = [gather_blocks(hop, ("x",))]
        if kz < zs - 2:
            hop = shift(hop, "z", 1)
        back_moves = moves(back_chain, back_parts, kz)
        kept = call_experts(kz, ready, kept)
        coming, hop, kept, back_moves = lax.optimization_barrier((coming, hop, kept, back_moves))
        settle(back_chain, back_parts, back_moves)
        ready = coming[0] if coming else None

    def weight_grads(left, right):
        return lax.dot_general(
            kept[left], kept[right], (((1,), (1,)), ((0,), (0,))), preferred_element_type=F32
        ).astype(BF)

    expert_grads, waiting = [], [(2, 1), (0, 3), (0, 4)]
    while back_chain["hops"] < zs:
        back_moves = moves(back_chain, back_parts, zs)
        last = back_chain["hops"] == zs - 1 and len(back_chain["sums"]) == zs
        combined_moves = moves(combined_chain, combined_parts, zs) if last else {}
        some, waiting = waiting[:1], waiting[1:]
        some = [weight_grads(*pair) for pair in some]
        some, kept, back_moves, combined_moves = lax.optimization_barrier(
            (some, kept, back_moves, combined_moves)
        )
        expert_grads += some
        settle(back_chain, back_parts, back_moves)
        settle(combined_chain, combined_parts, combined_moves)
    back = final(back_chain)

    def beside(value, others):
        parts = tied(combined_parts, others)
        started = moves(combined_chain, parts, zs)
        value, started = lax.optimization_barrier((value, started))
        settle(combined_chain, combined_parts, started)
        return value

    probs_grad = from_three(back[:, D:], experts)
    logits_grad = (
        gate_probs * (probs_grad - jnp.sum(gate_probs * probs_grad, axis=-1, keepdims=True))
    ).astype(BF)
    router_grad = inner(routed_in, logits_grad)
    routed_grad = back[:, :D] + times_t(logits_grad, router)
    hidden_add, ffn_gain_grad = norm_back(routed_grad, hidden_unit, hidden_scale, ffn_gain_f)
    hidden_grad = cotangent.astype(F32) + hidden_add
    attn_out_grad = hidden_grad.astype(BF)

    both_grads = jnp.concatenate([attn_out_grad, swap(attn_out_grad)], axis=0)
    mixed_grad = times_t(both_grads, out_weight).astype(BF)
    output_grad = inner(mixed, both_grads).astype(BF)
    mixed_grad = jnp.concatenate(
        sent_along("x", lambda i: lax.dynamic_slice_in_dim(mixed_grad, i * width, width, 1)), axis=0
    )
    qkv_grad, head_gain_grads = attend_back(
        qkv, mixed_grad, group_lengths, head_gains, cosine, sine, rows, heads
    )
    output_grad = output_grad.reshape(ys, zs, xs, shard_rows, D)
    qkv_grad = beside(qkv_grad, mixed_grad)
    normed_part = times_t(qkv_grad, qkv_weight)
    qkv_weight_grad = inner(normed, tied(qkv_grad, normed_part)).astype(BF)
    normed_sums = [
        reduce_blocks(lambda key: normed_part[(kx * 2 + key[0]) * own :][:own], ("c",)).astype(BF)
        for kx in range(xs)
    ]
    qkv_weight_grad, normed_sums = beside((qkv_weight_grad, normed_sums), qkv_grad)
    late = qkv_weight_grad.reshape(ys, 2, zs, xs, shard_rows, -1)

    def finish(normed_grad):
        token_unit = rows_f * token_scale[:own]
        tokens_add, attn_gain_grad = norm_back(
            normed_grad, token_unit, token_scale[:own], attn_gain_f
        )
        small_grad = jnp.concatenate(
            [
                attn_gain_grad[:, None],
                ffn_gain_grad[:, None],
                router_grad,
                jnp.pad(
                    head_gain_grads.reshape(2, -1, head_shard),
                    ((0, 0), (0, 0), (0, shard_rows - head_shard)),
                )
                .reshape(2, D)
                .T,
            ],
            axis=1,
        )
        small = widen(small_grad, EXTRA).astype(BF)
        return hidden_grad + tokens_add, small.reshape(ys, 2, zs, xs, shard_rows, EXTRA)

    def part_of(value, axis, dim, k):
        return lax.dynamic_index_in_dim(value, came_from(axis, k), dim, keepdims=False)

    ring = [*range(2, zs), 0]
    late_total = part_of(late, "z", 2, 1)
    output_x = output_y = output_total = None
    small_hops, output_hops = 0, 0
    for n, k in enumerate(ring):
        arrived = {"late": shift(late_total.astype(BF), "z", 1)}
        if n == 0:
            combined_parts = tied(combined_parts, late)
            arrived["combined"] = moves(combined_chain, combined_parts, zs)
            kept = tied(kept, late)
            arrived["grads"] = [weight_grads(*pair) for pair in waiting]
            arrived["normed"] = reduce_blocks(lambda key: normed_sums[key[0]], ("x",))
        if n == 1:
            arrived["x"] = reduce_axis(tied(output_grad, late_total), "x", 2).astype(BF)
        if n == 2:
            arrived["y"] = reduce_axis(output_x, "y", 0).astype(BF)
            arrived["experts"] = expert_totals
        if n >= 1:
            arrived["small"] = shift(small_total.astype(BF), "z", 1)
        arrived = lax.optimization_barrier(arrived)
        late_total = part_of(late, "z", 2, k) + arrived["late"].astype(F32)
        if n == 0:
            settle(combined_chain, combined_parts, arrived["combined"])
            expert_totals = [
                lax.psum_scatter(grad, ("y", "c"), scatter_dimension=1, tiled=True).astype(F32)
                for grad in expert_grads + arrived["grads"]
            ]
            tokens_grad, small = finish(arrived["normed"])
            small_total = part_of(small, "z", 2, 1)
        if n == 1:
            output_x = arrived["x"]
        if n == 2:
            output_y = arrived["y"]
            expert_totals = arrived["experts"]
            output_total = part_of(output_y, "z", 0, 1)
        if n >= 1:
            part = part_of(small, "z", 2, ring[small_hops])
            small_total = part + arrived["small"].astype(F32)
            small_hops += 1
    combined = final(combined_chain)
    layer_out = (hidden + combined).astype(BF)
    late = reduce_axis(late_total.astype(BF), "y", 0).astype(BF)
    arrived = [shift(small_total.astype(BF), "z", 1), shift(output_total.astype(BF), "z", 1)]
    late, arrived = lax.optimization_barrier((late, arrived))
    small = part_of(small, "z", 2, 0) + arrived[0].astype(F32)
    small = reduce_axis(small.astype(BF), "y", 0).astype(BF)
    output_total = part_of(output_y, "z", 0, ring[output_hops]) + arrived[1].astype(F32)
    output_hops += 1
    while output_hops < zs - 1:
        output_total = shift(output_total.astype(BF), "z", 1).astype(F32)
        output_total = part_of(output_y, "z", 0, ring[output_hops]) + output_total
        output_hops += 1
    output_weight_grad = output_total
    total = jnp.concatenate([late, small], axis=-1)
    columns = sent_along("x", lambda i: lax.dynamic_index_in_dim(total, i, 1, keepdims=False))
    columns = jnp.stack(columns)
    columns = sent_along("c", lambda i: lax.dynamic_index_in_dim(columns, i, 1, keepdims=False))
    small_total = sum(jnp.sum(some[:, :, 3 * width :].astype(F32), axis=0) for some in columns)

    def all_heads(at):
        halves = []
        for some in columns:
            half = jnp.zeros((shard_rows, half_width), BF)
            for k in range(xs):
                part = some[k][:, at * width : (at + 1) * width]
                half = lax.dynamic_update_slice(half, part, (0, jnp.mod(x - k, xs) * width))
            halves.append(half)
        low = jnp.where(c == 0, halves[0], halves[1]).reshape(shard_rows, ys, chunk)
        high = jnp.where(c == 0, halves[1], halves[0]).reshape(shard_rows, ys, chunk)
        return jnp.stack([low, high], axis=2).reshape(shard_rows, D).astype(F32)

    shape = (batches, 1, rows, D)
    return (
        layer_out.reshape(shape),
        tokens_grad.reshape(shape),
        small_total[:, 0],
        all_heads(0),
        all_heads(1),
        all_heads(2),
        output_weight_grad,
        small_total[:head_shard, 2 + experts],
        small_total[:head_shard, 3 + experts],
        small_total[:, 1],
        small_total[:, 2 : 2 + experts],
        expert_totals[1],
        expert_totals[2],
        expert_totals[0],
    )


def solution(mesh):
    dp, expert = mesh.shape["dp"], mesh.shape["expert"]
    zs = math.gcd(expert, 4)
    grid = Mesh(
        mesh.devices.reshape(dp // 2, 2, zs, expert // zs),
        ("y", "c", "z", "x"),
    )
    every, dps, exps = ("y", "c", "z", "x"), ("y", "c"), ("z", "x")
    in_specs = (
        P(None, every, None, None),
        P(None, every, None, None),
        P(None, every),
        P(None, every, None, None),
        P(None, every, None),
        P(every),
        P(every, None),
        P(every, None),
        P(every, None),
        P(every, None),
        P(every),
        P(every),
        P(every),
        P(every, None),
        P(exps, dps, None),
        P(exps, dps, None),
        P(exps, dps, None),
    )
    out_specs = (
        P(None, every, None, None),
        P(None, every, None, None),
        P(every),
        P(every, None),
        P(every, None),
        P(every, None),
        P(every, None),
        P(every),
        P(every),
        P(every),
        P(every, None),
        P(exps, dps, None),
        P(exps, dps, None),
        P(exps, dps, None),
    )
    return jax.shard_map(shards, mesh=grid, in_specs=in_specs, out_specs=out_specs, check_vma=False)
```

```python
import functools
import math

import jax
import jax.numpy as jnp
from jax import lax
from jax.experimental import pallas as pl
from jax.experimental.pallas import tpu as pltpu
from jax.sharding import Mesh
from jax.sharding import PartitionSpec as P

D = 2048
HEADS = 16
HD = 128
TOP = 8
EXTRA = 128

EPSILON = 1e-06
THETA = 50000.0
NEGATIVE = -1e30
BF = jnp.bfloat16
F32 = jnp.float32


def plain(left, right):
    return jnp.dot(left, right, preferred_element_type=F32)


def inner(left, right):
    return lax.dot_general(left, right, (((0,), (0,)), ((), ())), preferred_element_type=F32)


def times_t(left, right):
    return lax.dot_general(left, right, (((1,), (1,)), ((), ())), preferred_element_type=F32)


def tied(values, others):
    return lax.optimization_barrier((values, others))[0]


def ring_place(axis, at):
    return at ^ (at >> 1) if axis == "z" and lax.axis_size(axis) == 4 else at


def shift(value, axis, step):
    size = lax.axis_size(axis)
    pairs = [(ring_place(axis, i), ring_place(axis, (i + step) % size)) for i in range(size)]
    return lax.ppermute(value, axis, pairs)


def came_from(axis, k):
    at = ring_place(axis, lax.axis_index(axis))
    return ring_place(axis, jnp.mod(at - k, lax.axis_size(axis)))


def gather_blocks(block, order):
    held = {(): block}
    for axis in order:
        grown = {}
        for key, value in held.items():
            for k in range(lax.axis_size(axis)):
                if k:
                    value = shift(value, axis, 1)
                grown[key + (k,)] = value
        held = grown
    return held


def reduce_blocks(part, order):
    def reduce_from(key, depth):
        if depth == len(order):
            return part(key)
        axis = order[depth]
        size = lax.axis_size(axis)
        total = reduce_from(key + (1,), depth + 1)
        for k in [*range(2, size), 0]:
            arrived = shift(total.astype(BF), axis, 1)
            total = reduce_from(key + (k,), depth + 1).astype(F32) + arrived.astype(F32)
        return total

    return reduce_from((), 0)


def gather_pieces(block, order, merges):
    held = [(block, [()])]
    for depth, axis in enumerate(order):
        grown, level = [], held
        for k in range(lax.axis_size(axis)):
            if k:
                level = [(shift(value, axis, 1), keys) for value, keys in level]
            grown += [(value, [key + (k,) for key in keys]) for value, keys in level]
        if depth < len(merges):
            size = max(1, len(grown) // merges[depth])
            grown = [grown[i : i + size] for i in range(0, len(grown), size)]
            grown = [
                (
                    jnp.concatenate([value for value, _ in some], axis=0),
                    [key for _, keys in some for key in keys],
                )
                for some in grown
            ]
        held = grown
    return held


def reduce_axis(value, axis, dim):
    def part(k):
        return lax.dynamic_index_in_dim(value, came_from(axis, k), dim, keepdims=False)

    total = part(1)
    for k in [*range(2, lax.axis_size(axis)), 0]:
        arrived = shift(total.astype(BF), axis, 1)
        total = part(k).astype(F32) + arrived.astype(F32)
    return total


def place_kernel(plan, rows, offsets_ref, *refs):
    blocks, out, sems = refs[:-2], refs[-2], refs[-1]
    copies = []
    for i, (array, sub, column, width) in enumerate(plan):
        start = pl.multiple_of(offsets_ref[i], 16)
        copies.append(
            pltpu.make_async_copy(
                blocks[array].at[sub * rows : (sub + 1) * rows],
                out.at[pl.ds(start, rows), column : column + width],
                sems.at[i],
            )
        )
    for copy in copies:
        copy.start()
    for copy in copies:
        copy.wait()


def place(pieces, rows, shape):
    plan, offsets = [], []
    for array, (value, starts, column) in enumerate(pieces):
        for sub, start in enumerate(starts):
            plan.append((array, sub, column, value.shape[1]))
            offsets.append(start)
    return pl.pallas_call(
        functools.partial(place_kernel, plan, rows),
        out_shape=jax.ShapeDtypeStruct(shape, BF),
        grid_spec=pltpu.PrefetchScalarGridSpec(
            num_scalar_prefetch=1,
            in_specs=[pl.BlockSpec(memory_space=pl.ANY)] * len(pieces),
            out_specs=pl.BlockSpec(memory_space=pltpu.VMEM),
            scratch_shapes=[pltpu.SemaphoreType.DMA((len(plan),))],
        ),
        compiler_params=pltpu.CompilerParams(vmem_limit_bytes=24 << 20),
    )(jnp.stack(offsets).astype(jnp.int32), *[value for value, _, _ in pieces])


def rope_tables(row_count):
    half = HD // 2
    frequency = THETA ** (-jnp.arange(half, dtype=F32) / half)
    angles = jnp.arange(row_count, dtype=F32)[:, None] * frequency[None, :]
    cosine, sine = jnp.cos(angles), jnp.sin(angles)
    return jnp.concatenate([cosine, cosine], axis=1), jnp.concatenate([-sine, sine], axis=1)


def head_forward(raw, gain, cosine, sine):
    scale = lax.rsqrt(jnp.mean(raw * raw, axis=-1, keepdims=True) + EPSILON)
    unit = raw * scale
    value = unit * gain
    turned = value * cosine + pltpu.roll(value, HD // 2, 1) * sine
    return unit, scale, turned.astype(BF)


def head_backward(grad, unit, scale, gain, cosine, sine):
    grad = grad * cosine - pltpu.roll(grad, HD // 2, 1) * sine
    gain_grad = jnp.sum(grad * unit, axis=0, keepdims=True)
    grad = grad * gain
    grad = scale * (grad - unit * jnp.mean(grad * unit, axis=-1, keepdims=True))
    return grad.astype(BF), gain_grad


def attention_of(query, key, length):
    scores = times_t(query, key) * (1.0 / math.sqrt(HD))
    valid = lax.broadcasted_iota(jnp.int32, scores.shape, 1) < length
    scores = jnp.where(valid, scores, NEGATIVE)
    weight = jnp.exp(scores - jnp.max(scores, axis=-1, keepdims=True))
    return weight / jnp.sum(weight, axis=-1, keepdims=True)


def attend_kernel(heads, lengths_ref, qkv_ref, gains_ref, cosine_ref, sine_ref, mixed_ref):
    length = lengths_ref[pl.program_id(0)]
    cosine, sine = cosine_ref[...], sine_ref[...]
    query_gain, key_gain = gains_ref[0:1, :], gains_ref[1:2, :]
    width = heads * HD
    for h in range(heads):
        lo = h * HD
        query = head_forward(qkv_ref[:, lo : lo + HD], query_gain, cosine, sine)[2]
        key = head_forward(qkv_ref[:, width + lo : width + lo + HD], key_gain, cosine, sine)[2]
        value = qkv_ref[:, 2 * width + lo : 2 * width + lo + HD].astype(BF)
        attention = attention_of(query, key, length)
        mixed_ref[:, lo : lo + HD] = plain(attention.astype(BF), value).astype(BF)


def attend_back_kernel(
    heads, lengths_ref, qkv_ref, mixed_grad_ref, gains_ref, cosine_ref, sine_ref, out_ref, gain_ref
):
    @pl.when(pl.program_id(0) == 0)
    def _():
        gain_ref[...] = jnp.zeros_like(gain_ref)

    length = lengths_ref[pl.program_id(0)]
    cosine, sine = cosine_ref[...], sine_ref[...]
    query_gain, key_gain = gains_ref[0:1, :], gains_ref[1:2, :]
    width = heads * HD
    score_scale = 1.0 / math.sqrt(HD)
    for h in range(heads):
        lo = h * HD
        query_unit, query_scale, query = head_forward(
            qkv_ref[:, lo : lo + HD], query_gain, cosine, sine
        )
        key_unit, key_scale, key = head_forward(
            qkv_ref[:, width + lo : width + lo + HD], key_gain, cosine, sine
        )
        value = qkv_ref[:, 2 * width + lo : 2 * width + lo + HD].astype(BF)
        attention = attention_of(query, key, length)
        mixed_grad = mixed_grad_ref[:, lo : lo + HD]
        value_grad = inner(attention.astype(BF), mixed_grad)
        attention_grad = times_t(mixed_grad, value)
        score_grad = attention * (
            attention_grad - jnp.sum(attention * attention_grad, axis=-1, keepdims=True)
        )
        score_grad = score_grad.astype(BF)
        query_grad, query_gain_grad = head_backward(
            plain(score_grad, key) * score_scale, query_unit, query_scale, query_gain, cosine, sine
        )
        key_grad, key_gain_grad = head_backward(
            inner(score_grad, query) * score_scale, key_unit, key_scale, key_gain, cosine, sine
        )
        out_ref[:, lo : lo + HD] = query_grad
        out_ref[:, width + lo : width + lo + HD] = key_grad
        out_ref[:, 2 * width + lo : 2 * width + lo + HD] = value_grad.astype(BF)
        gain_ref[0:1, :] += query_gain_grad
        gain_ref[1:2, :] += key_gain_grad


def attend(qkv, lengths, gains, cosine, sine, rows, heads):
    sequences = qkv.shape[0] // rows
    width = heads * HD
    whole = pl.BlockSpec((2, HD), lambda s, n: (0, 0))
    table = pl.BlockSpec((rows, HD), lambda s, n: (0, 0))
    return pl.pallas_call(
        functools.partial(attend_kernel, heads),
        out_shape=jax.ShapeDtypeStruct((qkv.shape[0], width), BF),
        grid_spec=pltpu.PrefetchScalarGridSpec(
            num_scalar_prefetch=1,
            grid=(sequences,),
            in_specs=[
                pl.BlockSpec((rows, 3 * width), lambda s, n: (s, 0)),
                whole,
                table,
                table,
            ],
            out_specs=pl.BlockSpec((rows, width), lambda s, n: (s, 0)),
        ),
        compiler_params=pltpu.CompilerParams(vmem_limit_bytes=32 << 20),
        cost_estimate=pl.CostEstimate(flops=14 * 10**9, bytes_accessed=14 << 20, transcendentals=0),
    )(lengths, qkv, gains, cosine, sine)


def attend_back(qkv, mixed_grad, lengths, gains, cosine, sine, rows, heads):
    sequences = qkv.shape[0] // rows
    width = heads * HD
    whole = pl.BlockSpec((2, HD), lambda s, n: (0, 0))
    table = pl.BlockSpec((rows, HD), lambda s, n: (0, 0))
    return pl.pallas_call(
        functools.partial(attend_back_kernel, heads),
        out_shape=(
            jax.ShapeDtypeStruct((qkv.shape[0], 3 * width), BF),
            jax.ShapeDtypeStruct((2, HD), F32),
        ),
        grid_spec=pltpu.PrefetchScalarGridSpec(
            num_scalar_prefetch=1,
            grid=(sequences,),
            in_specs=[
                pl.BlockSpec((rows, 3 * width), lambda s, n: (s, 0)),
                pl.BlockSpec((rows, width), lambda s, n: (s, 0)),
                whole,
                table,
                table,
            ],
            out_specs=(
                pl.BlockSpec((rows, 3 * width), lambda s, n: (s, 0)),
                whole,
            ),
        ),
        compiler_params=pltpu.CompilerParams(vmem_limit_bytes=32 << 20),
        cost_estimate=pl.CostEstimate(flops=20 * 10**9, bytes_accessed=20 << 20, transcendentals=0),
    )(lengths, qkv, mixed_grad, gains, cosine, sine)


def experts_kernel(sizes, places_ref, *refs):
    part, groups, rows, experts, slots, local, ff = sizes
    take = iter(refs)
    row_refs = [next(take) for _ in range(groups)]
    cot_refs = [next(take) for _ in range(groups)]
    weight_refs = [next(take) for _ in range(3)]
    if part:
        for _ in range(5):
            next(take)
    combined_refs = [next(take) for _ in range(groups)]
    back_refs = [next(take) for _ in range(groups)]
    kept_refs = [next(take) for _ in range(5)]
    (rows_v, cots_v, gate_v, up_v, down_v, sent_v, grad_v, active_v, gate_grad_v, up_grad_v) = (
        next(take) for _ in range(10)
    )
    (cot_slots_v, returned_v, sent_grad_v, rank_v, prob_v, onehot_v, gated_v, sum_v) = (
        next(take) for _ in range(8)
    )
    in_sems, weight_sems, out_sems = (next(take) for _ in range(3))
    own = row_refs[0].shape[0]
    batches = own // rows
    sequences = groups * batches
    count = sequences * slots
    first = places_ref[0]

    loads = []
    for i in range(groups):
        loads.append(pltpu.make_async_copy(row_refs[i], rows_v.at[i], in_sems.at[2 * i]))
        loads.append(pltpu.make_async_copy(cot_refs[i], cots_v.at[i], in_sems.at[2 * i + 1]))
    for copy in loads:
        copy.start()
    weight_loads = [[] for _ in range(local)]
    for j in range(local):
        for w, target in enumerate((gate_v, up_v, down_v)):
            copy = pltpu.make_async_copy(
                weight_refs[w].at[j], target.at[j], weight_sems.at[j * 3 + w]
            )
            copy.start()
            weight_loads[j].append(copy)
    for copy in loads:
        copy.wait()

    slot = lax.broadcasted_iota(jnp.int32, (slots, rows), 0).astype(F32)
    for q in range(sequences):
        i, lo = q // batches, (q % batches) * rows
        rank_v[q] = cots_v[i, lo : lo + rows, D:].astype(F32).T
        prob_v[q] = rows_v[i, lo : lo + rows, D:].astype(F32).T
        onehots, gates = [], []
        for j in range(local):
            rank = rank_v[q, pl.ds(first + j, 1), :]
            prob = (
                prob_v[q, pl.ds(first + j, 1), :]
                + prob_v[q, pl.ds(experts + first + j, 1), :]
                + prob_v[q, pl.ds(2 * experts + first + j, 1), :]
            )
            chosen = rank == slot
            gated = jnp.where(chosen, prob, 0.0)
            onehot = jnp.where(chosen, 1.0, 0.0).astype(BF)
            onehot_v[q, j * slots : (j + 1) * slots, :] = onehot
            gated_v[q, j * slots : (j + 1) * slots, :] = gated.astype(BF)
            gates.append(jnp.sum(gated, axis=1, keepdims=True))
        gate_slots = jnp.concatenate(gates, axis=0)
        onehots = onehot_v[q]

        sent = plain(onehots, rows_v[i, lo : lo + rows, :D]).astype(BF)
        cots = plain(onehots, cots_v[i, lo : lo + rows, :D])
        grads = (cots * gate_slots).astype(BF)
        cots = cots.astype(BF)
        for j in range(local):
            window = slice(j * slots, (j + 1) * slots)
            place = slice(q * slots, (q + 1) * slots)
            sent_v[j, place, :] = sent[window]
            cot_slots_v[j, place, :] = cots[window]
            grad_v[j, place, :] = grads[window]

    stores = []

    def store(index, source, j):
        target = kept_refs[index].at[j, pl.ds(part * count, count)]
        copy = pltpu.make_async_copy(source.at[j], target, out_sems.at[index * local + j])
        copy.start()
        stores.append(copy)

    for j in range(local):
        store(0, sent_v, j)
        store(1, grad_v, j)
    for j in range(local):
        for copy in weight_loads[j]:
            copy.wait()

        @pl.loop(0, ff // 512)
        def _(n):
            at = pl.ds(pl.multiple_of(n * 512, 512), 512)
            gate_hidden = plain(sent_v[j], gate_v[j, :, at])
            up_hidden = plain(sent_v[j], up_v[j, :, at])
            active_grad = times_t(grad_v[j], down_v[j, at, :])
            sigmoid = jax.nn.sigmoid(gate_hidden)
            silu = gate_hidden * sigmoid
            active_v[j, :, at] = (silu * up_hidden).astype(BF)
            gate_grad_v[j, :, at] = (
                active_grad * up_hidden * sigmoid * (1.0 + gate_hidden * (1.0 - sigmoid))
            ).astype(BF)
            up_grad_v[j, :, at] = (active_grad * silu).astype(BF)

        store(2, active_v, j)
        store(3, gate_grad_v, j)
        store(4, up_grad_v, j)

        sum_v[j] = jnp.zeros_like(sum_v[j])

        @pl.loop(0, D // 1024)
        def _(n):
            at = pl.ds(pl.multiple_of(n * 1024, 1024), 1024)
            returned = plain(active_v[j], down_v[j, :, at]).astype(BF)
            returned_v[j, :, at] = returned
            product = cot_slots_v[j, :, at].astype(F32) * returned.astype(F32)
            folded = product[:, :128]
            for m in range(1, 1024 // 128):
                folded = folded + product[:, m * 128 : (m + 1) * 128]
            sum_v[j] += folded
            sent_grad = times_t(gate_grad_v[j], gate_v[j, at, :])
            sent_grad = sent_grad + times_t(up_grad_v[j], up_v[j, at, :])
            sent_grad_v[j, :, at] = sent_grad.astype(BF)

    column = lax.broadcasted_iota(jnp.int32, (EXTRA, rows), 0)
    for q in range(sequences):
        i, lo = q // batches, (q % batches) * rows
        place = slice(q * slots, (q + 1) * slots)
        table = jnp.zeros((EXTRA, rows), F32)
        for j in range(local):
            gates_grad = jnp.sum(sum_v[j, place, :], axis=1, keepdims=True)
            onehot = onehot_v[q, j * slots : (j + 1) * slots, :].astype(F32)
            value = jnp.sum(onehot * gates_grad, axis=0, keepdims=True)
            for m in range(3):
                high = value.astype(BF).astype(F32)
                table = table + jnp.where(column == m * experts + first + j, high, 0.0)
                value = value - high
        back_refs[i][lo : lo + rows, D:] = table.T.astype(BF)
        onehots, gates = onehot_v[q], gated_v[q]

        returned = jnp.concatenate([returned_v[j, place, :] for j in range(local)], axis=0)
        sent_grad = jnp.concatenate([sent_grad_v[j, place, :] for j in range(local)], axis=0)
        combined_refs[i][lo : lo + rows, :] = inner(gates, returned).astype(BF)
        back_refs[i][lo : lo + rows, :D] = inner(onehots, sent_grad).astype(BF)

    for copy in stores:
        copy.wait()


def run_experts(
    places, row_blocks, cot_blocks, weights, kept, part, parts, experts, rows, capacity
):
    groups = len(row_blocks)
    own = row_blocks[0].shape[0]
    sequences = groups * (own // rows)
    slots = (capacity + 15) // 16 * 16
    count = sequences * slots
    local, _, ff = weights[0].shape
    any_space = pl.BlockSpec(memory_space=pl.ANY)
    in_vmem = pl.BlockSpec(memory_space=pltpu.VMEM)
    widths = (D, D, ff, ff, ff)
    operands = [*row_blocks, *cot_blocks, *weights]
    aliases = {}
    if kept is not None:
        aliases = {1 + len(operands) + i: 2 * groups + i for i in range(5)}
        operands = operands + list(kept)
    scratch = [
        pltpu.VMEM((groups, own, D + EXTRA), BF),
        pltpu.VMEM((groups, own, D + EXTRA), BF),
        *[pltpu.VMEM(w.shape, BF) for w in weights],
        *[pltpu.VMEM((local, count, w), BF) for w in widths],
        pltpu.VMEM((local, count, D), BF),
        pltpu.VMEM((local, count, D), BF),
        pltpu.VMEM((local, count, D), BF),
        pltpu.VMEM((sequences, EXTRA, rows), F32),
        pltpu.VMEM((sequences, EXTRA, rows), F32),
        pltpu.VMEM((sequences, local * slots, rows), BF),
        pltpu.VMEM((sequences, local * slots, rows), BF),
        pltpu.VMEM((local, count, 128), F32),
        pltpu.SemaphoreType.DMA((2 * groups,)),
        pltpu.SemaphoreType.DMA((3 * local,)),
        pltpu.SemaphoreType.DMA((5 * local,)),
    ]
    sizes = (part, groups, rows, experts, slots, local, ff)
    results = pl.pallas_call(
        functools.partial(experts_kernel, sizes),
        out_shape=(
            *[jax.ShapeDtypeStruct((own, D), BF)] * groups,
            *[jax.ShapeDtypeStruct((own, D + EXTRA), BF)] * groups,
            *[jax.ShapeDtypeStruct((local, parts * count, w), BF) for w in widths],
        ),
        grid_spec=pltpu.PrefetchScalarGridSpec(
            num_scalar_prefetch=1,
            in_specs=[any_space] * len(operands),
            out_specs=(*[in_vmem] * (2 * groups), *[any_space] * 5),
            scratch_shapes=scratch,
        ),
        input_output_aliases=aliases,
        compiler_params=pltpu.CompilerParams(vmem_limit_bytes=60 << 20),
        cost_estimate=pl.CostEstimate(
            flops=40 * local * count * D * ff, bytes_accessed=40 << 20, transcendentals=0
        ),
    )(places, *operands)
    return results[:groups], results[groups : 2 * groups], results[2 * groups :]


def norm_back(grad, unit, scale, gain):
    scaled = grad * gain
    values_grad = scale * (scaled - unit * jnp.mean(scaled * unit, axis=-1, keepdims=True))
    return values_grad, jnp.sum(grad * unit, axis=0)


def slot_ranks(route, priority, experts, capacity):
    rows = route.shape[0]
    expert = jnp.arange(experts, dtype=jnp.int32)
    chosen = route[:, :, None] == expert[None, None, :]
    order = jnp.sum(jnp.where(chosen, priority.reshape(rows, TOP)[:, :, None], 0), axis=1)
    routed = jnp.any(chosen, axis=1)
    order = jnp.where(routed, order, rows * TOP).T
    rank = jnp.sum((order[:, None, :] < order[:, :, None]).astype(jnp.int32), axis=2).T
    return jnp.where(routed & (rank < capacity), rank, -1)


def in_three(value):
    high = value.astype(BF)
    rest = value - high.astype(F32)
    middle = rest.astype(BF)
    low = (rest - middle.astype(F32)).astype(BF)
    return jnp.concatenate([high, middle, low], axis=-1)


def from_three(columns, count):
    return (
        columns[..., :count].astype(F32)
        + columns[..., count : 2 * count].astype(F32)
        + columns[..., 2 * count : 3 * count].astype(F32)
    )


def widen(columns, width):
    return jnp.pad(columns, ((0, 0), (0, width - columns.shape[-1])))


def shards(
    tokens,
    out_cotangent,
    lengths,
    routes,
    priority,
    attn_gain,
    query_weight,
    key_weight,
    value_weight,
    output_weight,
    query_gain,
    key_gain,
    ffn_gain,
    router_weight,
    gate_weight,
    up_weight,
    down_weight,
):
    batches, rows = tokens.shape[0], tokens.shape[2]
    own = batches * rows
    experts = router_weight.shape[1]
    capacity = 5 * rows * TOP // (4 * experts)
    local = gate_weight.shape[0]
    ys, zs, xs = lax.axis_size("y"), lax.axis_size("z"), lax.axis_size("x")
    y, c, z, x = (lax.axis_index(name) for name in ("y", "c", "z", "x"))
    shard_rows = query_weight.shape[0]
    head_shard = query_gain.shape[0]
    heads = HEADS // (2 * xs)
    width = heads * HD
    half_width = D // 2
    chunk = D // (2 * ys)

    def swap(value):
        return lax.ppermute(value, "c", [(0, 1), (1, 0)])

    def sent_along(axis, piece_for):
        at, size = lax.axis_index(axis), lax.axis_size(axis)
        return [
            shift(piece_for(jnp.mod(at + k, size)), axis, k) if k else piece_for(at)
            for k in range(size)
        ]

    token_rows = tokens.reshape(own, D)
    length = lengths.reshape(batches)
    group_keys = [(kx, kc) for kx in range(xs) for kc in range(2)]
    x_tokens = gather_blocks(token_rows, ("x",))
    held = gather_blocks(length, ("x", "c"))
    group_lengths = jnp.concatenate([held[key] for key in group_keys])
    extra = jnp.concatenate(
        [
            attn_gain[:, None],
            ffn_gain[:, None],
            router_weight,
            jnp.pad(query_gain, (0, shard_rows - head_shard))[:, None],
            jnp.pad(key_gain, (0, shard_rows - head_shard))[:, None],
        ],
        axis=1,
    )
    extra = widen(extra, EXTRA)

    def row_offset(ky, kc, kz, kx):
        sources = (came_from("y", ky), came_from("c", kc), came_from("z", kz), came_from("x", kx))
        return (
            ((sources[0] * 2 + sources[1]) * zs + sources[2]) * xs + sources[3]
        ) * shard_rows

    def half_columns(weight, core):
        return jnp.concatenate(
            [
                lax.dynamic_slice_in_dim(weight, (2 * i + core) * chunk, chunk, 1)
                for i in range(ys)
            ],
            axis=1,
        )

    def packed(core):
        halves = [half_columns(w, core) for w in (query_weight, key_weight, value_weight)]
        return jnp.stack(
            [
                jnp.concatenate(
                    [half[:, i * width : (i + 1) * width] for half in halves] + [extra], axis=1
                )
                for i in range(xs)
            ]
        )

    out_hops = [output_weight]
    for _ in range(1, zs):
        out_hops.append(shift(out_hops[-1], "z", 1))
    block = jnp.concatenate(sent_along("c", packed), axis=1)
    block = jnp.concatenate(
        sent_along("x", lambda i: lax.dynamic_index_in_dim(block, i, 0, keepdims=False)), axis=0
    )
    ZX = ("z", "x")
    ranks = jnp.concatenate(
        [
            slot_ranks(routes[b, 0], priority[b, 0], experts, capacity)
            for b in range(batches)
        ],
        axis=0,
    )
    cotangent = out_cotangent.reshape(own, D)
    cot_rows = jnp.concatenate([cotangent, widen(ranks.astype(BF), EXTRA)], axis=1)
    cot_blocks = {(0, kx): v for (kx,), v in gather_blocks(cot_rows, ("x",)).items()}
    block = tied(block, out_hops[1])
    late = list(gather_blocks(block, ("y",)).values())
    late = jnp.concatenate(tied(late, out_hops[2:3]), axis=0)
    weight_shards = tied((gate_weight, up_weight, down_weight), late)

    def offsets_of(kz):
        return [
            row_offset(ky, kc, kz, kx)
            for ky in range(ys)
            for kx in range(xs)
            for kc in range(2)
        ]

    qkv_pieces = []
    hop = late
    for kz in range(zs):
        if kz:
            hop = shift(hop, "z", 1)
            if kz == 1:
                hop, out_hops, x_tokens = lax.optimization_barrier((hop, out_hops, x_tokens))
                out_rows = jnp.concatenate(out_hops, axis=0)
                out_rows = list(gather_blocks(out_rows, ("y",)).values())
            if kz == 2:
                hop, out_rows, cot_blocks = lax.optimization_barrier((hop, out_rows, cot_blocks))
        qkv_pieces.append((hop, offsets_of(kz), 0))
    qkv_weight = place(qkv_pieces, shard_rows, (D, 3 * width + EXTRA))
    out_pieces = []
    out_rows = jnp.concatenate(out_rows, axis=0)
    for (kx,), value in gather_blocks(out_rows, ("x",)).items():
        starts = [
            ((came_from("y", ky) * zs + came_from("z", kz)) * xs + came_from("x", kx)) * shard_rows
            for ky in range(ys)
            for kz in range(zs)
        ]
        out_pieces.append((value, starts, 0))
    cot_hops = [tied(cot_rows, hop)]
    for _ in range(1, zs):
        cot_hops.append(shift(cot_hops[-1], "z", 1))
    for kz in range(1, zs):
        for (kx,), value in gather_blocks(cot_hops[kz], ("x",)).items():
            cot_blocks[(kz, kx)] = value

    weights = [
        lax.all_gather(w, ("y", "c"), axis=1, tiled=True)
        for w in weight_shards
    ]

    small = qkv_weight[:, 3 * width :].astype(F32)
    qkv_weight = qkv_weight[:, : 3 * width]
    attn_gain_f = small[:, 0][None, :]
    ffn_gain_f = small[:, 1][None, :]
    router = small[:, 2 : 2 + experts].astype(BF)
    per_device = small.reshape(-1, shard_rows, EXTRA)[:, :head_shard]
    head_gains = jnp.stack(
        [per_device[:, :, 2 + experts].reshape(HD), per_device[:, :, 3 + experts].reshape(HD)]
    )
    held = [value for kx in range(xs) for value in (x_tokens[(kx,)], swap(x_tokens[(kx,)]))]
    group_tokens = jnp.concatenate(held, axis=0)
    tokens_f = group_tokens.astype(F32)
    token_scale = lax.rsqrt(jnp.mean(tokens_f * tokens_f, axis=-1, keepdims=True) + EPSILON)
    normed = (tokens_f * token_scale * attn_gain_f).astype(BF)
    qkv = plain(normed, qkv_weight)
    qkv = tied(qkv, (cot_hops[1], [value for value, _, _ in out_pieces]))
    out_weight = place(out_pieces, shard_rows, (half_width, D))
    cosine, sine = rope_tables(rows)
    mixed = attend(qkv, group_lengths, head_gains, cosine, sine, rows, heads)
    chip_rows = 2 * own
    parts = [mixed[:chip_rows]]
    for k in range(1, xs):
        parts.append(shift(mixed[k * chip_rows : (k + 1) * chip_rows], "x", -k))
    mixed = jnp.zeros((chip_rows, half_width), BF)
    for k, part in enumerate(parts):
        place_at = jnp.mod(x + k, xs) * width
        mixed = lax.dynamic_update_slice(mixed, part, (0, place_at))
    early_swaps = [cot_blocks[(1, kx)] for kx in range(xs)]
    mixed = tied(mixed, (cot_hops[min(2, zs - 1)], early_swaps))
    partial = plain(mixed, out_weight)
    rows_f = token_rows.astype(F32)
    hidden = rows_f + (partial[:own] + swap(partial[own:]))
    hidden_scale = lax.rsqrt(jnp.mean(hidden * hidden, axis=-1, keepdims=True) + EPSILON)
    hidden_unit = hidden * hidden_scale
    routed_in = (hidden_unit * ffn_gain_f).astype(BF)
    gate_probs = jax.nn.softmax(plain(routed_in, router), axis=-1)

    routed_rows = jnp.concatenate([routed_in, widen(in_three(gate_probs), EXTRA)], axis=1)
    swaps = [[cot_blocks[(kz, kx)] for kx in range(xs)] for kz in range(zs)]
    hop = tied(routed_rows, (cot_hops[-1], swaps[: max(2, zs - 1)]))
    first_expert = ((z * xs + x) * local).astype(jnp.int32).reshape(1)
    per_call = math.gcd(xs, 2)
    back_parts, combined_parts, kept = {}, {}, None

    def call_experts(kz, swapped, kept):
        for some in range(0, xs, per_call):
            keys = [(kz, kx) for kx in range(some, some + per_call)]
            combined_part, back_part, kept = run_experts(
                first_expert,
                [swapped[(kx,)] for _, kx in keys],
                [cot_blocks[key] for key in keys],
                weights,
                kept,
                (kz * xs + some) // per_call,
                zs * xs // per_call,
                experts,
                rows,
                capacity,
            )
            back_parts.update(zip(keys, back_part, strict=True))
            combined_parts.update(zip(keys, combined_part, strict=True))
        return kept

    def moves(chain, parts, given):
        started = {}
        done = len(chain["sums"])
        if done < given:
            kz = chain["order"][done]
            total = parts[(kz, 1)]
            for kx in range(2, xs):
                total = parts[(kz, kx)].astype(F32) + shift(total.astype(BF), "x", 1).astype(F32)
            started["x"] = shift(total.astype(BF), "x", 1)
        if chain["hops"] < min(zs, done + chain["order"][0]):
            total = chain["sums"][chain["hops"] - chain["order"][0]]
            if chain["arrived"] is not None:
                total = total + chain["arrived"].astype(F32)
            started["z"] = shift(total.astype(BF), "z", 1)
        return started

    def settle(chain, parts, started):
        if "x" in started:
            kz = chain["order"][len(chain["sums"])]
            chain["sums"].append(parts[(kz, 0)].astype(F32) + started["x"].astype(F32))
        if "z" in started:
            chain["arrived"] = started["z"]
            chain["hops"] += 1

    def final(chain):
        return chain["sums"][chain["order"].index(0)] + chain["arrived"].astype(F32)

    back_chain = {"sums": [], "hops": 1, "arrived": None, "order": [*range(zs)]}
    combined_chain = {"sums": [], "hops": 1, "arrived": None, "order": [*range(1, zs), 0]}

    swapped = gather_blocks(hop, ("x",))
    hop = shift(hop, "z", 1)
    ready, hop = lax.optimization_barrier((swapped, hop))
    for kz in range(zs):
        coming = []
        if kz < zs - 1:
            coming = [gather_blocks(hop, ("x",))]
        if kz < zs - 2:
            hop = shift(hop, "z", 1)
        back_moves = moves(back_chain, back_parts, kz)
        kept = call_experts(kz, ready, kept)
        coming, hop, kept, back_moves = lax.optimization_barrier((coming, hop, kept, back_moves))
        settle(back_chain, back_parts, back_moves)
        ready = coming[0] if coming else None

    def weight_grads(left, right):
        return lax.dot_general(
            kept[left], kept[right], (((1,), (1,)), ((0,), (0,))), preferred_element_type=F32
        ).astype(BF)

    expert_grads, waiting = [], [(2, 1), (0, 3), (0, 4)]
    while back_chain["hops"] < zs:
        back_moves = moves(back_chain, back_parts, zs)
        last = back_chain["hops"] == zs - 1 and len(back_chain["sums"]) == zs
        combined_moves = moves(combined_chain, combined_parts, zs) if last else {}
        some, waiting = waiting[:1], waiting[1:]
        some = [weight_grads(*pair) for pair in some]
        some, kept, back_moves, combined_moves = lax.optimization_barrier(
            (some, kept, back_moves, combined_moves)
        )
        expert_grads += some
        settle(back_chain, back_parts, back_moves)
        settle(combined_chain, combined_parts, combined_moves)
    back = final(back_chain)

    def beside(value, others):
        parts = tied(combined_parts, others)
        started = moves(combined_chain, parts, zs)
        value, started = lax.optimization_barrier((value, started))
        settle(combined_chain, combined_parts, started)
        return value

    probs_grad = from_three(back[:, D:], experts)
    logits_grad = (
        gate_probs * (probs_grad - jnp.sum(gate_probs * probs_grad, axis=-1, keepdims=True))
    ).astype(BF)
    router_grad = inner(routed_in, logits_grad)
    routed_grad = back[:, :D] + times_t(logits_grad, router)
    hidden_add, ffn_gain_grad = norm_back(routed_grad, hidden_unit, hidden_scale, ffn_gain_f)
    hidden_grad = cotangent.astype(F32) + hidden_add
    attn_out_grad = hidden_grad.astype(BF)

    both_grads = jnp.concatenate([attn_out_grad, swap(attn_out_grad)], axis=0)
    mixed_grad = times_t(both_grads, out_weight).astype(BF)
    output_grad = inner(mixed, both_grads).astype(BF)
    mixed_grad = jnp.concatenate(
        sent_along("x", lambda i: lax.dynamic_slice_in_dim(mixed_grad, i * width, width, 1)), axis=0
    )
    qkv_grad, head_gain_grads = attend_back(
        qkv, mixed_grad, group_lengths, head_gains, cosine, sine, rows, heads
    )
    output_grad = output_grad.reshape(ys, zs, xs, shard_rows, D)
    qkv_grad = beside(qkv_grad, mixed_grad)
    normed_part = times_t(qkv_grad, qkv_weight)
    qkv_weight_grad = inner(normed, tied(qkv_grad, normed_part)).astype(BF)
    normed_sums = [
        reduce_blocks(lambda key: normed_part[(kx * 2 + key[0]) * own :][:own], ("c",)).astype(BF)
        for kx in range(xs)
    ]
    qkv_weight_grad, normed_sums = beside((qkv_weight_grad, normed_sums), qkv_grad)
    late = qkv_weight_grad.reshape(ys, 2, zs, xs, shard_rows, -1)

    def finish(normed_grad):
        token_unit = rows_f * token_scale[:own]
        tokens_add, attn_gain_grad = norm_back(
            normed_grad, token_unit, token_scale[:own], attn_gain_f
        )
        small_grad = jnp.concatenate(
            [
                attn_gain_grad[:, None],
                ffn_gain_grad[:, None],
                router_grad,
                jnp.pad(
                    head_gain_grads.reshape(2, -1, head_shard),
                    ((0, 0), (0, 0), (0, shard_rows - head_shard)),
                )
                .reshape(2, D)
                .T,
            ],
            axis=1,
        )
        small = widen(small_grad, EXTRA).astype(BF)
        return hidden_grad + tokens_add, small.reshape(ys, 2, zs, xs, shard_rows, EXTRA)

    def part_of(value, axis, dim, k):
        return lax.dynamic_index_in_dim(value, came_from(axis, k), dim, keepdims=False)

    ring = [*range(2, zs), 0]
    late_total = part_of(late, "z", 2, 1)
    output_x = output_y = output_total = None
    small_hops, output_hops = 0, 0
    for n, k in enumerate(ring):
        arrived = {"late": shift(late_total.astype(BF), "z", 1)}
        if n == 0:
            combined_parts = tied(combined_parts, late)
            arrived["combined"] = moves(combined_chain, combined_parts, zs)
            kept = tied(kept, late)
            arrived["grads"] = [weight_grads(*pair) for pair in waiting]
            arrived["normed"] = reduce_blocks(lambda key: normed_sums[key[0]], ("x",))
        if n == 1:
            arrived["x"] = reduce_axis(tied(output_grad, late_total), "x", 2).astype(BF)
            arrived["experts"] = expert_totals[:2]
        if n == 2:
            arrived["y"] = reduce_axis(output_x, "y", 0).astype(BF)
        if n >= 1:
            arrived["small"] = shift(small_total.astype(BF), "z", 1)
        arrived = lax.optimization_barrier(arrived)
        late_total = part_of(late, "z", 2, k) + arrived["late"].astype(F32)
        if n == 0:
            settle(combined_chain, combined_parts, arrived["combined"])
            expert_totals = [
                lax.psum_scatter(grad, ("y", "c"), scatter_dimension=1, tiled=True).astype(F32)
                for grad in expert_grads + arrived["grads"]
            ]
            tokens_grad, small = finish(arrived["normed"])
            small_total = part_of(small, "z", 2, 1)
        if n == 1:
            output_x = arrived["x"]
            expert_totals[:2] = arrived["experts"]
        if n == 2:
            output_y = arrived["y"]
            output_total = part_of(output_y, "z", 0, 1)
        if n >= 1:
            part = part_of(small, "z", 2, ring[small_hops])
            small_total = part + arrived["small"].astype(F32)
            small_hops += 1
    combined = final(combined_chain)
    layer_out = (hidden + combined).astype(BF)
    late = reduce_axis(late_total.astype(BF), "y", 0).astype(BF)
    arrived = [shift(small_total.astype(BF), "z", 1), shift(output_total.astype(BF), "z", 1)]
    late, arrived, expert_totals[2] = lax.optimization_barrier((late, arrived, expert_totals[2]))
    small = part_of(small, "z", 2, 0) + arrived[0].astype(F32)
    small = reduce_axis(small.astype(BF), "y", 0).astype(BF)
    output_total = part_of(output_y, "z", 0, ring[output_hops]) + arrived[1].astype(F32)
    output_hops += 1
    while output_hops < zs - 1:
        output_total = shift(output_total.astype(BF), "z", 1).astype(F32)
        output_total = part_of(output_y, "z", 0, ring[output_hops]) + output_total
        output_hops += 1
    output_weight_grad = output_total
    total = jnp.concatenate([late, small], axis=-1)
    columns = sent_along("x", lambda i: lax.dynamic_index_in_dim(total, i, 1, keepdims=False))
    columns = jnp.stack(columns)
    columns = sent_along("c", lambda i: lax.dynamic_index_in_dim(columns, i, 1, keepdims=False))
    small_total = sum(jnp.sum(some[:, :, 3 * width :].astype(F32), axis=0) for some in columns)

    def all_heads(at):
        halves = []
        for some in columns:
            half = jnp.zeros((shard_rows, half_width), BF)
            for k in range(xs):
                part = some[k][:, at * width : (at + 1) * width]
                half = lax.dynamic_update_slice(half, part, (0, jnp.mod(x - k, xs) * width))
            halves.append(half)
        low = jnp.where(c == 0, halves[0], halves[1]).reshape(shard_rows, ys, chunk)
        high = jnp.where(c == 0, halves[1], halves[0]).reshape(shard_rows, ys, chunk)
        return jnp.stack([low, high], axis=2).reshape(shard_rows, D).astype(F32)

    shape = (batches, 1, rows, D)
    return (
        layer_out.reshape(shape),
        tokens_grad.reshape(shape),
        small_total[:, 0],
        all_heads(0),
        all_heads(1),
        all_heads(2),
        output_weight_grad,
        small_total[:head_shard, 2 + experts],
        small_total[:head_shard, 3 + experts],
        small_total[:, 1],
        small_total[:, 2 : 2 + experts],
        expert_totals[1],
        expert_totals[2],
        expert_totals[0],
    )


def solution(mesh):
    dp, expert = mesh.shape["dp"], mesh.shape["expert"]
    zs = math.gcd(expert, 4)
    grid = Mesh(
        mesh.devices.reshape(dp // 2, 2, zs, expert // zs),
        ("y", "c", "z", "x"),
    )
    every, dps, exps = ("y", "c", "z", "x"), ("y", "c"), ("z", "x")
    in_specs = (
        P(None, every, None, None),
        P(None, every, None, None),
        P(None, every),
        P(None, every, None, None),
        P(None, every, None),
        P(every),
        P(every, None),
        P(every, None),
        P(every, None),
        P(every, None),
        P(every),
        P(every),
        P(every),
        P(every, None),
        P(exps, dps, None),
        P(exps, dps, None),
        P(exps, dps, None),
    )
    out_specs = (
        P(None, every, None, None),
        P(None, every, None, None),
        P(every),
        P(every, None),
        P(every, None),
        P(every, None),
        P(every, None),
        P(every),
        P(every),
        P(every),
        P(every, None),
        P(exps, dps, None),
        P(exps, dps, None),
        P(exps, dps, None),
    )
    return jax.shard_map(shards, mesh=grid, in_specs=in_specs, out_specs=out_specs, check_vma=False)
```
